32 devices in a mesh: dp: 16 (over z, y, core), tensor: 2 (over x).
Axes of the slice: x: 2, y: 2, z: 4, core: 2. Of those that a mesh axis runs over, the one named last changes fastest.
Arguments:
- layer_in: bfloat16 [2, 16, 1024, 1024], P(None, 'dp'), may hold values from -6 to 6
- ln1_gain: float32 [1024], replicated, may hold values from 0.25 to 1.75
- ln1_bias: float32 [1024], replicated, may hold values from -1.2 to 1.2
- qkv_weight: bfloat16 [3, 1024, 1024], P(None, None, 'tensor'), may hold values from -0.1875 to 0.1875
- out_weight: bfloat16 [1024, 1024], P('tensor'), may hold values from -1.5 to 1.5
- ssm_coef: float32 [16, 1024], P(None, 'tensor'), may hold values from -1.5 to 1.5
- ssm_skip: float32 [1024], P('tensor'), may hold values from -2 to 2
- ln2_gain: float32 [1024], replicated, may hold values from 0.25 to 1.75
- ln2_bias: float32 [1024], replicated, may hold values from -1.2 to 1.2
- up_weight: bfloat16 [1024, 4096], P(None, 'tensor'), may hold values from -0.1875 to 0.1875
- down_weight: bfloat16 [4096, 1024], P('tensor'), may hold values from -0.09375 to 0.09375
- cotangent: bfloat16 [2, 16, 1024, 1024], P(None, 'dp'), may hold values from -6 to 6
Outputs:
- layer_out: bfloat16 [2, 16, 1024, 1024], P(None, 'dp')
- grad_in: float32 [2, 16, 1024, 1024], P(None, 'dp')
- grad_ln1_gain: float32 [1024], replicated
- grad_ln1_bias: float32 [1024], replicated
- grad_qkv: float32 [3, 1024, 1024], P(None, 'dp', 'tensor')
- grad_out: float32 [1024, 1024], P('tensor', 'dp')
- grad_coef: float32 [16, 1024], P(None, 'tensor')
- grad_skip: float32 [1024], P('tensor')
- grad_ln2_gain: float32 [1024], replicated
- grad_ln2_bias: float32 [1024], replicated
- grad_up: float32 [1024, 4096], P('dp', 'tensor')
- grad_down: float32 [4096, 1024], P('tensor', 'dp')
The draws below stay inside these ranges and needn't reach their ends.
All inputs are finite; a program needn't handle non-finite values.
Results may differ from the reference program's by a relative error of at most 0.015.
Values may be sent and summed in bfloat16 or wider, within the bound.
No kernel may reach another device: no remote copies, remote signals or barrier semaphores. Data moves between devices by JAX's collectives and lax.ppermute only.
A program may use at most 320 MiB of HBM per device.

```python
import jax
import jax.numpy as jnp
from jax import lax

D = 1024
HEADS = 8
HD = 128
NS = 16
FF = 4096
BLK = 512
CTX = 128
CH = 128
MB = 2
SEQ = 1024
NSEQ = 16
TGROUPS = 2


def strengthened(array, stream_key, source, target, shards_of, factor):
    def block_of(axis_at):
        return (jnp.arange(array.shape[axis_at]) // (array.shape[axis_at] // shards_of)).reshape((-1,) + (1,) * (array.ndim - 1 - axis_at))

    first = jax.random.permutation(stream_key, shards_of)[block_of(target)]
    second = (block_of(target) + shards_of // 2) % shards_of
    return jnp.where((block_of(source) == first) | (block_of(source) == second), factor * array, array)


def levels(stream_key, extent, shards, low, high):
    gain = 1.0
    for dim, shards_of in shards:
        draws = jax.random.uniform(jax.random.fold_in(jax.random.fold_in(stream_key, 6), dim), (shards_of,), jnp.float32, low / len(shards), high / len(shards))
        gain = gain * jnp.repeat(jnp.exp(draws), extent[dim] // shards_of).reshape((-1,) + (1,) * (len(extent) - 1 - dim))
    return gain


def bell_draw(stream_key, dims, deviation, most, shards=(), held_as=jnp.bfloat16):
    level = levels(stream_key, dims, shards, -0.22, 0.18) if shards else 1.0
    entries = jax.random.normal(stream_key, dims, jnp.float32) * deviation * level
    return jnp.minimum(jnp.maximum(entries, -most), most).astype(held_as)


def heavy_noise(own_key, shape, scale, reach, cuts, heavy, kind=jnp.bfloat16):
    drawn = scale * jax.random.normal(own_key, shape, jnp.float32)
    if cuts:
        drawn = drawn * levels(own_key, shape, cuts, -0.22, 0.18)
    return jnp.clip(strengthened(drawn, jax.random.fold_in(own_key, 3), *heavy), -reach, reach).astype(kind)


def setup_inputs(seed: int = 0) -> dict:
    arg_keys = jax.random.split(jax.random.key(seed), 13)
    layer_in = bell_draw(arg_keys[0], (MB, NSEQ, SEQ, D), 1.0, 6.0, ((1, 16),))
    ln1_gain = jnp.clip(1.0 + 0.15 * jax.random.normal(arg_keys[1], (D,), jnp.float32), 0.25, 1.75)
    ln1_bias = bell_draw(arg_keys[2], (D,), 0.3, 1.2, (), jnp.float32)
    qkv_weight = bell_draw(arg_keys[3], (3, D, D), D ** -0.5, 0.1875, ((2, 2),))
    out_weight = bell_draw(arg_keys[4], (D, D), (D // 64) ** -0.5, 1.5, ((0, 2),))
    ssm_coef = bell_draw(arg_keys[5], (NS, D), 0.25, 1.5, ((1, 2),), jnp.float32)
    ssm_skip = bell_draw(arg_keys[6], (D,), 0.5, 2.0, ((0, 2),), jnp.float32)
    ln2_gain = jnp.clip(1.0 + 0.15 * jax.random.normal(arg_keys[7], (D,), jnp.float32), 0.25, 1.75)
    ln2_bias = bell_draw(arg_keys[8], (D,), 0.3, 1.2, (), jnp.float32)
    up_weight = bell_draw(arg_keys[9], (D, FF), D ** -0.5, 0.1875, ((1, 2),))
    down_weight = bell_draw(arg_keys[10], (FF, D), FF ** -0.5, 0.09375, ((0, 2),))
    cotangent = heavy_noise(arg_keys[11], (MB, NSEQ, SEQ, D), 1.0, 6.0, ((1, 16),), (1, 3, 16, 2.0))
    return dict(layer_in=layer_in, ln1_gain=ln1_gain, ln1_bias=ln1_bias, qkv_weight=qkv_weight, out_weight=out_weight, ssm_coef=ssm_coef, ssm_skip=ssm_skip, ln2_gain=ln2_gain, ln2_bias=ln2_bias, up_weight=up_weight, down_weight=down_weight, cotangent=cotangent)


@jax.custom_vjp
def low(v):
    return lax.optimization_barrier(v.astype(jnp.bfloat16)).astype(jnp.float32)

@jax.custom_vjp
def low_back(v):
    return v

def low_keep(v):
    return (low(v), None)

def low_pass(kept, grad):
    return (grad,)

def back_keep(v):
    return (v, None)

def back_low(kept, grad):
    return (low(grad),)
low.defvjp(low_keep, low_pass)
low_back.defvjp(back_keep, back_low)
epsilon = 1e-05
highest = lax.Precision.HIGHEST

def layer_norm(values, gain_vec, shift_vec):
    center = values - lax.optimization_barrier(jnp.mean(values, axis=-1, keepdims=True))
    spread = lax.optimization_barrier(jnp.mean(center * center, axis=-1, keepdims=True))
    return center * lax.rsqrt(spread + epsilon) * gain_vec + shift_vec

def decay_tables():
    index_n = jnp.arange(NS, dtype=jnp.float32)
    decay_rates = 4.0 / CH * jnp.exp2(-8.0 * index_n / (NS - 1))
    norm_factor = jnp.sqrt(-jnp.expm1(-2.0 * decay_rates))
    positions = jnp.arange(CH, dtype=jnp.float32)
    offsets = positions[:, None] - positions[None, :]
    powers = jnp.exp(-decay_rates[:, None, None] * jnp.maximum(offsets, 0.0)[None])
    within = low(jnp.where(offsets[None] >= 0.0, norm_factor[:, None, None] * powers, 0.0))
    carry_in = jnp.exp(-decay_rates[None, :] * (positions[:, None] + 1.0))
    carry_out = within[:, CH - 1, :]
    whole_decay = jnp.exp(-decay_rates * CH)
    return (within, carry_in, carry_out, whole_decay)

def ssm_apply(channels, coef_rows, skip_vec, tables):
    within, carry_in, carry_out, whole_decay = tables
    width_here = channels.shape[1]
    pieces = channels.reshape(SEQ // CH, CH, width_here)

    def block_step(carry_state, block_rows):
        inner = jnp.einsum('ntj,jc->ntc', within, block_rows, precision=highest)
        inner = inner + carry_in.T[:, :, None] * carry_state[:, None, :]
        result_rows = lax.optimization_barrier(jnp.sum(coef_rows[:, None, :] * inner, axis=0)) + skip_vec * block_rows
        next_state = whole_decay[:, None] * carry_state + jnp.einsum('nj,jc->nc', carry_out, block_rows, precision=highest)
        return (next_state, result_rows)
    starting = jnp.zeros((NS, width_here), jnp.float32)
    _, results = lax.scan(jax.checkpoint(block_step), starting, pieces)
    return results.reshape(SEQ, width_here)

def visible(first_block):
    row_ids = lax.broadcasted_iota(jnp.int32, (BLK, CTX + BLK), 0)
    col_ids = lax.broadcasted_iota(jnp.int32, (BLK, CTX + BLK), 1)
    return jnp.where(col_ids < CTX, jnp.logical_not(first_block), col_ids - CTX <= row_ids)

def attend_block(item):
    first_block, query_rows, key_rows, value_rows = item
    scores = jnp.einsum('thd,shd->hts', query_rows, key_rows, precision=highest) * HD ** (-0.5)
    scores = low_back(jnp.where(visible(first_block)[None], scores, -1e+30))
    row_top = lax.optimization_barrier(jnp.max(scores, axis=-1, keepdims=True))
    exps_rows = jnp.exp(scores - row_top)
    probs_low = low(exps_rows / lax.optimization_barrier(jnp.sum(exps_rows, axis=-1, keepdims=True)))
    return jnp.einsum('hts,shd->thd', probs_low, value_rows, precision=highest)

def forward(inputs, weights, tables):
    ln1_gain, ln1_bias, qkv_weight, out_weight, ssm_coef, ssm_skip, ln2_gain, ln2_bias, up_weight, down_weight = weights
    width_group = D // TGROUPS
    heads_group = HEADS // TGROUPS
    hidden_group = FF // TGROUPS
    blocks = SEQ // BLK
    rounded = low(layer_norm(inputs, ln1_gain, ln1_bias))
    group_inputs = [low_back(rounded) for group_index in range(TGROUPS)]
    channels = jnp.concatenate([group_inputs[group_index][:, group_index * width_group:(group_index + 1) * width_group] for group_index in range(TGROUPS)], axis=1)
    ssm_out = low_back(ssm_apply(channels, ssm_coef, ssm_skip, tables))
    context = low(ssm_out.reshape(blocks, BLK, D)[:-1, BLK - CTX:, :])
    firsts = jnp.arange(blocks) == 0
    attn_out = jnp.zeros((SEQ, D), jnp.float32)
    for group_index in range(TGROUPS):
        low_col = group_index * width_group
        high_col = low_col + width_group
        projected = low(low_back(jnp.einsum('td,sde->ste', group_inputs[group_index], qkv_weight[:, :, low_col:high_col], precision=highest)))
        context_kv = low(low_back(jnp.einsum('bcd,sde->sbce', context, qkv_weight[1:, :, low_col:high_col], precision=highest)))
        shaped = projected.reshape(3, blocks, BLK, heads_group, HD)
        padded = jnp.concatenate([jnp.zeros((2, 1, CTX, heads_group, HD), jnp.float32), context_kv.reshape(2, blocks - 1, CTX, heads_group, HD)], axis=1)
        joined = jnp.concatenate([padded, shaped[1:]], axis=2)
        heads_out = lax.map(jax.checkpoint(attend_block), (firsts, shaped[0], joined[0], joined[1]))
        heads_flat = low(low_back(heads_out.reshape(SEQ, width_group)))
        attn_out = attn_out + low(jnp.dot(heads_flat, out_weight[low_col:high_col, :], precision=highest))
    middle = inputs + low_back(attn_out)
    second = low(layer_norm(middle, ln2_gain, ln2_bias))
    mixed = jnp.zeros((SEQ, D), jnp.float32)
    for group_index in range(TGROUPS):
        low_col = group_index * hidden_group
        high_col = low_col + hidden_group
        pre_act = low_back(jnp.dot(low_back(second), up_weight[:, low_col:high_col], precision=highest))
        hidden = low(jax.nn.gelu(pre_act, approximate=True))
        mixed = mixed + low(jnp.dot(hidden, down_weight[low_col:high_col, :], precision=highest))
    return middle + low_back(mixed)

def reference(layer_in, ln1_gain, ln1_bias, qkv_weight, out_weight, ssm_coef, ssm_skip, ln2_gain, ln2_bias, up_weight, down_weight, cotangent):
    tables = decay_tables()
    params = (ln1_gain, ln1_bias, qkv_weight.astype(jnp.float32), out_weight.astype(jnp.float32), ssm_coef, ssm_skip, ln2_gain, ln2_bias, up_weight.astype(jnp.float32), down_weight.astype(jnp.float32))
    seq_inputs = layer_in.reshape(MB * NSEQ, SEQ, D)
    seq_cotangents = cotangent.reshape(MB * NSEQ, SEQ, D)

    def per_sequence(totals, item):
        seq_rows, seq_cot = item

        def apply_layer(inputs, *weights):
            return forward(inputs, weights, tables)
        result_rows, pull_back = jax.vjp(apply_layer, seq_rows.astype(jnp.float32), *params)
        grads = pull_back(seq_cot.astype(jnp.float32))
        totals = tuple((total_part + grad_part for total_part, grad_part in zip(totals, grads[1:])))
        return (totals, (result_rows.astype(jnp.bfloat16), grads[0]))
    starting = tuple((jnp.zeros(param_part.shape, jnp.float32) for param_part in params))
    totals, (results, grad_rows) = lax.scan(per_sequence, starting, (seq_inputs, seq_cotangents))
    return (results.reshape(MB, NSEQ, SEQ, D), grad_rows.reshape(MB, NSEQ, SEQ, D), totals[0], totals[1], totals[2], totals[3], totals[4], totals[5], totals[6], totals[7], totals[8], totals[9])
```

```python
import functools
import math

import jax
import jax.numpy as jnp
from jax import lax
from jax.experimental import pallas as pl
from jax.experimental.pallas import tpu as pltpu
from jax.sharding import PartitionSpec as P

HD = 128
NS = 16
BLK = 512
CTX = 128
CH = 128
TILE = 256
EPS = 1e-05
F32 = jnp.float32
BF16 = jnp.bfloat16
HIGHEST = lax.Precision.HIGHEST
SCALE = HD**-0.5
LOG2 = SCALE * math.log2(math.e)


def swap(value, axis, mask, count):
    return lax.ppermute(value, axis, [(i, i ^ mask) for i in range(count)])


def mm(left, right):
    return lax.dot_general(left, right, (((1,), (0,)), ((), ())), preferred_element_type=F32)


def mm_nt(left, right):
    return lax.dot_general(left, right, (((1,), (1,)), ((), ())), preferred_element_type=F32)


def mm_tn(left, right):
    return lax.dot_general(left, right, (((0,), (0,)), ((), ())), preferred_element_type=F32)


def decay_tables():
    index_n = jnp.arange(NS, dtype=F32)
    rates = 4.0 / CH * jnp.exp2(-8.0 * index_n / (NS - 1))
    norm = jnp.sqrt(-jnp.expm1(-2.0 * rates))
    positions = jnp.arange(CH, dtype=F32)
    offsets = positions[:, None] - positions[None, :]
    powers = jnp.exp(-rates[:, None, None] * jnp.maximum(offsets, 0.0)[None])
    within = jnp.where(offsets[None] >= 0.0, norm[:, None, None] * powers, 0.0).astype(BF16)
    carry_in = jnp.exp(-rates[None, :] * (positions[:, None] + 1.0))
    carry_out = within[:, CH - 1, :]
    whole = jnp.exp(-rates * CH)
    return within, carry_in, carry_out, whole[:, None]


def ssm_forward_kernel(v_ref, within_ref, carry_in_ref, carry_out_ref, whole_ref, coef_ref, skip_ref, out_ref, state_ref):
    whole = whole_ref[...]
    before = BLK // CH - 1
    state = jnp.zeros(state_ref.shape, F32)
    for k in range(before):
        state = whole * state + mm(carry_out_ref[...], v_ref[k * CH : (k + 1) * CH, :])
    state_ref[...] = state
    rows = v_ref[before * CH :, :]
    total = skip_ref[...] * rows.astype(F32)
    total += jnp.dot(carry_in_ref[...], coef_ref[...] * state, precision=HIGHEST, preferred_element_type=F32)
    for n in range(NS):
        total += coef_ref[n : n + 1, :] * mm(within_ref[n], rows)
    out_ref[...] = total.astype(BF16)


def ssm_forward(rows, tables, coef, skip):
    within, carry_in, carry_out, whole = tables
    width = rows.shape[1]
    step = 256
    column = lambda c: (0, c)
    fixed2 = lambda c: (0, 0)
    return pl.pallas_call(
        ssm_forward_kernel,
        grid=(width // step,),
        in_specs=[
            pl.BlockSpec((BLK, step), column),
            pl.BlockSpec((NS, CH, CH), lambda c: (0, 0, 0)),
            pl.BlockSpec((CH, NS), fixed2),
            pl.BlockSpec((NS, CH), fixed2),
            pl.BlockSpec((NS, 1), fixed2),
            pl.BlockSpec((NS, step), column),
            pl.BlockSpec((1, step), column),
        ],
        out_specs=[pl.BlockSpec((CH, step), column), pl.BlockSpec((NS, step), column)],
        out_shape=[jax.ShapeDtypeStruct((CH, width), BF16), jax.ShapeDtypeStruct((NS, width), F32)],
        cost_estimate=pl.CostEstimate(flops=2 * NS * CH * CH * width, bytes_accessed=3 << 20, transcendentals=0),
        name="ssm_forward",
    )(rows, within, carry_in, carry_out, whole, coef, skip)


def ssm_backward_kernel(v_ref, grad_ref, within_ref, carry_in_ref, carry_out_ref, whole_ref, coef_ref, skip_ref, state_ref, du_ref, small_ref):
    before = BLK // CH - 1
    rows = v_ref[...].astype(F32)
    grad = grad_ref[...]
    wide = grad.astype(F32)
    du = skip_ref[...] * wide
    reach = jnp.dot(carry_in_ref[...], wide, precision=HIGHEST, preferred_element_type=F32)
    for n in range(NS):
        back = mm(within_ref[n], grad)
        du += coef_ref[n : n + 1, :] * back
        small_ref[n : n + 1, :] = (
            jnp.sum(rows * back, axis=0, keepdims=True) + state_ref[n : n + 1, :] * reach[n : n + 1, :]
        )
    small_ref[NS : NS + 1, :] = jnp.sum(rows * wide, axis=0, keepdims=True)
    du_ref[before * CH :, :] = du
    state = coef_ref[...] * reach
    for k in reversed(range(before)):
        du_ref[k * CH : (k + 1) * CH, :] = jnp.dot(
            carry_out_ref[...], state, precision=HIGHEST, preferred_element_type=F32
        )
        state = whole_ref[...] * state


def ssm_backward(rows, grad, tables, coef, skip, state):
    within, carry_in, carry_out, whole = tables
    width = rows.shape[1]
    step = 256
    column = lambda c: (0, c)
    fixed2 = lambda c: (0, 0)
    return pl.pallas_call(
        ssm_backward_kernel,
        grid=(width // step,),
        in_specs=[
            pl.BlockSpec((CH, step), lambda c: (BLK // CH - 1, c)),
            pl.BlockSpec((CH, step), column),
            pl.BlockSpec((NS, CH, CH), lambda c: (0, 0, 0)),
            pl.BlockSpec((NS, CH), fixed2),
            pl.BlockSpec((CH, NS), fixed2),
            pl.BlockSpec((NS, 1), fixed2),
            pl.BlockSpec((NS, step), column),
            pl.BlockSpec((1, step), column),
            pl.BlockSpec((NS, step), column),
        ],
        out_specs=[pl.BlockSpec((BLK, step), column), pl.BlockSpec((NS + 1, step), column)],
        out_shape=[jax.ShapeDtypeStruct((BLK, width), F32), jax.ShapeDtypeStruct((NS + 1, width), F32)],
        cost_estimate=pl.CostEstimate(flops=2 * NS * CH * CH * width, bytes_accessed=4 << 20, transcendentals=0),
        name="ssm_backward",
    )(rows, grad, within.swapaxes(1, 2), carry_in.T, carry_out.astype(F32).T, whole, coef, skip, state)


def key_parts(block, tile, k_ref, v_ref, ck_ref, cv_ref):
    parts = []
    if block > 0:
        parts.append((None, ck_ref[0], cv_ref[0], False))
    for piece in range(tile + 1):
        where = slice(block * BLK + piece * TILE, block * BLK + (piece + 1) * TILE)
        parts.append((piece, k_ref[0, where, :], v_ref[0, where, :], piece == tile))
    return parts


def tile_scores(keys, query, masked):
    scores = mm_nt(keys, query)
    if masked:
        key_ids = lax.broadcasted_iota(jnp.int32, scores.shape, 0)
        query_ids = lax.broadcasted_iota(jnp.int32, scores.shape, 1)
        scores = jnp.where(key_ids <= query_ids, scores, -1e30)
    return scores


def attend_forward_kernel(q_ref, k_ref, v_ref, ck_ref, cv_ref, out_ref, lse_ref):
    for block in range(2):
        for tile in range(BLK // TILE):
            base = block * BLK + tile * TILE
            query = q_ref[0, base : base + TILE, :]
            parts = key_parts(block, tile, k_ref, v_ref, ck_ref, cv_ref)
            scores = [tile_scores(keys, query, masked) for _, keys, _, masked in parts]
            top = functools.reduce(jnp.maximum, [jnp.max(s, axis=0, keepdims=True) for s in scores]) * LOG2
            exps = [jnp.exp2(s * LOG2 - top) for s in scores]
            total = functools.reduce(jnp.add, [jnp.sum(e, axis=0, keepdims=True) for e in exps])
            inverse = 1.0 / total
            out = functools.reduce(
                jnp.add,
                [mm_tn(values, (e * inverse).astype(BF16)) for (_, _, values, _), e in zip(parts, exps)],
            )
            out_ref[base : base + TILE, :] = out.T.astype(BF16)
            lse_ref[0, :, base : base + TILE] = top + jnp.log2(total)


def attend_forward(qkv, ckv):
    length, width = qkv.shape[1], qkv.shape[2]
    heads = width // HD
    pick = lambda s: pl.BlockSpec((1, length, HD), lambda h: (s, 0, h))
    pick_context = lambda s: pl.BlockSpec((1, CTX, HD), lambda h: (s, 0, h))
    return pl.pallas_call(
        attend_forward_kernel,
        grid=(heads,),
        in_specs=[pick(0), pick(1), pick(2), pick_context(0), pick_context(1)],
        out_specs=[
            pl.BlockSpec((length, HD), lambda h: (0, h)),
            pl.BlockSpec((1, 1, length), lambda h: (h, 0, 0)),
        ],
        out_shape=[
            jax.ShapeDtypeStruct((length, width), BF16),
            jax.ShapeDtypeStruct((heads, 1, length), F32),
        ],
        cost_estimate=pl.CostEstimate(
            flops=4 * heads * length * BLK * HD, bytes_accessed=5 << 20, transcendentals=heads * length * BLK
        ),
        name="attend_forward",
    )(qkv, qkv, qkv, ckv, ckv)


def attend_backward_kernel(q_ref, k_ref, v_ref, ck_ref, cv_ref, dout_ref, lse_ref, grad_ref, cgrad_ref):
    for block in range(2):
        grads = {}
        for tile in range(BLK // TILE):
            base = block * BLK + tile * TILE
            query = q_ref[0, base : base + TILE, :]
            dout = dout_ref[base : base + TILE, :]
            lse = lse_ref[0, :, base : base + TILE]
            parts = key_parts(block, tile, k_ref, v_ref, ck_ref, cv_ref)
            probs = [jnp.exp2(tile_scores(keys, query, masked) * LOG2 - lse) for _, keys, _, masked in parts]
            dprobs = [mm_nt(values, dout) for _, _, values, _ in parts]
            inner = functools.reduce(
                jnp.add, [jnp.sum(p * d, axis=0, keepdims=True) for p, d in zip(probs, dprobs)]
            )
            dquery = None
            for (name, keys, _, _), p, d in zip(parts, probs, dprobs):
                dscore = (p * (d - inner)).astype(BF16)
                term = mm_tn(keys, dscore)
                dquery = term if dquery is None else dquery + term
                dkey, dvalue = mm(dscore, query), mm(p.astype(BF16), dout)
                if name in grads:
                    grads[name] = (grads[name][0] + dkey, grads[name][1] + dvalue)
                else:
                    grads[name] = (dkey, dvalue)
            grad_ref[0, base : base + TILE, :] = (dquery.T * SCALE).astype(BF16)
        for name, (dkey, dvalue) in grads.items():
            dkey, dvalue = (dkey * SCALE).astype(BF16), dvalue.astype(BF16)
            if name is None:
                cgrad_ref[0] = dkey
                cgrad_ref[1] = dvalue
            else:
                where = slice(block * BLK + name * TILE, block * BLK + (name + 1) * TILE)
                grad_ref[1, where, :] = dkey
                grad_ref[2, where, :] = dvalue


def attend_backward(qkv, ckv, dheads, lse):
    length, width = qkv.shape[1], qkv.shape[2]
    heads = width // HD
    pick = lambda s: pl.BlockSpec((1, length, HD), lambda h: (s, 0, h))
    pick_context = lambda s: pl.BlockSpec((1, CTX, HD), lambda h: (s, 0, h))
    return pl.pallas_call(
        attend_backward_kernel,
        grid=(heads,),
        in_specs=[
            pick(0),
            pick(1),
            pick(2),
            pick_context(0),
            pick_context(1),
            pl.BlockSpec((length, HD), lambda h: (0, h)),
            pl.BlockSpec((1, 1, length), lambda h: (h, 0, 0)),
        ],
        out_specs=[
            pl.BlockSpec((3, length, HD), lambda h: (0, 0, h)),
            pl.BlockSpec((2, CTX, HD), lambda h: (0, 0, h)),
        ],
        out_shape=[
            jax.ShapeDtypeStruct((3, length, width), BF16),
            jax.ShapeDtypeStruct((2, CTX, width), BF16),
        ],
        cost_estimate=pl.CostEstimate(
            flops=10 * heads * length * BLK * HD, bytes_accessed=9 << 20, transcendentals=heads * length * BLK
        ),
        name="attend_backward",
    )(qkv, qkv, qkv, ckv, ckv, dheads, lse)


def normalize(values):
    center = values - jnp.mean(values, axis=-1, keepdims=True)
    rstd = lax.rsqrt(jnp.mean(center * center, axis=-1, keepdims=True) + EPS)
    return center * rstd, rstd


def normalize_backward(grad, hat, rstd, gain):
    dn = grad * gain
    dx = rstd * (dn - jnp.mean(dn, axis=-1, keepdims=True) - hat * jnp.mean(dn * hat, axis=-1, keepdims=True))
    return dx, jnp.sum(grad * hat, axis=0, keepdims=True), jnp.sum(grad, axis=0, keepdims=True)


def gelu_pair(pre):
    root = math.sqrt(2.0 / math.pi)
    squared = pre * pre
    bend = jnp.tanh(root * pre * (1.0 + 0.044715 * squared))
    half = 0.5 * (1.0 + bend)
    slope = half + 0.5 * pre * (1.0 - bend * bend) * (root * (1.0 + 3 * 0.044715 * squared))
    return (pre * half).astype(BF16), slope.astype(BF16)


def shards(dp_count, layer_in, ln1_gain, ln1_bias, qkv_weight, out_weight, ssm_coef, ssm_skip, ln2_gain, ln2_bias, up_weight, down_weight, cotangent):
    width = layer_in.shape[3]
    group = qkv_weight.shape[2]
    hidden_group = up_weight.shape[1]
    mine = lax.axis_index("tensor")
    place = lax.axis_index("dp")
    bits = dp_count.bit_length() - 1
    rows_each = width // dp_count

    over_x = lambda v: swap(v, "tensor", 1, 2)
    over = lambda v, bit: swap(v, "dp", 1 << bit, dp_count)

    quarter = place & 3

    def fetch(weight):
        flat = weight.reshape(-1, weight.shape[-1])
        size = flat.shape[0] // 4
        first = over_x(lax.dynamic_slice_in_dim(flat, quarter * size, size, 0))
        beside = over(first, 1)
        pieces = [(first, 0), (over(first, 0), 1), (beside, 2), (over(beside, 0), 3)]
        whole = jnp.zeros_like(flat)
        for piece, mask in pieces:
            whole = lax.dynamic_update_slice_in_dim(whole, piece, (quarter ^ mask) * size, 0)
        return whole.reshape(weight.shape)

    small = over_x(jnp.concatenate([ssm_coef, ssm_skip[None]], axis=0))
    qkv_other = fetch(qkv_weight)
    out_other = fetch(out_weight)
    up_other = fetch(up_weight)
    down_other = fetch(down_weight)

    def in_order(own, other, axis):
        return jnp.where(
            mine == 0, jnp.concatenate([own, other], axis=axis), jnp.concatenate([other, own], axis=axis)
        )

    coef = in_order(ssm_coef, small[:NS], 1)
    skip = in_order(ssm_skip[None], small[NS:], 1)
    tables = decay_tables()

    column = jnp.arange(width)
    spot = column // rows_each
    code = jnp.zeros_like(spot)
    for bit in range(bits):
        code = code | (((spot >> (bits - 1 - bit)) & 1) << bit)
    source = (code ^ place) * rows_each + column % rows_each
    permutation = (column[:, None] == source[None, :]).astype(BF16)

    def rows_first(values):
        return lax.dot_general(
            permutation, values, (((0,), (1,)), ((), ())), preferred_element_type=F32
        ).astype(BF16)

    def scatter(left, right_own, right_other, x_first):
        half = width // 2
        quart = width // 4
        got_other = over(mm(left[half:], right_other).astype(BF16), 0)
        got_own = over(mm(left[half:], right_own).astype(BF16), 0)
        if x_first:
            got = over_x((mm(left[:half], right_other) + got_other).astype(BF16))
            total = mm(left[:half], right_own) + got_own + got
            got = over(total[quart:].astype(BF16), 1)
            total = total[:quart] + got
        else:
            sum_other = mm(left[:half], right_other) + got_other
            sum_own = mm(left[:half], right_own) + got_own
            beside_other = over(sum_other[quart:].astype(BF16), 1)
            beside_own = over(sum_own[quart:].astype(BF16), 1)
            got = over_x((sum_other[:quart] + beside_other).astype(BF16))
            total = sum_own[:quart] + beside_own + got
        rows = quart
        for bit in range(2, bits):
            rows //= 2
            total = total[:rows] + over(total[rows:].astype(BF16), bit)
        return total

    inputs = lax.dynamic_index_in_dim(layer_in[:, 0], mine, 0, keepdims=False).astype(F32)
    grads = lax.dynamic_index_in_dim(cotangent[:, 0], mine, 0, keepdims=False)
    hat1, rstd1 = normalize(inputs)
    u1 = (hat1 * ln1_gain + ln1_bias).astype(BF16)
    context, state = ssm_forward(u1, tables, coef, skip)

    def project(rows, weight):
        return jnp.einsum("td,sde->ste", rows, weight, preferred_element_type=F32).astype(BF16)

    sides = []
    for weight in (qkv_weight, qkv_other):
        qkv = project(u1, weight)
        ckv = project(context, weight[1:])
        heads, lse = attend_forward(qkv, ckv)
        sides.append((qkv, ckv, heads, lse))
    attn_out = mm(sides[0][2], out_weight) + mm(sides[1][2], out_other)
    middle = inputs + attn_out
    hat2, rstd2 = normalize(middle)
    u2 = (hat2 * ln2_gain + ln2_bias).astype(BF16)
    hid_own, slope_own = gelu_pair(mm(u2, up_weight))
    hid_other, slope_other = gelu_pair(mm(u2, up_other))
    mixed = mm(hid_own, down_weight) + mm(hid_other, down_other)
    layer_out = (middle + mixed).astype(BF16)
    layer_out_other = over_x(layer_out)

    grad_down = scatter(rows_first(grads), hid_own, hid_other, False)
    dpre_own = (mm_nt(grads, down_weight) * slope_own.astype(F32)).astype(BF16)
    dpre_other = (mm_nt(grads, down_other) * slope_other.astype(F32)).astype(BF16)
    grad_up = scatter(rows_first(u2), dpre_own, dpre_other, True)
    du2 = mm_nt(dpre_own, up_weight) + mm_nt(dpre_other, up_other)
    dx2, grad_gain2, grad_bias2 = normalize_backward(du2, hat2, rstd2, ln2_gain)
    dx1 = grads.astype(F32) + dx2
    dattn = dx1.astype(BF16)
    grad_out = scatter(rows_first(dattn), sides[0][2], sides[1][2], False)
    dsides = []
    for (qkv, ckv, heads, lse), weight in zip(sides, (out_weight, out_other)):
        dheads = mm_nt(dattn, weight).astype(BF16)
        dsides.append(attend_backward(qkv, ckv, dheads, lse))
    both = ((dsides[0], qkv_weight), (dsides[1], qkv_other))
    dcontext = sum(
        jnp.einsum("sce,sde->cd", dckv, weight[1:], preferred_element_type=F32) for (_, dckv), weight in both
    )
    du_ssm, small_ssm = ssm_backward(u1, dcontext.astype(BF16), tables, coef, skip, state)
    du1 = sum(jnp.einsum("ste,sde->td", dqkv, weight, preferred_element_type=F32) for (dqkv, _), weight in both)
    du1 = du1 + jnp.concatenate([du_ssm, jnp.zeros_like(du_ssm)], axis=0)
    dx0, grad_gain1, grad_bias1 = normalize_backward(du1, hat1, rstd1, ln1_gain)
    grad_in = (dx1 + dx0).astype(BF16)
    grad_in_other = over_x(grad_in)

    tall = jnp.concatenate([u1, context], axis=0)
    sides_tall = []
    for dqkv, dckv in dsides:
        extra = jnp.concatenate([jnp.zeros_like(dckv[:1]), dckv], axis=0)
        stacked = jnp.concatenate([dqkv, extra], axis=1)
        sides_tall.append(stacked.swapaxes(0, 1).reshape(stacked.shape[1], -1))
    grad_qkv = scatter(rows_first(tall), sides_tall[0], sides_tall[1], True)

    small_all = jnp.concatenate([small_ssm, grad_gain2, grad_bias2, grad_gain1, grad_bias1], axis=0)
    small_all = small_all + over_x(small_all)
    for bit in range(bits):
        small_all = small_all + over(small_all, bit)
    here = lax.dynamic_slice_in_dim(small_all[: NS + 1], mine * group, group, 1)

    def both_parts(own, other):
        stacked = jnp.where(mine == 0, jnp.stack([own, other]), jnp.stack([other, own]))
        return stacked[:, None]

    return (
        both_parts(layer_out, layer_out_other),
        both_parts(grad_in, grad_in_other).astype(F32),
        small_all[NS + 3],
        small_all[NS + 4],
        grad_qkv.reshape(rows_each, 3, group).swapaxes(0, 1),
        grad_out.T,
        here[:NS],
        here[NS],
        small_all[NS + 1],
        small_all[NS + 2],
        grad_up,
        grad_down.T,
    )


def solution(mesh):
    in_specs = (
        P(None, "dp", None, None),
        P(),
        P(),
        P(None, None, "tensor"),
        P("tensor", None),
        P(None, "tensor"),
        P("tensor"),
        P(),
        P(),
        P(None, "tensor"),
        P("tensor", None),
        P(None, "dp", None, None),
    )
    out_specs = (
        P(None, "dp", None, None),
        P(None, "dp", None, None),
        P(),
        P(),
        P(None, "dp", "tensor"),
        P("tensor", "dp"),
        P(None, "tensor"),
        P("tensor"),
        P(),
        P(),
        P("dp", "tensor"),
        P("tensor", "dp"),
    )
    body = functools.partial(shards, mesh.shape["dp"])
    return jax.shard_map(body, mesh=mesh, in_specs=in_specs, out_specs=out_specs, check_vma=False)
```

```python
import functools
import math

import jax
import jax.numpy as jnp
from jax import lax
from jax.experimental import pallas as pl
from jax.experimental.pallas import tpu as pltpu
from jax.sharding import PartitionSpec as P
import numpy as np

HD = 128
NS = 16
BLK = 512
CTX = 128
CH = 128
TILE = 256
EPS = 1e-05
F32 = jnp.float32
BF16 = jnp.bfloat16
HIGHEST = lax.Precision.HIGHEST
SCALE = HD**-0.5
LOG2 = SCALE * math.log2(math.e)


def swap(value, axis, mask, count):
    return lax.ppermute(value, axis, [(i, i ^ mask) for i in range(count)])


def tie(value, *deps):
    return lax.optimization_barrier((value, *deps))[0] if deps else value


def mm(left, right):
    return lax.dot_general(left, right, (((1,), (0,)), ((), ())), preferred_element_type=F32)


def mm_nt(left, right):
    return lax.dot_general(left, right, (((1,), (1,)), ((), ())), preferred_element_type=F32)


def mm_tn(left, right):
    return lax.dot_general(left, right, (((0,), (0,)), ((), ())), preferred_element_type=F32)


def decay_constants():
    rates = 4.0 / CH * np.exp2(-8.0 * np.arange(NS, dtype=np.float64) / (NS - 1))
    return rates, np.sqrt(-np.expm1(-2.0 * rates))


RATES, NORMS = decay_constants()


def decay_within(n, transposed):
    rows = lax.broadcasted_iota(jnp.int32, (CH, CH), 0)
    columns = lax.broadcasted_iota(jnp.int32, (CH, CH), 1)
    offset = columns - rows if transposed else rows - columns
    powers = jnp.exp(offset.astype(F32) * -float(RATES[n]))
    return jnp.where(offset >= 0, float(NORMS[n]) * powers, 0.0).astype(BF16)


def decay_vectors(rates, norms):
    steps = lax.broadcasted_iota(jnp.int32, (NS, CH), 1).astype(F32)
    carry_in = jnp.exp(-rates * (steps + 1.0))
    carry_out = (norms * jnp.exp(-rates * (CH - 1.0 - steps))).astype(BF16)
    return carry_in, carry_out, jnp.exp(-rates * CH)


def ssm_forward_kernel(v_ref, rates_ref, norms_ref, coef_ref, skip_ref, out_ref, state_ref, within_ref):
    @pl.when(pl.program_id(0) == 0)
    def _():
        for n in range(NS):
            within_ref[n] = decay_within(n, False)

    carry_in, carry_out, whole = decay_vectors(rates_ref[...], norms_ref[...])
    before = BLK // CH - 1
    state = jnp.zeros(state_ref.shape, F32)
    for k in range(before):
        state = whole * state + mm(carry_out, v_ref[k * CH : (k + 1) * CH, :])
    state_ref[...] = state
    rows = v_ref[before * CH :, :]
    total = skip_ref[...] * rows.astype(F32)
    total += lax.dot_general(
        carry_in, coef_ref[...] * state, (((0,), (0,)), ((), ())), precision=HIGHEST, preferred_element_type=F32
    )
    for n in range(NS):
        total += coef_ref[n : n + 1, :] * mm(within_ref[n], rows)
    out_ref[...] = total.astype(BF16)


def decay_arrays():
    return jnp.asarray(RATES[:, None], F32), jnp.asarray(NORMS[:, None], F32)


def ssm_forward(rows, coef, skip):
    width = rows.shape[1]
    step = 256
    column = lambda c: (0, c)
    fixed = pl.BlockSpec((NS, 1), lambda c: (0, 0))
    return pl.pallas_call(
        ssm_forward_kernel,
        grid=(width // step,),
        in_specs=[
            pl.BlockSpec((BLK, step), column),
            fixed,
            fixed,
            pl.BlockSpec((NS, step), column),
            pl.BlockSpec((1, step), column),
        ],
        out_specs=[pl.BlockSpec((CH, step), column), pl.BlockSpec((NS, step), column)],
        out_shape=[jax.ShapeDtypeStruct((CH, width), BF16), jax.ShapeDtypeStruct((NS, width), F32)],
        scratch_shapes=[pltpu.VMEM((NS, CH, CH), BF16)],
        cost_estimate=brief(),
        name="ssm_forward",
    )(rows, *decay_arrays(), coef, skip)


def ssm_backward_kernel(v_ref, grad_ref, rates_ref, norms_ref, coef_ref, skip_ref, state_ref, du_ref, small_ref, within_ref):
    @pl.when(pl.program_id(0) == 0)
    def _():
        for n in range(NS):
            within_ref[n] = decay_within(n, True)

    carry_in, carry_out, whole = decay_vectors(rates_ref[...], norms_ref[...])
    before = BLK // CH - 1
    rows = v_ref[...].astype(F32)
    grad = grad_ref[...].astype(BF16)
    wide = grad.astype(F32)
    du = skip_ref[...] * wide
    reach = jnp.dot(carry_in, wide, precision=HIGHEST, preferred_element_type=F32)
    for n in range(NS):
        back = mm(within_ref[n], grad)
        du += coef_ref[n : n + 1, :] * back
        small_ref[n : n + 1, :] = (
            jnp.sum(rows * back, axis=0, keepdims=True) + state_ref[n : n + 1, :] * reach[n : n + 1, :]
        )
    small_ref[NS : NS + 1, :] = jnp.sum(rows * wide, axis=0, keepdims=True)
    du_ref[before * CH :, :] = du
    state = coef_ref[...] * reach
    for k in reversed(range(before)):
        du_ref[k * CH : (k + 1) * CH, :] = lax.dot_general(
            carry_out.astype(F32), state, (((0,), (0,)), ((), ())), precision=HIGHEST, preferred_element_type=F32
        )
        state = whole * state


def ssm_backward(rows, grad, coef, skip, state):
    width = rows.shape[1]
    step = 256
    column = lambda c: (0, c)
    fixed = pl.BlockSpec((NS, 1), lambda c: (0, 0))
    return pl.pallas_call(
        ssm_backward_kernel,
        grid=(width // step,),
        in_specs=[
            pl.BlockSpec((CH, step), lambda c: (BLK // CH - 1, c)),
            pl.BlockSpec((CH, step), column),
            fixed,
            fixed,
            pl.BlockSpec((NS, step), column),
            pl.BlockSpec((1, step), column),
            pl.BlockSpec((NS, step), column),
        ],
        out_specs=[pl.BlockSpec((BLK, step), column), pl.BlockSpec((NS + 1, step), column)],
        out_shape=[jax.ShapeDtypeStruct((BLK, width), F32), jax.ShapeDtypeStruct((NS + 1, width), F32)],
        scratch_shapes=[pltpu.VMEM((NS, CH, CH), BF16)],
        cost_estimate=brief(),
        name="ssm_backward",
    )(rows, grad, *decay_arrays(), coef, skip, state)


def key_parts(block, tile, k_ref, v_ref, ck_ref, cv_ref):
    parts = []
    if block > 0:
        parts.append((None, ck_ref[0], cv_ref[0], False))
    for piece in range(tile + 1):
        where = slice(block * BLK + piece * TILE, block * BLK + (piece + 1) * TILE)
        parts.append((piece, k_ref[0, where, :], v_ref[0, where, :], piece == tile))
    return parts


def tile_scores(keys, query, masked):
    scores = mm_nt(keys, query)
    if masked:
        key_ids = lax.broadcasted_iota(jnp.int32, scores.shape, 0)
        query_ids = lax.broadcasted_iota(jnp.int32, scores.shape, 1)
        scores = jnp.where(key_ids <= query_ids, scores, -1e30)
    return scores


def attend_forward_kernel(q_ref, k_ref, v_ref, ck_ref, cv_ref, out_ref, lse_ref):
    for block in range(2):
        for tile in range(BLK // TILE):
            base = block * BLK + tile * TILE
            query = q_ref[0, base : base + TILE, :]
            parts = key_parts(block, tile, k_ref, v_ref, ck_ref, cv_ref)
            scores = [tile_scores(keys, query, masked) for _, keys, _, masked in parts]
            top = functools.reduce(jnp.maximum, [jnp.max(s, axis=0, keepdims=True) for s in scores]) * LOG2
            exps = [jnp.exp2(s * LOG2 - top) for s in scores]
            total = functools.reduce(jnp.add, [jnp.sum(e, axis=0, keepdims=True) for e in exps])
            inverse = 1.0 / total
            out = functools.reduce(
                jnp.add,
                [mm_tn(values, (e * inverse).astype(BF16)) for (_, _, values, _), e in zip(parts, exps)],
            )
            out_ref[base : base + TILE, :] = out.T.astype(BF16)
            lse_ref[0, :, base : base + TILE] = top + jnp.log2(total)


def attend_forward(qkv, ckv):
    length, width = qkv.shape[1], qkv.shape[2]
    heads = width // HD
    pick = lambda s: pl.BlockSpec((1, length, HD), lambda h: (s, 0, h))
    pick_context = lambda s: pl.BlockSpec((1, CTX, HD), lambda h: (s, 0, h))
    return pl.pallas_call(
        attend_forward_kernel,
        grid=(heads,),
        in_specs=[pick(0), pick(1), pick(2), pick_context(0), pick_context(1)],
        out_specs=[
            pl.BlockSpec((length, HD), lambda h: (0, h)),
            pl.BlockSpec((1, 1, length), lambda h: (h, 0, 0)),
        ],
        out_shape=[
            jax.ShapeDtypeStruct((length, width), BF16),
            jax.ShapeDtypeStruct((heads, 1, length), F32),
        ],
        cost_estimate=brief(),
        name="attend_forward",
    )(qkv, qkv, qkv, ckv, ckv)


def attend_backward_kernel(q_ref, k_ref, v_ref, ck_ref, cv_ref, dout_ref, lse_ref, grad_ref, cgrad_ref):
    for block in range(2):
        grads = {}
        for tile in range(BLK // TILE):
            base = block * BLK + tile * TILE
            query = q_ref[0, base : base + TILE, :]
            dout = dout_ref[base : base + TILE, :]
            lse = lse_ref[0, :, base : base + TILE]
            parts = key_parts(block, tile, k_ref, v_ref, ck_ref, cv_ref)
            probs = [jnp.exp2(tile_scores(keys, query, masked) * LOG2 - lse) for _, keys, _, masked in parts]
            dprobs = [mm_nt(values, dout) for _, _, values, _ in parts]
            inner = functools.reduce(
                jnp.add, [jnp.sum(p * d, axis=0, keepdims=True) for p, d in zip(probs, dprobs)]
            )
            dquery = None
            for (name, keys, _, _), p, d in zip(parts, probs, dprobs):
                dscore = (p * (d - inner)).astype(BF16)
                term = mm_tn(keys, dscore)
                dquery = term if dquery is None else dquery + term
                dkey, dvalue = mm(dscore, query), mm(p.astype(BF16), dout)
                if name in grads:
                    grads[name] = (grads[name][0] + dkey, grads[name][1] + dvalue)
                else:
                    grads[name] = (dkey, dvalue)
            grad_ref[0, base : base + TILE, :] = (dquery.T * SCALE).astype(BF16)
        for name, (dkey, dvalue) in grads.items():
            dkey, dvalue = (dkey * SCALE).astype(BF16), dvalue.astype(BF16)
            if name is None:
                cgrad_ref[0] = dkey
                cgrad_ref[1] = dvalue
            else:
                where = slice(block * BLK + name * TILE, block * BLK + (name + 1) * TILE)
                grad_ref[1, where, :] = dkey
                grad_ref[2, where, :] = dvalue


def attend_backward(qkv, ckv, dheads, lse):
    length, width = qkv.shape[1], qkv.shape[2]
    heads = width // HD
    pick = lambda s: pl.BlockSpec((1, length, HD), lambda h: (s, 0, h))
    pick_context = lambda s: pl.BlockSpec((1, CTX, HD), lambda h: (s, 0, h))
    return pl.pallas_call(
        attend_backward_kernel,
        grid=(heads,),
        in_specs=[
            pick(0),
            pick(1),
            pick(2),
            pick_context(0),
            pick_context(1),
            pl.BlockSpec((length, HD), lambda h: (0, h)),
            pl.BlockSpec((1, 1, length), lambda h: (h, 0, 0)),
        ],
        out_specs=[
            pl.BlockSpec((3, length, HD), lambda h: (0, 0, h)),
            pl.BlockSpec((2, CTX, HD), lambda h: (0, 0, h)),
        ],
        out_shape=[
            jax.ShapeDtypeStruct((3, length, width), BF16),
            jax.ShapeDtypeStruct((2, CTX, width), BF16),
        ],
        cost_estimate=brief(),
        name="attend_backward",
    )(qkv, qkv, qkv, ckv, ckv, dheads, lse)


def brief():
    return pl.CostEstimate(flops=1 << 32, bytes_accessed=1 << 16, transcendentals=0)


def roomy():
    return pltpu.CompilerParams(vmem_limit_bytes=56 << 20)


def halving_order(count):
    bits = count.bit_length() - 1
    return [sum(((p >> (bits - 1 - b)) & 1) << b for b in range(bits)) for p in range(count)]


def place_rows(where_ref, tall_ref, out_ref, count):
    size = tall_ref.shape[0] // count
    for p, code in enumerate(halving_order(count)):
        start = pl.multiple_of((where_ref[1] ^ code) * size, size)
        out_ref[p * size : (p + 1) * size, :] = tall_ref[pl.ds(start, size), :]


def whole_block(shape):
    return pl.BlockSpec(shape, lambda *_: (0,) * len(shape), pipeline_mode=pl.Buffered(1))


def normalize(values):
    center = values - jnp.mean(values, axis=-1, keepdims=True)
    rstd = lax.rsqrt(jnp.mean(center * center, axis=-1, keepdims=True) + EPS)
    return center * rstd, rstd


def normalize_backward(grad, hat, rstd, gain):
    dn = grad * gain
    return rstd * (dn - jnp.mean(dn, axis=-1, keepdims=True) - hat * jnp.mean(dn * hat, axis=-1, keepdims=True))


def first_norm(where, layer_in, cotangent, gain, bias, count):
    length, width = layer_in.shape[2:]
    step = 256

    def kernel(where_ref, x_ref, dy_ref, gain_ref, bias_ref, u_ref, ut_ref, dyt_ref, tall):
        hat, _ = normalize(x_ref[0, 0].astype(F32))
        u = (hat * gain_ref[...] + bias_ref[...]).astype(BF16)
        u_ref[...] = u
        tall[...] = u.T
        place_rows(where_ref, tall, ut_ref, count)
        tall[...] = dy_ref[0, 0].T
        place_rows(where_ref, tall, dyt_ref, count)

    mine = lambda i, w: (w[0], 0, i, 0)
    return pl.pallas_call(
        kernel,
        grid_spec=pltpu.PrefetchScalarGridSpec(
            num_scalar_prefetch=1,
            grid=(length // step,),
            in_specs=[
                pl.BlockSpec((1, 1, step, width), mine),
                pl.BlockSpec((1, 1, step, width), mine),
                whole_block((1, width)),
                whole_block((1, width)),
            ],
            out_specs=[
                pl.BlockSpec((step, width), lambda i, w: (i, 0)),
                pl.BlockSpec((width, step), lambda i, w: (0, i)),
                pl.BlockSpec((width, step), lambda i, w: (0, i)),
            ],
            scratch_shapes=[pltpu.VMEM((width, step), BF16)],
        ),
        out_shape=[
            jax.ShapeDtypeStruct((length, width), BF16),
            jax.ShapeDtypeStruct((width, length), BF16),
            jax.ShapeDtypeStruct((width, length), BF16),
        ],
        cost_estimate=brief(),
        name="first_norm",
    )(where, layer_in, cotangent, gain, bias)


def context_rows(where, context, count):
    def kernel(where_ref, c_ref, out_ref, tall):
        tall[...] = c_ref[...].T
        place_rows(where_ref, tall, out_ref, count)

    rows, width = context.shape
    return pl.pallas_call(
        kernel,
        in_specs=[pl.BlockSpec(memory_space=pltpu.SMEM), pl.BlockSpec(memory_space=pltpu.VMEM)],
        out_specs=pl.BlockSpec(memory_space=pltpu.VMEM),
        out_shape=jax.ShapeDtypeStruct((width, rows), BF16),
        scratch_shapes=[pltpu.VMEM((width, rows), BF16)],
        cost_estimate=brief(),
        name="context_rows",
    )(where, context)


def attention_out(where, layer_in, heads_own, heads_other, out_own, out_other, gain, bias, count):
    length, width = layer_in.shape[2:]
    group = heads_own.shape[1]
    step = 256

    def kernel(where_ref, x_ref, ho_ref, ht_ref, wo_ref, wt_ref, gain_ref, bias_ref, x1_ref, u_ref, ut_ref, tall):
        x1 = x_ref[0, 0].astype(F32) + mm(ho_ref[...], wo_ref[...]) + mm(ht_ref[...], wt_ref[...])
        x1_ref[...] = x1
        hat, _ = normalize(x1)
        u = (hat * gain_ref[...] + bias_ref[...]).astype(BF16)
        u_ref[...] = u
        tall[...] = u.T
        place_rows(where_ref, tall, ut_ref, count)

    row = lambda i, w: (i, 0)
    return pl.pallas_call(
        kernel,
        grid_spec=pltpu.PrefetchScalarGridSpec(
            num_scalar_prefetch=1,
            grid=(length // step,),
            in_specs=[
                pl.BlockSpec((1, 1, step, width), lambda i, w: (w[0], 0, i, 0)),
                pl.BlockSpec((step, group), row),
                pl.BlockSpec((step, group), row),
                whole_block((group, width)),
                whole_block((group, width)),
                whole_block((1, width)),
                whole_block((1, width)),
            ],
            out_specs=[
                pl.BlockSpec((step, width), row),
                pl.BlockSpec((step, width), row),
                pl.BlockSpec((width, step), lambda i, w: (0, i)),
            ],
            scratch_shapes=[pltpu.VMEM((width, step), BF16)],
        ),
        out_shape=[
            jax.ShapeDtypeStruct((length, width), F32),
            jax.ShapeDtypeStruct((length, width), BF16),
            jax.ShapeDtypeStruct((width, length), BF16),
        ],
        compiler_params=roomy(),
        cost_estimate=brief(),
        name="attention_out",
    )(where, layer_in, heads_own, heads_other, out_own, out_other, gain, bias)


STEP = 1024


def weight_copies(own_ref, piece_refs, held, sems, axis):
    count = own_ref.shape[axis] // STEP
    size = piece_refs[0].shape[axis]
    per = STEP // size

    def part(ref, start, extent):
        return ref.at[pl.ds(start, extent), :] if axis == 0 else ref.at[:, pl.ds(start, extent)]

    copies = []
    for j in range(count):
        copies.append([pltpu.make_async_copy(part(own_ref, j * STEP, STEP), held.at[j], sems.at[j, 0])])
    for j in range(len(piece_refs) // per):
        copies.append(
            [
                pltpu.make_async_copy(
                    piece_refs[j * per + k], part(held.at[count + j], k * size, size), sems.at[count + j, k]
                )
                for k in range(per)
            ]
        )
    return copies


def stream_weights(copies):
    step = pl.program_id(0)

    @pl.when(step == 0)
    def _():
        for some in copies:
            for copy in some:
                copy.start()

    for j, some in enumerate(copies):

        @pl.when(step == j)
        def _(some=some):
            for copy in some:
                copy.wait()


ANYWHERE = pl.BlockSpec(memory_space=pl.ANY)


def gelu_pair(pre):
    root = math.sqrt(2.0 / math.pi)
    squared = pre * pre
    bend = jnp.tanh(pre * (root + (root * 0.044715) * squared))
    half = 0.5 + 0.5 * bend
    slope = half + pre * ((0.5 - 0.5 * bend * bend) * (root + (3 * 0.044715 * root) * squared))
    return (pre * half).astype(BF16), slope.astype(BF16)


def hidden_forward(u2, up_own, up_pieces):
    length, width = u2.shape
    steps = 2 * up_own.shape[1] // STEP
    chunk = 256

    def kernel(u_ref, own_ref, p0, p1, p2, p3, hid_ref, slope_ref, held, sems):
        stream_weights(weight_copies(own_ref, (p0, p1, p2, p3), held, sems, 1))
        j = pl.program_id(0)
        for i in range(length // chunk):
            rows = slice(i * chunk, (i + 1) * chunk)
            hid, slope = gelu_pair(mm(u_ref[rows, :], held[j]))
            hid_ref[rows, :] = hid
            slope_ref[rows, :] = slope

    tile = pl.BlockSpec((length, STEP), lambda j: (0, j))
    return pl.pallas_call(
        kernel,
        grid=(steps,),
        in_specs=[whole_block((length, width))] + [ANYWHERE] * 5,
        out_specs=[tile, tile],
        out_shape=[jax.ShapeDtypeStruct((length, steps * STEP), BF16)] * 2,
        scratch_shapes=[pltpu.VMEM((steps, width, STEP), BF16), pltpu.SemaphoreType.DMA((steps, 2))],
        compiler_params=roomy(),
        cost_estimate=brief(),
        name="hidden_forward",
    )(u2, up_own, *up_pieces)


def hidden_backward(where, cotangent, down_own, down_pieces, slope):
    length, width = cotangent.shape[2:]
    steps = 2 * down_own.shape[0] // STEP
    chunk = 256

    def kernel(where_ref, dy_ref, own_ref, p0, p1, p2, p3, slope_ref, out_ref, held, sems):
        stream_weights(weight_copies(own_ref, (p0, p1, p2, p3), held, sems, 0))
        j = pl.program_id(0)
        for i in range(length // chunk):
            rows = slice(i * chunk, (i + 1) * chunk)
            out_ref[rows, :] = (mm_nt(dy_ref[0, 0, rows, :], held[j]) * slope_ref[rows, :].astype(F32)).astype(BF16)

    tile = pl.BlockSpec((length, STEP), lambda j, w: (0, j))
    return pl.pallas_call(
        kernel,
        grid_spec=pltpu.PrefetchScalarGridSpec(
            num_scalar_prefetch=1,
            grid=(steps,),
            in_specs=[
                pl.BlockSpec((1, 1, length, width), lambda j, w: (w[0], 0, 0, 0), pipeline_mode=pl.Buffered(1))
            ]
            + [ANYWHERE] * 5
            + [tile],
            out_specs=tile,
            scratch_shapes=[pltpu.VMEM((steps, STEP, width), BF16), pltpu.SemaphoreType.DMA((steps, 2))],
        ),
        out_shape=jax.ShapeDtypeStruct((length, steps * STEP), BF16),
        compiler_params=roomy(),
        cost_estimate=brief(),
        name="hidden_backward",
    )(where, cotangent, down_own, *down_pieces, slope)


def hidden_out(hid, down_own, down_pieces, x1):
    length, width = x1.shape
    steps = 2 * down_own.shape[0] // STEP

    def kernel(hid_ref, own_ref, p0, p1, p2, p3, x1_ref, out_ref, held, total, sems):
        stream_weights(weight_copies(own_ref, (p0, p1, p2, p3), held, sems, 0))
        j = pl.program_id(0)

        @pl.when(j == 0)
        def _():
            total[...] = x1_ref[...]

        total[...] += mm(hid_ref[...], held[j])

        @pl.when(j == steps - 1)
        def _():
            out_ref[...] = total[...].astype(BF16)

    return pl.pallas_call(
        kernel,
        grid=(steps,),
        in_specs=[pl.BlockSpec((length, STEP), lambda j: (0, j))] + [ANYWHERE] * 5 + [whole_block((length, width))],
        out_specs=whole_block((length, width)),
        out_shape=jax.ShapeDtypeStruct((length, width), BF16),
        scratch_shapes=[
            pltpu.VMEM((steps, STEP, width), BF16),
            pltpu.VMEM((length, width), F32),
            pltpu.SemaphoreType.DMA((steps, 2)),
        ],
        compiler_params=roomy(),
        cost_estimate=brief(),
        name="hidden_out",
    )(hid, down_own, *down_pieces, x1)


def second_norm_backward(where, dpre, up_own, up_pieces, x1, cotangent, gain, count):
    length, width = x1.shape
    steps = 2 * up_own.shape[1] // STEP
    chunk = 128

    def kernel(where_ref, dpre_ref, own_ref, p0, p1, p2, p3, x1_ref, dy_ref, gain_ref, out_ref, outt_ref, sums_ref, held, total, tall, sems):
        stream_weights(weight_copies(own_ref, (p0, p1, p2, p3), held, sems, 1))
        j = pl.program_id(0)

        @pl.when(j == 0)
        def _():
            total[...] = mm_nt(dpre_ref[...], held[j])
            sums_ref[...] = jnp.zeros_like(sums_ref)

        @pl.when(j > 0)
        def _():
            total[...] += mm_nt(dpre_ref[...], held[j])

        @pl.when(j == steps - 1)
        def _():
            @pl.loop(0, length // chunk)
            def _(i):
                rows = pl.ds(pl.multiple_of(i * chunk, chunk), chunk)
                du = total[rows, :]
                hat, rstd = normalize(x1_ref[rows, :])
                sums_ref[0:1, :] += jnp.sum(du * hat, axis=0, keepdims=True)
                sums_ref[1:2, :] += jnp.sum(du, axis=0, keepdims=True)
                out = dy_ref[0, 0, rows, :].astype(F32) + normalize_backward(du, hat, rstd, gain_ref[...])
                out = out.astype(BF16)
                out_ref[rows, :] = out
                tall[:, rows] = out.T

            place_rows(where_ref, tall, outt_ref, count)

    mine = pl.BlockSpec((1, 1, length, width), lambda j, w: (w[0], 0, 0, 0), pipeline_mode=pl.Buffered(1))
    return pl.pallas_call(
        kernel,
        grid_spec=pltpu.PrefetchScalarGridSpec(
            num_scalar_prefetch=1,
            grid=(steps,),
            in_specs=[pl.BlockSpec((length, STEP), lambda j, w: (0, j))]
            + [ANYWHERE] * 5
            + [whole_block((length, width)), mine, whole_block((1, width))],
            out_specs=[whole_block((length, width)), whole_block((width, length)), whole_block((2, width))],
            scratch_shapes=[
                pltpu.VMEM((steps, width, STEP), BF16),
                pltpu.VMEM((length, width), F32),
                pltpu.VMEM((width, length), BF16),
                pltpu.SemaphoreType.DMA((steps, 2)),
            ],
        ),
        out_shape=[
            jax.ShapeDtypeStruct((length, width), BF16),
            jax.ShapeDtypeStruct((width, length), BF16),
            jax.ShapeDtypeStruct((2, width), F32),
        ],
        compiler_params=roomy(),
        cost_estimate=brief(),
        name="second_norm_backward",
    )(where, dpre, up_own, *up_pieces, x1, cotangent, gain)


def first_norm_backward(where, dsides, qkv_own, qkv_pieces, du_ssm, layer_in, dattn, gain):
    length, width = layer_in.shape[2:]
    group = qkv_own.shape[2]
    size = qkv_pieces[0].shape[2]
    chunk = 128
    steps = 6

    def kernel(where_ref, do_ref, dt_ref, own_ref, p0, p1, p2, p3, ssm_ref, x_ref, dx_ref, gain_ref, out_ref, sums_ref, held, grads, total, sems):
        copies = []
        for s in range(3):
            copies.append(
                [
                    pltpu.make_async_copy(do_ref.at[s], grads.at[s], sems.at[s, 0]),
                    pltpu.make_async_copy(own_ref.at[s], held.at[s], sems.at[s, 1]),
                ]
            )
        for s in range(3):
            some = [pltpu.make_async_copy(dt_ref.at[s], grads.at[3 + s], sems.at[3 + s, 0])]
            for k, piece in enumerate((p0, p1, p2, p3)):
                some.append(
                    pltpu.make_async_copy(
                        piece.at[s], held.at[3 + s, :, pl.ds(k * size, size)], sems.at[3 + s, 1 + k]
                    )
                )
            copies.append(some)
        stream_weights(copies)
        j = pl.program_id(0)

        @pl.when(j == 0)
        def _():
            total[0 : ssm_ref.shape[0], :] = ssm_ref[...]
            total[ssm_ref.shape[0] :, :] = jnp.zeros((length - ssm_ref.shape[0], width), F32)
            sums_ref[...] = jnp.zeros_like(sums_ref)

        total[...] += mm_nt(grads[j], held[j])

        @pl.when(j == steps - 1)
        def _():
            @pl.loop(0, length // chunk)
            def _(i):
                rows = pl.ds(pl.multiple_of(i * chunk, chunk), chunk)
                du = total[rows, :]
                hat, rstd = normalize(x_ref[0, 0, rows, :].astype(F32))
                sums_ref[0:1, :] += jnp.sum(du * hat, axis=0, keepdims=True)
                sums_ref[1:2, :] += jnp.sum(du, axis=0, keepdims=True)
                out = dx_ref[rows, :].astype(F32) + normalize_backward(du, hat, rstd, gain_ref[...])
                out_ref[rows, :] = out.astype(BF16)

    mine = pl.BlockSpec((1, 1, length, width), lambda j, w: (w[0], 0, 0, 0), pipeline_mode=pl.Buffered(1))
    return pl.pallas_call(
        kernel,
        grid_spec=pltpu.PrefetchScalarGridSpec(
            num_scalar_prefetch=1,
            grid=(steps,),
            in_specs=[ANYWHERE] * 7
            + [whole_block(du_ssm.shape), mine, whole_block((length, width)), whole_block((1, width))],
            out_specs=[whole_block((length, width)), whole_block((2, width))],
            scratch_shapes=[
                pltpu.VMEM((steps, width, group), BF16),
                pltpu.VMEM((steps, length, group), BF16),
                pltpu.VMEM((length, width), F32),
                pltpu.SemaphoreType.DMA((steps, 5)),
            ],
        ),
        out_shape=[jax.ShapeDtypeStruct((length, width), BF16), jax.ShapeDtypeStruct((2, width), F32)],
        compiler_params=roomy(),
        cost_estimate=brief(),
        name="first_norm_backward",
    )(where, dsides[0], dsides[1], qkv_own, *qkv_pieces, du_ssm, layer_in, dattn, gain)


def rows_sent(left, right):
    width, length = left.shape
    half = width // 2
    columns = right.shape[1]

    def kernel(left_ref, right_ref, out_ref):
        out_ref[...] = mm(left_ref[...], right_ref[...]).astype(BF16)

    return pl.pallas_call(
        kernel,
        grid=(columns // STEP,),
        in_specs=[
            pl.BlockSpec((half, length), lambda j: (1, 0), pipeline_mode=pl.Buffered(1)),
            pl.BlockSpec((length, STEP), lambda j: (0, j)),
        ],
        out_specs=pl.BlockSpec((half, STEP), lambda j: (0, j)),
        out_shape=jax.ShapeDtypeStruct((half, columns), BF16),
        compiler_params=roomy(),
        cost_estimate=brief(),
        name="rows_sent",
    )(left, right)


def rows_kept(left, right, got):
    width, length = left.shape
    half = width // 2
    quart = width // 4
    columns = right.shape[1]
    piece = columns // 8
    steps = columns // STEP

    def kernel(left_ref, right_ref, got_ref, keep_ref, send_ref):
        j = pl.program_id(0)
        for part, out_ref in enumerate((keep_ref, send_ref)):
            rows = slice(part * quart, (part + 1) * quart)
            total = mm(left_ref[rows, :], right_ref[...])

            @pl.when(j < steps // 2)
            def _(total=total, out_ref=out_ref, rows=rows):
                out_ref[...] = (total + got_ref[rows, :].astype(F32)).astype(BF16)

            @pl.when(j >= steps // 2)
            def _(total=total, out_ref=out_ref, rows=rows):
                for k in range(STEP // piece):
                    here = slice(k * piece, (k + 1) * piece)
                    there = slice((k ^ 1) * piece, ((k ^ 1) + 1) * piece)
                    out_ref[:, here] = (total[:, here] + got_ref[rows, there].astype(F32)).astype(BF16)

    tile = pl.BlockSpec((quart, STEP), lambda j: (0, j))
    return pl.pallas_call(
        kernel,
        grid=(steps,),
        in_specs=[
            pl.BlockSpec((half, length), lambda j: (0, 0), pipeline_mode=pl.Buffered(1)),
            pl.BlockSpec((length, STEP), lambda j: (0, j)),
            pl.BlockSpec((half, STEP), lambda j: (0, j)),
        ],
        out_specs=[tile, tile],
        out_shape=[jax.ShapeDtypeStruct((quart, columns), BF16)] * 2,
        compiler_params=roomy(),
        cost_estimate=brief(),
        name="rows_kept",
    )(left, right, got)


def group_rows(left, own, other, extra, got):
    width, length = left.shape
    half = width // 2
    quart = width // 4
    count, _, group = own.shape
    piece = group // 4
    keeping = got is not None

    def kernel(*refs):
        refs = list(refs)
        left_ref, sides = refs.pop(0), [refs.pop(0), refs.pop(0)]
        if extra is not None:
            cleft_ref, csides = refs.pop(0), [refs.pop(0), refs.pop(0)]
        got_ref = refs.pop(0) if keeping else None
        j = pl.program_id(0)
        for side in range(2):

            @pl.when((j >= count) if side else (j < count))
            def _(side=side):
                for part in range(2 if keeping else 1):
                    rows = slice(part * quart, (part + 1) * quart) if keeping else slice(0, half)
                    total = mm(left_ref[rows, :], sides[side][0])
                    if extra is not None:
                        term = mm(cleft_ref[rows, :], csides[side][0])
                        total += jnp.where(lax.rem(j, count) > 0, term, 0.0)
                    if not keeping:
                        refs[0][...] = total.astype(BF16)
                        continue
                    for k in range(4):
                        here = slice(k * piece, (k + 1) * piece)
                        come = k ^ side
                        there = slice(come * piece, (come + 1) * piece)
                        refs[part][:, here] = (total[:, here] + got_ref[rows, there].astype(F32)).astype(BF16)

    first = lambda j: jnp.minimum(j, count - 1)
    second = lambda j: jnp.maximum(j - count, 0)
    before = lambda s: jnp.maximum(s - 1, 0)
    pick = 0 if keeping else 1
    in_specs = [
        pl.BlockSpec((half, length), lambda j: (pick, 0), pipeline_mode=pl.Buffered(1)),
        pl.BlockSpec((1, length, group), lambda j: (first(j), 0, 0)),
        pl.BlockSpec((1, length, group), lambda j: (second(j), 0, 0)),
    ]
    operands = [left, own, other]
    if extra is not None:
        rows = extra[0].shape[1]
        in_specs += [
            pl.BlockSpec((half, rows), lambda j: (pick, 0), pipeline_mode=pl.Buffered(1)),
            pl.BlockSpec((1, rows, group), lambda j: (before(first(j)), 0, 0)),
            pl.BlockSpec((1, rows, group), lambda j: (before(second(j)), 0, 0)),
        ]
        operands += list(extra)
    columns = 2 * count * group
    if keeping:
        in_specs.append(pl.BlockSpec((half, group), lambda j: (0, j)))
        operands.append(got)
        out_specs = [pl.BlockSpec((quart, group), lambda j: (0, j))] * 2
        out_shape = [jax.ShapeDtypeStruct((quart, columns), BF16)] * 2
    else:
        out_specs = pl.BlockSpec((half, group), lambda j: (0, j))
        out_shape = jax.ShapeDtypeStruct((half, columns), BF16)
    return pl.pallas_call(
        kernel,
        grid=(2 * count,),
        in_specs=in_specs,
        out_specs=out_specs,
        out_shape=out_shape,
        compiler_params=roomy(),
        cost_estimate=brief(),
        name="group_kept" if keeping else "group_sent",
    )(*operands)


def reorder(values, count, mask):
    piece = values.shape[1] // (4 * count)
    order = [4 * c + (k ^ mask) for c in range(count) for k in range(4)]
    return jnp.concatenate([values[:, i * piece : (i + 1) * piece] for i in order], axis=1)


def shards(
    dp_count,
    layer_in,
    ln1_gain,
    ln1_bias,
    qkv_weight,
    out_weight,
    ssm_coef,
    ssm_skip,
    ln2_gain,
    ln2_bias,
    up_weight,
    down_weight,
    cotangent,
):
    width = layer_in.shape[3]
    group = qkv_weight.shape[2]
    mine = lax.axis_index("tensor")
    place = lax.axis_index("dp")
    where = jnp.stack([mine, place]).astype(jnp.int32)
    bits = dp_count.bit_length() - 1
    rows_each = width // dp_count
    gain1, bias1, gain2, bias2 = ln1_gain[None], ln1_bias[None], ln2_gain[None], ln2_bias[None]

    over_x = lambda v: swap(v, "tensor", 1, 2)
    over = lambda v, bit: swap(v, "dp", 1 << bit, dp_count)

    quarter = place & 3

    def quarter_of(weight, axis):
        size = weight.shape[axis] // 4
        return lax.dynamic_slice_in_dim(weight, quarter * size, size, axis)

    def pieces(first, beside):
        return [first, over(first, 0), beside, over(beside, 0)]

    small = over_x(jnp.concatenate([ssm_coef, ssm_skip[None]], axis=0))
    qkv_first = over_x(quarter_of(qkv_weight, 2))

    def in_order(own, other, axis):
        return jnp.where(
            mine == 0, jnp.concatenate([own, other], axis=axis), jnp.concatenate([other, own], axis=axis)
        )

    coef = in_order(ssm_coef, small[:NS], 1)
    skip = in_order(ssm_skip[None], small[NS:], 1)

    class Halvings:
        def __init__(self, keep, send, count):
            self.columns, self.count, self.bit, self.crossed = keep.shape[1] // 2, count, 2, False
            self.total, self.message = keep.astype(F32), send
            self.got = over(send, 1)

        def step(self, *deps):
            got = tie(self.got, *deps)
            if self.bit == 2:
                other = reorder(got[:, self.columns :], self.count, 2)
                got = jnp.concatenate([got[:, : self.columns], other], axis=1)
            self.total = self.total + got
            if self.bit < bits:
                rows = self.total.shape[0] // 2
                self.message = self.total[rows:].astype(BF16)
                self.total = self.total[:rows]
                self.got = over(self.message, self.bit)
                self.bit += 1
            else:
                self.message = self.total[:, self.columns :].astype(BF16)
                self.got = over_x(self.message)
                self.crossed = True
            return self.message

        def last(self):
            while not self.crossed:
                self.step()
            got = self.got
            for bit in range(2):
                got = jnp.where((place >> bit) & 1 == 1, reorder(got, self.count, 1 << bit), got)
            return self.total[:, : self.columns] + got

    u1, u1_rows, dy_rows = first_norm(where, layer_in, cotangent, gain1, bias1, dp_count)

    def project(rows, weight):
        return jnp.einsum("td,sde->ste", rows, weight, preferred_element_type=F32).astype(BF16)

    out_first = over_x(tie(quarter_of(out_weight, 0), u1))
    up_first = over_x(tie(quarter_of(up_weight, 1), u1))
    qkv_own = project(u1, qkv_weight)
    down_first = over_x(tie(quarter_of(down_weight, 0), qkv_own))
    context, state = ssm_forward(tie(u1, qkv_own), coef, skip)
    qkv_first = tie(qkv_first, context)
    qkv_beside = over(qkv_first, 1)
    context_turned = context_rows(tie(where, context, qkv_first), context, dp_count)
    ckv_own = project(tie(context, context_turned), qkv_weight[1:])
    heads_own, lse_own = attend_forward(qkv_own, ckv_own)
    out_first = tie(out_first, heads_own)
    out_beside = over(out_first, 1)
    qkv_pieces = pieces(qkv_first, tie(qkv_beside, heads_own))
    qkv_other_weight = tie(jnp.concatenate(qkv_pieces, axis=2), heads_own, out_first)
    qkv_other = project(u1, qkv_other_weight)
    up_first = tie(up_first, qkv_other)
    up_beside = over(up_first, 1)
    out_beside = tie(out_beside, qkv_other)
    out_pieces = pieces(out_first, out_beside)
    ckv_other = project(tie(context, up_first, out_beside), qkv_other_weight[1:])
    heads_other, lse_other = attend_forward(qkv_other, ckv_other)
    out_other = jnp.concatenate([tie(piece, heads_other) for piece in out_pieces], axis=0)
    x1, u2, u2_rows = attention_out(
        where, layer_in, heads_own, heads_other, out_weight, out_other, gain2, bias2, dp_count
    )
    up_pieces = pieces(up_first, tie(up_beside, u2))
    down_first = tie(down_first, u2)
    down_beside = over(down_first, 1)
    hid, slope = hidden_forward(tie(u2, down_first), up_weight, up_pieces)

    down_part = rows_sent(dy_rows, hid)
    down_got = over(down_part, 0)
    down_pieces = pieces(down_first, tie(down_beside, down_part))
    dpre = hidden_backward(tie(where, down_part), cotangent, down_weight, down_pieces, slope)
    down_keep, down_send = rows_kept(tie(dy_rows, dpre), hid, tie(down_got, dpre))
    down = Halvings(down_keep, down_send, 1)
    up_part = rows_sent(tie(u2_rows, down_keep), dpre)
    up_got = over(up_part, 0)
    dattn, dattn_rows, sums2 = second_norm_backward(
        tie(where, up_part), dpre, up_weight, up_pieces, x1, cotangent, gain2, dp_count
    )
    up_keep, up_send = rows_kept(tie(u2_rows, dattn), dpre, tie(up_got, dattn))
    up = Halvings(up_keep, up_send, 1)
    message = down.step(up_keep)
    layer_out = hidden_out(hid, down_weight, down_pieces, tie(x1, up_keep, message))
    layer_out_other = over_x(layer_out)

    out_part = group_rows(tie(dattn_rows, layer_out), heads_own[None], heads_other[None], None, None)
    out_got = over(out_part, 0)
    dattn_then = tie(dattn, out_part)
    dheads_other = mm_nt(dattn_then, out_other).astype(BF16)
    dheads_own = mm_nt(dattn_then, out_weight).astype(BF16)
    message = down.step(dheads_own, dheads_other)
    dqkv_other, dckv_other = attend_backward(
        qkv_other, ckv_other, tie(dheads_other, dheads_own, message), lse_other
    )
    out_keep, out_send = group_rows(
        tie(dattn_rows, dqkv_other), heads_own[None], heads_other[None], None, tie(out_got, dqkv_other)
    )
    out = Halvings(out_keep, out_send, 1)
    dqkv_own, dckv_own = attend_backward(qkv_own, ckv_own, tie(dheads_own, out_keep), lse_own)

    extra = (context_turned, dckv_own, dckv_other)
    message_up, message_down = up.step(dqkv_own), down.step(dqkv_own)
    qkv_part = group_rows(tie(u1_rows, message_up, message_down), dqkv_own, dqkv_other, extra, None)
    qkv_got = over(qkv_part, 0)
    message = out.step(qkv_part)
    dckv_then = tie(dckv_own, qkv_part, message)
    dcontext = jnp.einsum("sce,sde->cd", dckv_then, qkv_weight[1:], preferred_element_type=F32)
    dcontext += jnp.einsum("sce,sde->cd", dckv_other, qkv_other_weight[1:], preferred_element_type=F32)
    du_ssm, small_ssm = ssm_backward(u1, dcontext, coef, skip, state)
    message = out.step(du_ssm)
    qkv_keep, qkv_send = group_rows(
        tie(u1_rows, du_ssm, message), dqkv_own, dqkv_other, extra, tie(qkv_got, du_ssm)
    )
    qkv = Halvings(qkv_keep, qkv_send, 3)
    message_up, message_out = up.step(qkv_keep), out.step(qkv_keep)
    layer_out_other, down.got = tie(layer_out_other, qkv_keep), tie(down.got, qkv_keep)
    grad_in, sums1 = first_norm_backward(
        tie(where, qkv_keep, message_up, message_out, layer_out_other, down.got),
        (dqkv_own, dqkv_other),
        qkv_weight,
        qkv_pieces,
        du_ssm,
        layer_in,
        dattn,
        gain1,
    )
    grad_in_other = over_x(grad_in)
    up.step(grad_in)

    small_all = jnp.concatenate([small_ssm, sums2, sums1], axis=0)
    small_all = small_all + over_x(small_all)
    for bit in range(bits):
        small_all = small_all + over(small_all, bit)
    here = lax.dynamic_slice_in_dim(small_all[: NS + 1], mine * group, group, 1)
    grad_down, grad_up, grad_out, grad_qkv = down.last(), up.last(), out.last(), qkv.last()

    def both_parts(own, other):
        return jnp.where(mine == 0, jnp.stack([own, other]), jnp.stack([other, own]))[:, None]

    return (
        both_parts(layer_out, layer_out_other),
        both_parts(grad_in, grad_in_other).astype(F32),
        small_all[NS + 3],
        small_all[NS + 4],
        grad_qkv.reshape(rows_each, 3, group).swapaxes(0, 1),
        grad_out.T,
        here[:NS],
        here[NS],
        small_all[NS + 1],
        small_all[NS + 2],
        grad_up,
        grad_down.T,
    )


def solution(mesh):
    in_specs = (
        P(None, "dp", None, None),
        P(),
        P(),
        P(None, None, "tensor"),
        P("tensor", None),
        P(None, "tensor"),
        P("tensor"),
        P(),
        P(),
        P(None, "tensor"),
        P("tensor", None),
        P(None, "dp", None, None),
    )
    out_specs = (
        P(None, "dp", None, None),
        P(None, "dp", None, None),
        P(),
        P(),
        P(None, "dp", "tensor"),
        P("tensor", "dp"),
        P(None, "tensor"),
        P("tensor"),
        P(),
        P(),
        P("dp", "tensor"),
        P("tensor", "dp"),
    )
    body = functools.partial(shards, mesh.shape["dp"])
    return jax.shard_map(body, mesh=mesh, in_specs=in_specs, out_specs=out_specs, check_vma=False)
```

```python
import functools
import math

import jax
import jax.numpy as jnp
from jax import lax
from jax.experimental import pallas as pl
from jax.experimental.pallas import tpu as pltpu
from jax.sharding import PartitionSpec as P
import numpy as np

HD = 128
NS = 16
BLK = 512
CTX = 128
CH = 128
TILE = 256
EPS = 1e-05
F32 = jnp.float32
BF16 = jnp.bfloat16
HIGHEST = lax.Precision.HIGHEST
SCALE = HD**-0.5
LOG2 = SCALE * math.log2(math.e)


def swap(value, axis, mask, count):
    return lax.ppermute(value, axis, [(i, i ^ mask) for i in range(count)])


def tie(value, *deps):
    return lax.optimization_barrier((value, *deps))[0] if deps else value


def mm(left, right):
    return lax.dot_general(left, right, (((1,), (0,)), ((), ())), preferred_element_type=F32)


def mm_nt(left, right):
    return lax.dot_general(left, right, (((1,), (1,)), ((), ())), preferred_element_type=F32)


def mm_tn(left, right):
    return lax.dot_general(left, right, (((0,), (0,)), ((), ())), preferred_element_type=F32)


def decay_constants():
    rates = 4.0 / CH * np.exp2(-8.0 * np.arange(NS, dtype=np.float64) / (NS - 1))
    return rates, np.sqrt(-np.expm1(-2.0 * rates))


RATES, NORMS = decay_constants()


def decay_within(n, transposed):
    rows = lax.broadcasted_iota(jnp.int32, (CH, CH), 0)
    columns = lax.broadcasted_iota(jnp.int32, (CH, CH), 1)
    offset = columns - rows if transposed else rows - columns
    powers = jnp.exp(offset.astype(F32) * -float(RATES[n]))
    return jnp.where(offset >= 0, float(NORMS[n]) * powers, 0.0).astype(BF16)


def decay_vectors(rates, norms):
    steps = lax.broadcasted_iota(jnp.int32, (NS, CH), 1).astype(F32)
    carry_in = jnp.exp(-rates * (steps + 1.0))
    carry_out = (norms * jnp.exp(-rates * (CH - 1.0 - steps))).astype(BF16)
    return carry_in, carry_out, jnp.exp(-rates * CH)


def ssm_forward_kernel(v_ref, rates_ref, norms_ref, coef_ref, skip_ref, out_ref, state_ref, within_ref):
    @pl.when(pl.program_id(0) == 0)
    def _():
        for n in range(NS):
            within_ref[n] = decay_within(n, False)

    carry_in, carry_out, whole = decay_vectors(rates_ref[...], norms_ref[...])
    before = BLK // CH - 1
    state = jnp.zeros(state_ref.shape, F32)
    for k in range(before):
        state = whole * state + mm(carry_out, v_ref[k * CH : (k + 1) * CH, :])
    state_ref[...] = state
    rows = v_ref[before * CH :, :]
    total = skip_ref[...] * rows.astype(F32)
    total += lax.dot_general(
        carry_in, coef_ref[...] * state, (((0,), (0,)), ((), ())), precision=HIGHEST, preferred_element_type=F32
    )
    for n in range(NS):
        total += coef_ref[n : n + 1, :] * mm(within_ref[n], rows)
    out_ref[...] = total.astype(BF16)


def decay_arrays():
    return jnp.asarray(RATES[:, None], F32), jnp.asarray(NORMS[:, None], F32)


def ssm_forward(rows, coef, skip):
    width = rows.shape[1]
    step = 256
    column = lambda c: (0, c)
    fixed = pl.BlockSpec((NS, 1), lambda c: (0, 0))
    return pl.pallas_call(
        ssm_forward_kernel,
        grid=(width // step,),
        in_specs=[
            pl.BlockSpec((BLK, step), column),
            fixed,
            fixed,
            pl.BlockSpec((NS, step), column),
            pl.BlockSpec((1, step), column),
        ],
        out_specs=[pl.BlockSpec((CH, step), column), pl.BlockSpec((NS, step), column)],
        out_shape=[jax.ShapeDtypeStruct((CH, width), BF16), jax.ShapeDtypeStruct((NS, width), F32)],
        scratch_shapes=[pltpu.VMEM((NS, CH, CH), BF16)],
        cost_estimate=brief(),
        name="ssm_forward",
    )(rows, *decay_arrays(), coef, skip)


def ssm_backward_kernel(v_ref, grad_ref, rates_ref, norms_ref, coef_ref, skip_ref, state_ref, du_ref, small_ref, within_ref):
    @pl.when(pl.program_id(0) == 0)
    def _():
        for n in range(NS):
            within_ref[n] = decay_within(n, True)

    carry_in, carry_out, whole = decay_vectors(rates_ref[...], norms_ref[...])
    before = BLK // CH - 1
    rows = v_ref[...].astype(F32)
    grad = grad_ref[...].astype(BF16)
    wide = grad.astype(F32)
    du = skip_ref[...] * wide
    reach = jnp.dot(carry_in, wide, precision=HIGHEST, preferred_element_type=F32)
    for n in range(NS):
        back = mm(within_ref[n], grad)
        du += coef_ref[n : n + 1, :] * back
        small_ref[n : n + 1, :] = (
            jnp.sum(rows * back, axis=0, keepdims=True) + state_ref[n : n + 1, :] * reach[n : n + 1, :]
        )
    small_ref[NS : NS + 1, :] = jnp.sum(rows * wide, axis=0, keepdims=True)
    du_ref[before * CH :, :] = du
    state = coef_ref[...] * reach
    for k in reversed(range(before)):
        du_ref[k * CH : (k + 1) * CH, :] = lax.dot_general(
            carry_out.astype(F32), state, (((0,), (0,)), ((), ())), precision=HIGHEST, preferred_element_type=F32
        )
        state = whole * state


def ssm_backward(rows, grad, coef, skip, state):
    width = rows.shape[1]
    step = 256
    column = lambda c: (0, c)
    fixed = pl.BlockSpec((NS, 1), lambda c: (0, 0))
    return pl.pallas_call(
        ssm_backward_kernel,
        grid=(width // step,),
        in_specs=[
            pl.BlockSpec((CH, step), lambda c: (BLK // CH - 1, c)),
            pl.BlockSpec((CH, step), column),
            fixed,
            fixed,
            pl.BlockSpec((NS, step), column),
            pl.BlockSpec((1, step), column),
            pl.BlockSpec((NS, step), column),
        ],
        out_specs=[pl.BlockSpec((BLK, step), column), pl.BlockSpec((NS + 1, step), column)],
        out_shape=[jax.ShapeDtypeStruct((BLK, width), F32), jax.ShapeDtypeStruct((NS + 1, width), F32)],
        scratch_shapes=[pltpu.VMEM((NS, CH, CH), BF16)],
        cost_estimate=brief(),
        name="ssm_backward",
    )(rows, grad, *decay_arrays(), coef, skip, state)


def key_parts(block, tile, k_ref, v_ref, ck_ref, cv_ref):
    parts = []
    if block > 0:
        parts.append((None, ck_ref[0], cv_ref[0], False))
    for piece in range(tile + 1):
        where = slice(block * BLK + piece * TILE, block * BLK + (piece + 1) * TILE)
        parts.append((piece, k_ref[0, where, :], v_ref[0, where, :], piece == tile))
    return parts


def tile_scores(keys, query, masked):
    scores = mm_nt(keys, query)
    if masked:
        key_ids = lax.broadcasted_iota(jnp.int32, scores.shape, 0)
        query_ids = lax.broadcasted_iota(jnp.int32, scores.shape, 1)
        scores = jnp.where(key_ids <= query_ids, scores, -1e30)
    return scores


def attend_forward_kernel(q_ref, k_ref, v_ref, ck_ref, cv_ref, out_ref, lse_ref):
    for block in range(2):
        for tile in range(BLK // TILE):
            base = block * BLK + tile * TILE
            query = q_ref[0, base : base + TILE, :]
            parts = key_parts(block, tile, k_ref, v_ref, ck_ref, cv_ref)
            scores = [tile_scores(keys, query, masked) for _, keys, _, masked in parts]
            top = functools.reduce(jnp.maximum, [jnp.max(s, axis=0, keepdims=True) for s in scores]) * LOG2
            exps = [jnp.exp2(s * LOG2 - top) for s in scores]
            total = functools.reduce(jnp.add, [jnp.sum(e, axis=0, keepdims=True) for e in exps])
            inverse = 1.0 / total
            out = functools.reduce(
                jnp.add,
                [mm_tn(values, (e * inverse).astype(BF16)) for (_, _, values, _), e in zip(parts, exps)],
            )
            out_ref[base : base + TILE, :] = out.T.astype(BF16)
            lse_ref[0, :, base : base + TILE] = top + jnp.log2(total)


def attend_forward(qkv, ckv):
    length, width = qkv.shape[1], qkv.shape[2]
    heads = width // HD
    pick = lambda s: pl.BlockSpec((1, length, HD), lambda h: (s, 0, h))
    pick_context = lambda s: pl.BlockSpec((1, CTX, HD), lambda h: (s, 0, h))
    return pl.pallas_call(
        attend_forward_kernel,
        grid=(heads,),
        in_specs=[pick(0), pick(1), pick(2), pick_context(0), pick_context(1)],
        out_specs=[
            pl.BlockSpec((length, HD), lambda h: (0, h)),
            pl.BlockSpec((1, 1, length), lambda h: (h, 0, 0)),
        ],
        out_shape=[
            jax.ShapeDtypeStruct((length, width), BF16),
            jax.ShapeDtypeStruct((heads, 1, length), F32),
        ],
        cost_estimate=brief(),
        name="attend_forward",
    )(qkv, qkv, qkv, ckv, ckv)


def attend_backward_kernel(q_ref, k_ref, v_ref, ck_ref, cv_ref, dout_ref, lse_ref, grad_ref, cgrad_ref):
    for block in range(2):
        grads = {}
        for tile in range(BLK // TILE):
            base = block * BLK + tile * TILE
            query = q_ref[0, base : base + TILE, :]
            dout = dout_ref[base : base + TILE, :]
            lse = lse_ref[0, :, base : base + TILE]
            parts = key_parts(block, tile, k_ref, v_ref, ck_ref, cv_ref)
            probs = [jnp.exp2(tile_scores(keys, query, masked) * LOG2 - lse) for _, keys, _, masked in parts]
            dprobs = [mm_nt(values, dout) for _, _, values, _ in parts]
            inner = functools.reduce(
                jnp.add, [jnp.sum(p * d, axis=0, keepdims=True) for p, d in zip(probs, dprobs)]
            )
            dquery = None
            for (name, keys, _, _), p, d in zip(parts, probs, dprobs):
                dscore = (p * (d - inner)).astype(BF16)
                term = mm_tn(keys, dscore)
                dquery = term if dquery is None else dquery + term
                dkey, dvalue = mm(dscore, query), mm(p.astype(BF16), dout)
                if name in grads:
                    grads[name] = (grads[name][0] + dkey, grads[name][1] + dvalue)
                else:
                    grads[name] = (dkey, dvalue)
            grad_ref[0, base : base + TILE, :] = (dquery.T * SCALE).astype(BF16)
        for name, (dkey, dvalue) in grads.items():
            dkey, dvalue = (dkey * SCALE).astype(BF16), dvalue.astype(BF16)
            if name is None:
                cgrad_ref[0] = dkey
                cgrad_ref[1] = dvalue
            else:
                where = slice(block * BLK + name * TILE, block * BLK + (name + 1) * TILE)
                grad_ref[1, where, :] = dkey
                grad_ref[2, where, :] = dvalue


def attend_backward(qkv, ckv, dheads, lse):
    length, width = qkv.shape[1], qkv.shape[2]
    heads = width // HD
    pick = lambda s: pl.BlockSpec((1, length, HD), lambda h: (s, 0, h))
    pick_context = lambda s: pl.BlockSpec((1, CTX, HD), lambda h: (s, 0, h))
    return pl.pallas_call(
        attend_backward_kernel,
        grid=(heads,),
        in_specs=[
            pick(0),
            pick(1),
            pick(2),
            pick_context(0),
            pick_context(1),
            pl.BlockSpec((length, HD), lambda h: (0, h)),
            pl.BlockSpec((1, 1, length), lambda h: (h, 0, 0)),
        ],
        out_specs=[
            pl.BlockSpec((3, length, HD), lambda h: (0, 0, h)),
            pl.BlockSpec((2, CTX, HD), lambda h: (0, 0, h)),
        ],
        out_shape=[
            jax.ShapeDtypeStruct((3, length, width), BF16),
            jax.ShapeDtypeStruct((2, CTX, width), BF16),
        ],
        cost_estimate=brief(),
        name="attend_backward",
    )(qkv, qkv, qkv, ckv, ckv, dheads, lse)


def brief():
    return pl.CostEstimate(flops=1 << 32, bytes_accessed=1 << 16, transcendentals=0)


def roomy():
    return pltpu.CompilerParams(vmem_limit_bytes=56 << 20)


def place_rows(where_ref, tall_ref, out_ref, count, depth):
    size = tall_ref.shape[0] // count
    tail = count >> depth
    low = where_ref[1] & ((1 << depth) - 1)
    for p in range(count):
        code = sum(((p // tail >> (depth - 1 - b)) & 1) << b for b in range(depth))
        start = pl.multiple_of(((p % tail) * (1 << depth) + (low ^ code)) * size, size)
        out_ref[p * size : (p + 1) * size, :] = tall_ref[pl.ds(start, size), :]


def whole_block(shape):
    return pl.BlockSpec(shape, lambda *_: (0,) * len(shape), pipeline_mode=pl.Buffered(1))


def normalize(values):
    center = values - jnp.mean(values, axis=-1, keepdims=True)
    rstd = lax.rsqrt(jnp.mean(center * center, axis=-1, keepdims=True) + EPS)
    return center * rstd, rstd


def normalize_backward(grad, hat, rstd, gain):
    dn = grad * gain
    return rstd * (dn - jnp.mean(dn, axis=-1, keepdims=True) - hat * jnp.mean(dn * hat, axis=-1, keepdims=True))


def first_norm(where, layer_in, cotangent, gain, bias, count):
    length, width = layer_in.shape[2:]
    step = 256

    def kernel(where_ref, x_ref, dy_ref, gain_ref, bias_ref, u_ref, ut_ref, dyt_ref, tall):
        hat, _ = normalize(x_ref[0, 0].astype(F32))
        u = (hat * gain_ref[...] + bias_ref[...]).astype(BF16)
        u_ref[...] = u
        tall[...] = u.T
        place_rows(where_ref, tall, ut_ref, count, 2)
        tall[...] = dy_ref[0, 0].T
        place_rows(where_ref, tall, dyt_ref, count, 1)

    mine = lambda i, w: (w[0], 0, i, 0)
    return pl.pallas_call(
        kernel,
        grid_spec=pltpu.PrefetchScalarGridSpec(
            num_scalar_prefetch=1,
            grid=(length // step,),
            in_specs=[
                pl.BlockSpec((1, 1, step, width), mine),
                pl.BlockSpec((1, 1, step, width), mine),
                whole_block((1, width)),
                whole_block((1, width)),
            ],
            out_specs=[
                pl.BlockSpec((step, width), lambda i, w: (i, 0)),
                pl.BlockSpec((width, step), lambda i, w: (0, i)),
                pl.BlockSpec((width, step), lambda i, w: (0, i)),
            ],
            scratch_shapes=[pltpu.VMEM((width, step), BF16)],
        ),
        out_shape=[
            jax.ShapeDtypeStruct((length, width), BF16),
            jax.ShapeDtypeStruct((width, length), BF16),
            jax.ShapeDtypeStruct((width, length), BF16),
        ],
        cost_estimate=brief(),
        name="first_norm",
    )(where, layer_in, cotangent, gain, bias)


def context_rows(where, context, count):
    def kernel(where_ref, c_ref, out_ref, tall):
        tall[...] = c_ref[...].T
        place_rows(where_ref, tall, out_ref, count, 2)

    rows, width = context.shape
    return pl.pallas_call(
        kernel,
        in_specs=[pl.BlockSpec(memory_space=pltpu.SMEM), pl.BlockSpec(memory_space=pltpu.VMEM)],
        out_specs=pl.BlockSpec(memory_space=pltpu.VMEM),
        out_shape=jax.ShapeDtypeStruct((width, rows), BF16),
        scratch_shapes=[pltpu.VMEM((width, rows), BF16)],
        cost_estimate=brief(),
        name="context_rows",
    )(where, context)


def attention_out(where, layer_in, heads_own, heads_other, out_own, out_other, gain, bias, count):
    length, width = layer_in.shape[2:]
    group = heads_own.shape[1]
    step = 256

    def kernel(where_ref, x_ref, ho_ref, ht_ref, wo_ref, wt_ref, gain_ref, bias_ref, x1_ref, u_ref, ut_ref, tall):
        x1 = x_ref[0, 0].astype(F32) + mm(ho_ref[...], wo_ref[...]) + mm(ht_ref[...], wt_ref[...])
        x1_ref[...] = x1
        hat, _ = normalize(x1)
        u = (hat * gain_ref[...] + bias_ref[...]).astype(BF16)
        u_ref[...] = u
        tall[...] = u.T
        place_rows(where_ref, tall, ut_ref, count, 2)

    row = lambda i, w: (i, 0)
    return pl.pallas_call(
        kernel,
        grid_spec=pltpu.PrefetchScalarGridSpec(
            num_scalar_prefetch=1,
            grid=(length // step,),
            in_specs=[
                pl.BlockSpec((1, 1, step, width), lambda i, w: (w[0], 0, i, 0)),
                pl.BlockSpec((step, group), row),
                pl.BlockSpec((step, group), row),
                whole_block((group, width)),
                whole_block((group, width)),
                whole_block((1, width)),
                whole_block((1, width)),
            ],
            out_specs=[
                pl.BlockSpec((step, width), row),
                pl.BlockSpec((step, width), row),
                pl.BlockSpec((width, step), lambda i, w: (0, i)),
            ],
            scratch_shapes=[pltpu.VMEM((width, step), BF16)],
        ),
        out_shape=[
            jax.ShapeDtypeStruct((length, width), F32),
            jax.ShapeDtypeStruct((length, width), BF16),
            jax.ShapeDtypeStruct((width, length), BF16),
        ],
        compiler_params=roomy(),
        cost_estimate=brief(),
        name="attention_out",
    )(where, layer_in, heads_own, heads_other, out_own, out_other, gain, bias)


STEP = 1024


def weight_copies(sides, held, sems, axis):
    copies = []
    for ref in sides:
        for j in range(ref.shape[axis] // STEP):
            here = pl.ds(j * STEP, STEP)
            source = ref.at[here, :] if axis == 0 else ref.at[:, here]
            copies.append([pltpu.make_async_copy(source, held.at[len(copies)], sems.at[len(copies)])])
    return copies


def stream_weights(copies):
    step = pl.program_id(0)

    @pl.when(step == 0)
    def _():
        for some in copies:
            for copy in some:
                copy.start()

    for j, some in enumerate(copies):

        @pl.when(step == j)
        def _(some=some):
            for copy in some:
                copy.wait()


ANYWHERE = pl.BlockSpec(memory_space=pl.ANY)


def gelu_pair(pre):
    root = math.sqrt(2.0 / math.pi)
    squared = pre * pre
    bend = jnp.tanh(pre * (root + (root * 0.044715) * squared))
    half = 0.5 + 0.5 * bend
    slope = half + pre * ((0.5 - 0.5 * bend * bend) * (root + (3 * 0.044715 * root) * squared))
    return (pre * half).astype(BF16), slope.astype(BF16)


def hidden_forward(u2, up_own, up_other):
    length, width = u2.shape
    steps = 2 * up_own.shape[1] // STEP
    chunk = 256

    def kernel(u_ref, own_ref, other_ref, hid_ref, slope_ref, held, sems):
        stream_weights(weight_copies((own_ref, other_ref), held, sems, 1))
        j = pl.program_id(0)
        for i in range(length // chunk):
            rows = slice(i * chunk, (i + 1) * chunk)
            hid, slope = gelu_pair(mm(u_ref[rows, :], held[j]))
            hid_ref[rows, :] = hid
            slope_ref[rows, :] = slope

    tile = pl.BlockSpec((length, STEP), lambda j: (0, j))
    return pl.pallas_call(
        kernel,
        grid=(steps,),
        in_specs=[whole_block((length, width))] + [ANYWHERE] * 2,
        out_specs=[tile, tile],
        out_shape=[jax.ShapeDtypeStruct((length, steps * STEP), BF16)] * 2,
        scratch_shapes=[pltpu.VMEM((steps, width, STEP), BF16), pltpu.SemaphoreType.DMA((steps,))],
        compiler_params=roomy(),
        cost_estimate=brief(),
        name="hidden_forward",
    )(u2, up_own, up_other)


def hidden_backward(where, cotangent, down_own, down_other, slope):
    length, width = cotangent.shape[2:]
    steps = 2 * down_own.shape[0] // STEP
    chunk = 256

    def kernel(where_ref, dy_ref, own_ref, other_ref, slope_ref, out_ref, held, sems):
        stream_weights(weight_copies((own_ref, other_ref), held, sems, 0))
        j = pl.program_id(0)
        for i in range(length // chunk):
            rows = slice(i * chunk, (i + 1) * chunk)
            out_ref[rows, :] = (mm_nt(dy_ref[0, 0, rows, :], held[j]) * slope_ref[rows, :].astype(F32)).astype(BF16)

    tile = pl.BlockSpec((length, STEP), lambda j, w: (0, j))
    return pl.pallas_call(
        kernel,
        grid_spec=pltpu.PrefetchScalarGridSpec(
            num_scalar_prefetch=1,
            grid=(steps,),
            in_specs=[
                pl.BlockSpec((1, 1, length, width), lambda j, w: (w[0], 0, 0, 0), pipeline_mode=pl.Buffered(1))
            ]
            + [ANYWHERE] * 2
            + [tile],
            out_specs=tile,
            scratch_shapes=[pltpu.VMEM((steps, STEP, width), BF16), pltpu.SemaphoreType.DMA((steps,))],
        ),
        out_shape=jax.ShapeDtypeStruct((length, steps * STEP), BF16),
        compiler_params=roomy(),
        cost_estimate=brief(),
        name="hidden_backward",
    )(where, cotangent, down_own, down_other, slope)


def hidden_out(hid, down_own, down_other, x1):
    length, width = x1.shape
    steps = 2 * down_own.shape[0] // STEP

    def kernel(hid_ref, own_ref, other_ref, x1_ref, out_ref, held, total, sems):
        stream_weights(weight_copies((own_ref, other_ref), held, sems, 0))
        j = pl.program_id(0)

        @pl.when(j == 0)
        def _():
            total[...] = x1_ref[...]

        total[...] += mm(hid_ref[...], held[j])

        @pl.when(j == steps - 1)
        def _():
            out_ref[...] = total[...].astype(BF16)

    return pl.pallas_call(
        kernel,
        grid=(steps,),
        in_specs=[pl.BlockSpec((length, STEP), lambda j: (0, j))] + [ANYWHERE] * 2 + [whole_block((length, width))],
        out_specs=whole_block((length, width)),
        out_shape=jax.ShapeDtypeStruct((length, width), BF16),
        scratch_shapes=[
            pltpu.VMEM((steps, STEP, width), BF16),
            pltpu.VMEM((length, width), F32),
            pltpu.SemaphoreType.DMA((steps,)),
        ],
        compiler_params=roomy(),
        cost_estimate=brief(),
        name="hidden_out",
    )(hid, down_own, down_other, x1)


def second_norm_backward(where, dpre, up_own, up_other, x1, cotangent, gain, count):
    length, width = x1.shape
    steps = 2 * up_own.shape[1] // STEP
    chunk = 128

    def kernel(where_ref, dpre_ref, own_ref, other_ref, x1_ref, dy_ref, gain_ref, out_ref, outt_ref, sums_ref, held, total, tall, sems):
        stream_weights(weight_copies((own_ref, other_ref), held, sems, 1))
        j = pl.program_id(0)

        @pl.when(j == 0)
        def _():
            total[...] = mm_nt(dpre_ref[...], held[j])
            sums_ref[...] = jnp.zeros_like(sums_ref)

        @pl.when(j > 0)
        def _():
            total[...] += mm_nt(dpre_ref[...], held[j])

        @pl.when(j == steps - 1)
        def _():
            @pl.loop(0, length // chunk)
            def _(i):
                rows = pl.ds(pl.multiple_of(i * chunk, chunk), chunk)
                du = total[rows, :]
                hat, rstd = normalize(x1_ref[rows, :])
                sums_ref[0:1, :] += jnp.sum(du * hat, axis=0, keepdims=True)
                sums_ref[1:2, :] += jnp.sum(du, axis=0, keepdims=True)
                out = dy_ref[0, 0, rows, :].astype(F32) + normalize_backward(du, hat, rstd, gain_ref[...])
                out = out.astype(BF16)
                out_ref[rows, :] = out
                tall[:, rows] = out.T

            place_rows(where_ref, tall, outt_ref, count, 2)

    mine = pl.BlockSpec((1, 1, length, width), lambda j, w: (w[0], 0, 0, 0), pipeline_mode=pl.Buffered(1))
    return pl.pallas_call(
        kernel,
        grid_spec=pltpu.PrefetchScalarGridSpec(
            num_scalar_prefetch=1,
            grid=(steps,),
            in_specs=[pl.BlockSpec((length, STEP), lambda j, w: (0, j))]
            + [ANYWHERE] * 2
            + [whole_block((length, width)), mine, whole_block((1, width))],
            out_specs=[whole_block((length, width)), whole_block((width, length)), whole_block((2, width))],
            scratch_shapes=[
                pltpu.VMEM((steps, width, STEP), BF16),
                pltpu.VMEM((length, width), F32),
                pltpu.VMEM((width, length), BF16),
                pltpu.SemaphoreType.DMA((steps,)),
            ],
        ),
        out_shape=[
            jax.ShapeDtypeStruct((length, width), BF16),
            jax.ShapeDtypeStruct((width, length), BF16),
            jax.ShapeDtypeStruct((2, width), F32),
        ],
        compiler_params=roomy(),
        cost_estimate=brief(),
        name="second_norm_backward",
    )(where, dpre, up_own, up_other, x1, cotangent, gain)


def first_norm_backward(where, dsides, qkv_own, qkv_other, du_ssm, layer_in, dattn, gain):
    length, width = layer_in.shape[2:]
    group = qkv_own.shape[2]
    chunk = 128
    steps = 6

    def kernel(where_ref, do_ref, dt_ref, own_ref, other_ref, ssm_ref, x_ref, dx_ref, gain_ref, out_ref, sums_ref, held, grads, total, sems):
        copies = [
            [
                pltpu.make_async_copy(grad.at[s], grads.at[3 * k + s], sems.at[3 * k + s, 0]),
                pltpu.make_async_copy(weight.at[s], held.at[3 * k + s], sems.at[3 * k + s, 1]),
            ]
            for k, (grad, weight) in enumerate(((do_ref, own_ref), (dt_ref, other_ref)))
            for s in range(3)
        ]
        stream_weights(copies)
        j = pl.program_id(0)

        @pl.when(j == 0)
        def _():
            total[0 : ssm_ref.shape[0], :] = ssm_ref[...]
            total[ssm_ref.shape[0] :, :] = jnp.zeros((length - ssm_ref.shape[0], width), F32)
            sums_ref[...] = jnp.zeros_like(sums_ref)

        total[...] += mm_nt(grads[j], held[j])

        @pl.when(j == steps - 1)
        def _():
            @pl.loop(0, length // chunk)
            def _(i):
                rows = pl.ds(pl.multiple_of(i * chunk, chunk), chunk)
                du = total[rows, :]
                hat, rstd = normalize(x_ref[0, 0, rows, :].astype(F32))
                sums_ref[0:1, :] += jnp.sum(du * hat, axis=0, keepdims=True)
                sums_ref[1:2, :] += jnp.sum(du, axis=0, keepdims=True)
                out = dx_ref[rows, :].astype(F32) + normalize_backward(du, hat, rstd, gain_ref[...])
                out_ref[rows, :] = out.astype(BF16)

    mine = pl.BlockSpec((1, 1, length, width), lambda j, w: (w[0], 0, 0, 0), pipeline_mode=pl.Buffered(1))
    return pl.pallas_call(
        kernel,
        grid_spec=pltpu.PrefetchScalarGridSpec(
            num_scalar_prefetch=1,
            grid=(steps,),
            in_specs=[ANYWHERE] * 4
            + [whole_block(du_ssm.shape), mine, whole_block((length, width)), whole_block((1, width))],
            out_specs=[whole_block((length, width)), whole_block((2, width))],
            scratch_shapes=[
                pltpu.VMEM((steps, width, group), BF16),
                pltpu.VMEM((steps, length, group), BF16),
                pltpu.VMEM((length, width), F32),
                pltpu.SemaphoreType.DMA((steps, 2)),
            ],
        ),
        out_shape=[jax.ShapeDtypeStruct((length, width), BF16), jax.ShapeDtypeStruct((2, width), F32)],
        compiler_params=roomy(),
        cost_estimate=brief(),
        name="first_norm_backward",
    )(where, dsides[0], dsides[1], qkv_own, qkv_other, du_ssm, layer_in, dattn, gain)


def down_rows(left, right, got):
    width, length = left.shape
    half = width // 2
    columns = right.shape[1]

    def kernel(left_ref, right_ref, *rest):
        total = mm(left_ref[...], right_ref[...])
        if got is not None:
            total += rest[0][...].astype(F32)
        rest[-1][...] = total.astype(BF16)

    tile = pl.BlockSpec((half, STEP), lambda j: (0, j))
    pick = 1 if got is None else 0
    return pl.pallas_call(
        kernel,
        grid=(columns // STEP,),
        in_specs=[
            pl.BlockSpec((half, length), lambda j: (pick, 0), pipeline_mode=pl.Buffered(1)),
            pl.BlockSpec((length, STEP), lambda j: (0, j)),
        ]
        + ([] if got is None else [tile]),
        out_specs=tile,
        out_shape=jax.ShapeDtypeStruct((half, columns), BF16),
        compiler_params=roomy(),
        cost_estimate=brief(),
        name="down_sent" if got is None else "down_kept",
    )(left, right, *([] if got is None else [got]))


def up_rows(left, right, out_left, heads_own, heads_other, got):
    width, length = left.shape
    half = width // 2
    quart = width // 4
    columns = right.shape[1]
    group = heads_own.shape[1]
    tile = group
    ups = columns // 2 // tile
    steps = 2 * (ups + 1)
    keeping = got is not None

    def kernel(left_ref, right_ref, out_left_ref, own_ref, other_ref, *rest):
        j = pl.program_id(0)

        def emit(lref, rref, swap):
            for part in range(2 if keeping else 1):
                rows = slice(part * quart, (part + 1) * quart) if keeping else slice(0, half)
                total = mm(lref[rows, :], rref[...])
                if not keeping:
                    rest[0][...] = total.astype(BF16)
                    continue
                come = rest[0][rows, :].astype(F32)
                if swap:
                    come = jnp.concatenate([come[:, tile // 2 :], come[:, : tile // 2]], axis=1)
                rest[1 + part][...] = (total + come).astype(BF16)

        @pl.when(lax.rem(j, ups + 1) < ups)
        def _():
            emit(left_ref, right_ref, False)

        @pl.when(j == ups)
        def _():
            emit(out_left_ref, own_ref, False)

        @pl.when(j == 2 * ups + 1)
        def _():
            emit(out_left_ref, other_ref, True)

    pick = 0 if keeping else 1
    side = pl.BlockSpec((half, length), lambda j: (pick, 0), pipeline_mode=pl.Buffered(1))
    up_tile = lambda j: jnp.where(j <= ups, jnp.minimum(j, ups - 1), jnp.minimum(j - 1, 2 * ups - 1))
    in_specs = [
        side,
        pl.BlockSpec((length, tile), lambda j: (0, up_tile(j))),
        side,
        whole_block((length, group)),
        whole_block((length, group)),
    ]
    operands = [left, right, out_left, heads_own, heads_other]
    total_columns = steps * tile
    if keeping:
        in_specs.append(pl.BlockSpec((half, tile), lambda j: (0, j)))
        operands.append(got)
        out_specs = [pl.BlockSpec((quart, tile), lambda j: (0, j))] * 2
        out_shape = [jax.ShapeDtypeStruct((quart, total_columns), BF16)] * 2
    else:
        out_specs = pl.BlockSpec((half, tile), lambda j: (0, j))
        out_shape = jax.ShapeDtypeStruct((half, total_columns), BF16)
    return pl.pallas_call(
        kernel,
        grid=(steps,),
        in_specs=in_specs,
        out_specs=out_specs,
        out_shape=out_shape,
        compiler_params=roomy(),
        cost_estimate=brief(),
        name="up_kept" if keeping else "up_sent",
    )(*operands)


def group_rows(left, own, other, extra, got):
    width, length = left.shape
    half = width // 2
    quart = width // 4
    count, _, group = own.shape
    piece = group // 2
    keeping = got is not None

    def kernel(*refs):
        refs = list(refs)
        left_ref, sides = refs.pop(0), [refs.pop(0), refs.pop(0)]
        if extra is not None:
            cleft_ref, csides = refs.pop(0), [refs.pop(0), refs.pop(0)]
        got_ref = refs.pop(0) if keeping else None
        j = pl.program_id(0)
        for side in range(2):

            @pl.when((j >= count) if side else (j < count))
            def _(side=side):
                for part in range(2 if keeping else 1):
                    rows = slice(part * quart, (part + 1) * quart) if keeping else slice(0, half)
                    total = mm(left_ref[rows, :], sides[side][0])
                    if extra is not None:
                        term = mm(cleft_ref[rows, :], csides[side][0])
                        total += jnp.where(lax.rem(j, count) > 0, term, 0.0)
                    if not keeping:
                        refs[0][...] = total.astype(BF16)
                        continue
                    for k in range(2):
                        here = slice(k * piece, (k + 1) * piece)
                        come = k ^ side
                        there = slice(come * piece, (come + 1) * piece)
                        refs[part][:, here] = (total[:, here] + got_ref[rows, there].astype(F32)).astype(BF16)

    first = lambda j: jnp.minimum(j, count - 1)
    second = lambda j: jnp.maximum(j - count, 0)
    before = lambda s: jnp.maximum(s - 1, 0)
    pick = 0 if keeping else 1
    in_specs = [
        pl.BlockSpec((half, length), lambda j: (pick, 0), pipeline_mode=pl.Buffered(1)),
        pl.BlockSpec((1, length, group), lambda j: (first(j), 0, 0)),
        pl.BlockSpec((1, length, group), lambda j: (second(j), 0, 0)),
    ]
    operands = [left, own, other]
    if extra is not None:
        rows = extra[0].shape[1]
        in_specs += [
            pl.BlockSpec((half, rows), lambda j: (pick, 0), pipeline_mode=pl.Buffered(1)),
            pl.BlockSpec((1, rows, group), lambda j: (before(first(j)), 0, 0)),
            pl.BlockSpec((1, rows, group), lambda j: (before(second(j)), 0, 0)),
        ]
        operands += list(extra)
    columns = 2 * count * group
    if keeping:
        in_specs.append(pl.BlockSpec((half, group), lambda j: (0, j)))
        operands.append(got)
        out_specs = [pl.BlockSpec((quart, group), lambda j: (0, j))] * 2
        out_shape = [jax.ShapeDtypeStruct((quart, columns), BF16)] * 2
    else:
        out_specs = pl.BlockSpec((half, group), lambda j: (0, j))
        out_shape = jax.ShapeDtypeStruct((half, columns), BF16)
    return pl.pallas_call(
        kernel,
        grid=(2 * count,),
        in_specs=in_specs,
        out_specs=out_specs,
        out_shape=out_shape,
        compiler_params=roomy(),
        cost_estimate=brief(),
        name="group_kept" if keeping else "group_sent",
    )(*operands)


def swap_halves(values, width):
    half = width // 2
    order = [start + half * k for start in range(0, values.shape[1], width) for k in (1, 0)]
    return jnp.concatenate([values[:, i : i + half] for i in order], axis=1)


def shards(
    dp_count,
    layer_in,
    ln1_gain,
    ln1_bias,
    qkv_weight,
    out_weight,
    ssm_coef,
    ssm_skip,
    ln2_gain,
    ln2_bias,
    up_weight,
    down_weight,
    cotangent,
):
    width = layer_in.shape[3]
    group = qkv_weight.shape[2]
    mine = lax.axis_index("tensor")
    place = lax.axis_index("dp")
    where = jnp.stack([mine, place]).astype(jnp.int32)
    rows_each = width // dp_count
    gain1, bias1, gain2, bias2 = ln1_gain[None], ln1_bias[None], ln2_gain[None], ln2_bias[None]

    over_x = lambda v: swap(v, "tensor", 1, 2)
    over = lambda v, bit: swap(v, "dp", 1 << bit, dp_count)
    core = place & 1

    def scatter(values, depth):
        groups = [[(k << depth) | low for k in range(dp_count >> depth)] for low in range(1 << depth)]
        return lax.psum_scatter(values, "dp", scatter_dimension=0, axis_index_groups=groups, tiled=True)

    def part_of(weight, axis, index, count):
        size = weight.shape[axis] // count
        return lax.dynamic_slice_in_dim(weight, index * size, size, axis)

    small = over_x(jnp.concatenate([ssm_coef, ssm_skip[None]], axis=0))
    up_part = over_x(part_of(up_weight, 0, place, dp_count))
    qkv_first = over_x(part_of(qkv_weight, 2, core, 2))
    down_part = over_x(part_of(down_weight, 0, place, dp_count))
    out_first = over_x(part_of(out_weight, 0, core, 2))

    def in_order(own, other, axis):
        return jnp.where(
            mine == 0, jnp.concatenate([own, other], axis=axis), jnp.concatenate([other, own], axis=axis)
        )

    coef = in_order(ssm_coef, small[:NS], 1)
    skip = in_order(ssm_skip[None], small[NS:], 1)

    u1, u1_rows, dy_rows = first_norm(where, layer_in, cotangent, gain1, bias1, dp_count)

    def project(rows, weight):
        return jnp.einsum("td,sde->ste", rows, weight, preferred_element_type=F32).astype(BF16)

    up_other = lax.all_gather(up_part, "dp", axis=0, tiled=True)
    qkv_own = project(tie(u1, up_part), qkv_weight)
    down_other = lax.all_gather(tie(down_part, qkv_own), "dp", axis=0, tiled=True)
    context, state = ssm_forward(tie(u1, qkv_own, down_part), coef, skip)
    context_turned = context_rows(tie(where, context), context, dp_count)
    ckv_own = project(tie(context, context_turned), qkv_weight[1:])
    heads_own, lse_own = attend_forward(qkv_own, ckv_own)
    qkv_first = tie(qkv_first, heads_own)
    qkv_other_weight = jnp.concatenate([qkv_first, over(qkv_first, 0)], axis=2)
    qkv_other = project(tie(u1, heads_own), qkv_other_weight)
    ckv_other = project(context, qkv_other_weight[1:])
    out_first = tie(out_first, qkv_other)
    out_second = over(out_first, 0)
    heads_other, lse_other = attend_forward(qkv_other, tie(ckv_other, out_first))
    out_other = jnp.concatenate([out_first, tie(out_second, heads_other)], axis=0)
    x1, u2, u2_rows = attention_out(
        where, layer_in, heads_own, heads_other, out_weight, out_other, gain2, bias2, dp_count
    )
    hid, slope = hidden_forward(u2, up_weight, up_other)

    down_mine = down_rows(dy_rows, hid, None)
    down_got = over(down_mine, 0)
    dpre = hidden_backward(tie(where, down_mine), cotangent, down_weight, down_other, slope)
    down_kept = down_rows(tie(dy_rows, dpre), hid, tie(down_got, dpre))
    down_sum = scatter(down_kept, 1)
    dattn, dattn_rows, sums2 = second_norm_backward(
        tie(where, down_kept), dpre, up_weight, up_other, x1, cotangent, gain2, dp_count
    )
    up_mine = up_rows(u2_rows, dpre, dattn_rows, heads_own, heads_other, None)
    up_got = over(up_mine, 0)
    layer_out = hidden_out(hid, down_weight, down_other, tie(x1, up_mine))
    layer_out_other = over_x(layer_out)
    up_keep, up_send = up_rows(tie(u2_rows, layer_out), dpre, dattn_rows, heads_own, heads_other, tie(up_got, layer_out))
    up_got = over(up_send, 1)
    dattn_then = tie(dattn, up_keep)
    dheads_other = mm_nt(dattn_then, out_other).astype(BF16)
    dheads_own = mm_nt(dattn_then, out_weight).astype(BF16)
    dqkv_other, dckv_other = attend_backward(qkv_other, ckv_other, tie(dheads_other, dheads_own), lse_other)
    dqkv_own, dckv_own = attend_backward(qkv_own, ckv_own, tie(dheads_own, dqkv_other), lse_own)

    extra = (context_turned, dckv_own, dckv_other)
    layer_out_other, down_sum = tie(layer_out_other, dqkv_own), tie(down_sum, dqkv_own)
    down_cross = down_sum[:, down_sum.shape[1] // 2 :]
    qkv_mine = group_rows(tie(u1_rows, layer_out_other, down_cross), dqkv_own, dqkv_other, extra, None)
    qkv_got = over(qkv_mine, 0)
    dckv_then = tie(dckv_own, qkv_mine)
    dcontext = jnp.einsum("sce,sde->cd", dckv_then, qkv_weight[1:], preferred_element_type=F32)
    dcontext += jnp.einsum("sce,sde->cd", dckv_other, qkv_other_weight[1:], preferred_element_type=F32)
    du_ssm, small_ssm = ssm_backward(u1, dcontext, coef, skip, state)
    up_sum = (up_keep.astype(F32) + tie(up_got, du_ssm)).astype(BF16)
    qkv_keep, qkv_send = group_rows(
        tie(u1_rows, du_ssm, up_sum), dqkv_own, dqkv_other, extra, tie(qkv_got, du_ssm)
    )
    up_sum = scatter(up_sum, 2)
    qkv_got = over(qkv_send, 1)
    grad_in, sums1 = first_norm_backward(
        tie(where, qkv_keep),
        (dqkv_own, dqkv_other),
        qkv_weight,
        qkv_other_weight,
        du_ssm,
        layer_in,
        dattn,
        gain1,
    )
    grad_in_other = over_x(grad_in)
    qkv_sum = (qkv_keep.astype(F32) + tie(qkv_got, grad_in)).astype(BF16)

    small_all = jnp.concatenate([small_ssm, sums2, sums1], axis=0)
    small_all = small_all + tie(over_x(small_all), qkv_sum)
    qkv_sum = scatter(qkv_sum, 2)
    for bit in range(dp_count.bit_length() - 1):
        small_all = small_all + over(small_all, bit)
    here = lax.dynamic_slice_in_dim(small_all[: NS + 1], mine * group, group, 1)

    def cross(values):
        half = values.shape[1] // 2
        return values[:, :half].astype(F32), over_x(values[:, half:]).astype(F32)

    def ordered(values):
        return jnp.where(core == 1, swap_halves(values, group), values)

    down_own, down_come = cross(down_sum)
    up_own, up_come = cross(up_sum)
    qkv_mine, qkv_come = cross(qkv_sum)
    hidden = up_weight.shape[1]
    grad_down = down_own + down_come
    grad_up = up_own[:, :hidden] + up_come[:, :hidden]
    grad_out = up_own[:, hidden:] + ordered(up_come[:, hidden:])
    grad_qkv = qkv_mine + ordered(qkv_come)

    def both_parts(own, other):
        return jnp.where(mine == 0, jnp.stack([own, other]), jnp.stack([other, own]))[:, None]

    return (
        both_parts(layer_out, layer_out_other),
        both_parts(grad_in, grad_in_other).astype(F32),
        small_all[NS + 3],
        small_all[NS + 4],
        grad_qkv.reshape(rows_each, 3, group).swapaxes(0, 1),
        grad_out.T,
        here[:NS],
        here[NS],
        small_all[NS + 1],
        small_all[NS + 2],
        grad_up,
        grad_down.T,
    )


def solution(mesh):
    in_specs = (
        P(None, "dp", None, None),
        P(),
        P(),
        P(None, None, "tensor"),
        P("tensor", None),
        P(None, "tensor"),
        P("tensor"),
        P(),
        P(),
        P(None, "tensor"),
        P("tensor", None),
        P(None, "dp", None, None),
    )
    out_specs = (
        P(None, "dp", None, None),
        P(None, "dp", None, None),
        P(),
        P(),
        P(None, "dp", "tensor"),
        P("tensor", "dp"),
        P(None, "tensor"),
        P("tensor"),
        P(),
        P(),
        P("dp", "tensor"),
        P("tensor", "dp"),
    )
    body = functools.partial(shards, mesh.shape["dp"])
    return jax.shard_map(body, mesh=mesh, in_specs=in_specs, out_specs=out_specs, check_vma=False)
```

```python
import functools
import math

import jax
import jax.numpy as jnp
from jax import lax
from jax.experimental import pallas as pl
from jax.experimental.pallas import tpu as pltpu
from jax.sharding import PartitionSpec as P
import numpy as np

HD = 128
NS = 16
BLK = 512
CTX = 128
CH = 128
TILE = 256
EPS = 1e-05
F32 = jnp.float32
BF16 = jnp.bfloat16
HIGHEST = lax.Precision.HIGHEST
SCALE = HD**-0.5
LOG2 = SCALE * math.log2(math.e)


def swap(value, axis, mask, count):
    return lax.ppermute(value, axis, [(i, i ^ mask) for i in range(count)])


def tie(value, *deps):
    return lax.optimization_barrier((value, *deps))[0] if deps else value


def mm(left, right):
    return lax.dot_general(left, right, (((1,), (0,)), ((), ())), preferred_element_type=F32)


def mm_nt(left, right):
    return lax.dot_general(left, right, (((1,), (1,)), ((), ())), preferred_element_type=F32)


def mm_tn(left, right):
    return lax.dot_general(left, right, (((0,), (0,)), ((), ())), preferred_element_type=F32)


def decay_constants():
    rates = 4.0 / CH * np.exp2(-8.0 * np.arange(NS, dtype=np.float64) / (NS - 1))
    return rates, np.sqrt(-np.expm1(-2.0 * rates))


RATES, NORMS = decay_constants()


def decay_within(n, transposed):
    rows = lax.broadcasted_iota(jnp.int32, (CH, CH), 0)
    columns = lax.broadcasted_iota(jnp.int32, (CH, CH), 1)
    offset = columns - rows if transposed else rows - columns
    powers = jnp.exp(offset.astype(F32) * -float(RATES[n]))
    return jnp.where(offset >= 0, float(NORMS[n]) * powers, 0.0).astype(BF16)


def decay_vectors(rates, norms):
    steps = lax.broadcasted_iota(jnp.int32, (NS, CH), 1).astype(F32)
    carry_in = jnp.exp(-rates * (steps + 1.0))
    carry_out = (norms * jnp.exp(-rates * (CH - 1.0 - steps))).astype(BF16)
    return carry_in, carry_out, jnp.exp(-rates * CH)


def ssm_forward_kernel(v_ref, rates_ref, norms_ref, coef_ref, skip_ref, out_ref, state_ref, within_ref):
    @pl.when(pl.program_id(0) == 0)
    def _():
        for n in range(NS):
            within_ref[n] = decay_within(n, False)

    carry_in, carry_out, whole = decay_vectors(rates_ref[...], norms_ref[...])
    before = BLK // CH - 1
    state = jnp.zeros(state_ref.shape, F32)
    for k in range(before):
        state = whole * state + mm(carry_out, v_ref[k * CH : (k + 1) * CH, :])
    state_ref[...] = state
    rows = v_ref[before * CH :, :]
    total = skip_ref[...] * rows.astype(F32)
    total += lax.dot_general(
        carry_in, coef_ref[...] * state, (((0,), (0,)), ((), ())), precision=HIGHEST, preferred_element_type=F32
    )
    for n in range(NS):
        total += coef_ref[n : n + 1, :] * mm(within_ref[n], rows)
    out_ref[...] = total.astype(BF16)


def decay_arrays():
    return jnp.asarray(RATES[:, None], F32), jnp.asarray(NORMS[:, None], F32)


def ssm_forward(rows, coef, skip):
    width = rows.shape[1]
    step = 256
    column = lambda c: (0, c)
    fixed = pl.BlockSpec((NS, 1), lambda c: (0, 0))
    return pl.pallas_call(
        ssm_forward_kernel,
        grid=(width // step,),
        in_specs=[
            pl.BlockSpec((BLK, step), column),
            fixed,
            fixed,
            pl.BlockSpec((NS, step), column),
            pl.BlockSpec((1, step), column),
        ],
        out_specs=[pl.BlockSpec((CH, step), column), pl.BlockSpec((NS, step), column)],
        out_shape=[jax.ShapeDtypeStruct((CH, width), BF16), jax.ShapeDtypeStruct((NS, width), F32)],
        scratch_shapes=[pltpu.VMEM((NS, CH, CH), BF16)],
        cost_estimate=brief(20),
        name="ssm_forward",
    )(rows, *decay_arrays(), coef, skip)


def key_parts(block, tile, k_ref, v_ref, ck_ref, cv_ref):
    parts = []
    if block > 0:
        parts.append((None, ck_ref[0], cv_ref[0], False))
    for piece in range(tile + 1):
        where = slice(block * BLK + piece * TILE, block * BLK + (piece + 1) * TILE)
        parts.append((piece, k_ref[0, where, :], v_ref[0, where, :], piece == tile))
    return parts


def tile_scores(keys, query, masked):
    scores = mm_nt(keys, query)
    if masked:
        key_ids = lax.broadcasted_iota(jnp.int32, scores.shape, 0)
        query_ids = lax.broadcasted_iota(jnp.int32, scores.shape, 1)
        scores = jnp.where(key_ids <= query_ids, scores, -1e30)
    return scores


def attend_forward_kernel(q_ref, k_ref, v_ref, ck_ref, cv_ref, out_ref, lse_ref):
    for block in range(2):
        for tile in range(BLK // TILE):
            base = block * BLK + tile * TILE
            query = q_ref[0, base : base + TILE, :]
            parts = key_parts(block, tile, k_ref, v_ref, ck_ref, cv_ref)
            scores = [tile_scores(keys, query, masked) for _, keys, _, masked in parts]
            top = functools.reduce(jnp.maximum, [jnp.max(s, axis=0, keepdims=True) for s in scores]) * LOG2
            exps = [jnp.exp2(s * LOG2 - top) for s in scores]
            total = functools.reduce(jnp.add, [jnp.sum(e, axis=0, keepdims=True) for e in exps])
            inverse = 1.0 / total
            out = functools.reduce(
                jnp.add,
                [mm_tn(values, (e * inverse).astype(BF16)) for (_, _, values, _), e in zip(parts, exps)],
            )
            out_ref[base : base + TILE, :] = out.T.astype(BF16)
            lse_ref[0, :, base : base + TILE] = top + jnp.log2(total)


def attend_forward(qkv, ckv):
    length, width = qkv.shape[1], qkv.shape[2]
    heads = width // HD
    pick = lambda s: pl.BlockSpec((1, length, HD), lambda h: (s, 0, h))
    pick_context = lambda s: pl.BlockSpec((1, CTX, HD), lambda h: (s, 0, h))
    return pl.pallas_call(
        attend_forward_kernel,
        grid=(heads,),
        in_specs=[pick(0), pick(1), pick(2), pick_context(0), pick_context(1)],
        out_specs=[
            pl.BlockSpec((length, HD), lambda h: (0, h)),
            pl.BlockSpec((1, 1, length), lambda h: (h, 0, 0)),
        ],
        out_shape=[
            jax.ShapeDtypeStruct((length, width), BF16),
            jax.ShapeDtypeStruct((heads, 1, length), F32),
        ],
        cost_estimate=brief(20),
        name="attend_forward",
    )(qkv, qkv, qkv, ckv, ckv)


def attend_backward_kernel(q_ref, k_ref, v_ref, ck_ref, cv_ref, dout_ref, lse_ref, grad_ref, cgrad_ref):
    for block in range(2):
        grads = {}
        for tile in range(BLK // TILE):
            base = block * BLK + tile * TILE
            query = q_ref[0, base : base + TILE, :]
            dout = dout_ref[0, base : base + TILE, :]
            lse = lse_ref[0, :, base : base + TILE]
            parts = key_parts(block, tile, k_ref, v_ref, ck_ref, cv_ref)
            probs = [jnp.exp2(tile_scores(keys, query, masked) * LOG2 - lse) for _, keys, _, masked in parts]
            dprobs = [mm_nt(values, dout) for _, _, values, _ in parts]
            inner = functools.reduce(
                jnp.add, [jnp.sum(p * d, axis=0, keepdims=True) for p, d in zip(probs, dprobs)]
            )
            dquery = None
            for (name, keys, _, _), p, d in zip(parts, probs, dprobs):
                dscore = (p * (d - inner)).astype(BF16)
                term = mm_tn(keys, dscore)
                dquery = term if dquery is None else dquery + term
                dkey, dvalue = mm(dscore, query), mm(p.astype(BF16), dout)
                if name in grads:
                    grads[name] = (grads[name][0] + dkey, grads[name][1] + dvalue)
                else:
                    grads[name] = (dkey, dvalue)
            grad_ref[0, base : base + TILE, :] = (dquery.T * SCALE).astype(BF16)
        for name, (dkey, dvalue) in grads.items():
            dkey, dvalue = (dkey * SCALE).astype(BF16), dvalue.astype(BF16)
            if name is None:
                cgrad_ref[0] = dkey
                cgrad_ref[1] = dvalue
            else:
                where = slice(block * BLK + name * TILE, block * BLK + (name + 1) * TILE)
                grad_ref[1, where, :] = dkey
                grad_ref[2, where, :] = dvalue


def attend_backward(qkv, ckv, dheads, side, lse):
    length, width = qkv.shape[1], qkv.shape[2]
    heads = width // HD
    pick = lambda s: pl.BlockSpec((1, length, HD), lambda h: (s, 0, h))
    pick_context = lambda s: pl.BlockSpec((1, CTX, HD), lambda h: (s, 0, h))
    return pl.pallas_call(
        attend_backward_kernel,
        grid=(heads,),
        in_specs=[
            pick(0),
            pick(1),
            pick(2),
            pick_context(0),
            pick_context(1),
            pl.BlockSpec((1, length, HD), lambda h: (side, 0, h)),
            pl.BlockSpec((1, 1, length), lambda h: (h, 0, 0)),
        ],
        out_specs=[
            pl.BlockSpec((3, length, HD), lambda h: (0, 0, h)),
            pl.BlockSpec((2, CTX, HD), lambda h: (0, 0, h)),
        ],
        out_shape=[
            jax.ShapeDtypeStruct((3, length, width), BF16),
            jax.ShapeDtypeStruct((2, CTX, width), BF16),
        ],
        cost_estimate=brief(),
        name="attend_backward",
    )(qkv, qkv, qkv, ckv, ckv, dheads, lse)


def brief(power=32):
    return pl.CostEstimate(flops=1 << power, bytes_accessed=1 << 16, transcendentals=0)


def roomy():
    return pltpu.CompilerParams(vmem_limit_bytes=56 << 20)


def place_rows(where_ref, tall_ref, out_ref, count):
    size = tall_ref.shape[0] // count
    core = where_ref[1] & 1
    for p in range(count):
        start = pl.multiple_of((p % (count // 2) * 2 + (core ^ (p // (count // 2)))) * size, size)
        out_ref[p * size : (p + 1) * size, :] = tall_ref[pl.ds(start, size), :]


def whole_block(shape):
    return pl.BlockSpec(shape, lambda *_: (0,) * len(shape), pipeline_mode=pl.Buffered(1))


def normalize(values):
    center = values - jnp.mean(values, axis=-1, keepdims=True)
    rstd = lax.rsqrt(jnp.mean(center * center, axis=-1, keepdims=True) + EPS)
    return center * rstd, rstd


def normalize_backward(grad, hat, rstd, gain):
    dn = grad * gain
    return rstd * (dn - jnp.mean(dn, axis=-1, keepdims=True) - hat * jnp.mean(dn * hat, axis=-1, keepdims=True))


def turn_rows(where, values, count):
    length, width = values.shape[2:]
    step = 256

    def kernel(where_ref, x_ref, out_ref, tall):
        tall[...] = x_ref[0, 0].T
        place_rows(where_ref, tall, out_ref, count)

    return pl.pallas_call(
        kernel,
        grid_spec=pltpu.PrefetchScalarGridSpec(
            num_scalar_prefetch=1,
            grid=(length // step,),
            in_specs=[pl.BlockSpec((1, 1, step, width), lambda i, w: (w[0], 0, i, 0))],
            out_specs=pl.BlockSpec((width, step), lambda i, w: (0, i)),
            scratch_shapes=[pltpu.VMEM((width, step), BF16)],
        ),
        out_shape=jax.ShapeDtypeStruct((width, length), BF16),
        cost_estimate=brief(),
        name="turn_rows",
    )(where, values)


def first_norm(where, layer_in, gain, bias, count):
    length, width = layer_in.shape[2:]
    step = 256

    def kernel(where_ref, x_ref, gain_ref, bias_ref, u_ref, ut_ref, tall):
        hat, _ = normalize(x_ref[0, 0].astype(F32))
        u = (hat * gain_ref[...] + bias_ref[...]).astype(BF16)
        u_ref[...] = u
        tall[...] = u.T
        place_rows(where_ref, tall, ut_ref, count)

    return pl.pallas_call(
        kernel,
        grid_spec=pltpu.PrefetchScalarGridSpec(
            num_scalar_prefetch=1,
            grid=(length // step,),
            in_specs=[
                pl.BlockSpec((1, 1, step, width), lambda i, w: (w[0], 0, i, 0)),
                whole_block((1, width)),
                whole_block((1, width)),
            ],
            out_specs=[
                pl.BlockSpec((step, width), lambda i, w: (i, 0)),
                pl.BlockSpec((width, step), lambda i, w: (0, i)),
            ],
            scratch_shapes=[pltpu.VMEM((width, step), BF16)],
        ),
        out_shape=[
            jax.ShapeDtypeStruct((length, width), BF16),
            jax.ShapeDtypeStruct((width, length), BF16),
        ],
        cost_estimate=brief(),
        name="first_norm",
    )(where, layer_in, gain, bias)


def context_rows(where, context, count):
    def kernel(where_ref, c_ref, out_ref, tall):
        tall[...] = c_ref[...].T
        place_rows(where_ref, tall, out_ref, count)

    rows, width = context.shape
    return pl.pallas_call(
        kernel,
        in_specs=[pl.BlockSpec(memory_space=pltpu.SMEM), pl.BlockSpec(memory_space=pltpu.VMEM)],
        out_specs=pl.BlockSpec(memory_space=pltpu.VMEM),
        out_shape=jax.ShapeDtypeStruct((width, rows), BF16),
        scratch_shapes=[pltpu.VMEM((width, rows), BF16)],
        cost_estimate=brief(20),
        name="context_rows",
    )(where, context)


def project(u1, context, weights):
    length, width = u1.shape
    rows = context.shape[0]
    sizes = [w.shape[2] for w in weights]
    group = sum(sizes)

    def kernel(u_ref, c_ref, *refs):
        qkv_ref, ckv_ref, weight_s = refs[len(weights) :]
        start = 0
        for ref, size in zip(refs, sizes):
            weight_s[:, start : start + size] = ref[0]
            start += size
        for part in chunks(length):
            qkv_ref[0, part, :] = mm(u_ref[part, :], weight_s[...]).astype(BF16)

        @pl.when(pl.program_id(0) > 0)
        def _():
            ckv_ref[0] = mm(c_ref[...], weight_s[...]).astype(BF16)

    return pl.pallas_call(
        kernel,
        grid=(3,),
        in_specs=[whole_block((length, width)), whole_block((rows, width))]
        + [pl.BlockSpec((1, width, size), lambda s: (s, 0, 0)) for size in sizes],
        out_specs=[
            pl.BlockSpec((1, length, group), lambda s: (s, 0, 0)),
            pl.BlockSpec((1, rows, group), lambda s: (jnp.maximum(s - 1, 0), 0, 0)),
        ],
        out_shape=[
            jax.ShapeDtypeStruct((3, length, group), BF16),
            jax.ShapeDtypeStruct((2, rows, group), BF16),
        ],
        scratch_shapes=[pltpu.VMEM((width, group), BF16)],
        compiler_params=roomy(),
        cost_estimate=brief(20),
        name="project",
    )(u1, context, *weights)


def attention_out(where, layer_in, heads_own, heads_other, out_own, out_first, out_second, gain, bias, count):
    length, width = layer_in.shape[2:]
    group = heads_own.shape[1]
    half = group // 2
    step = 256

    def kernel(where_ref, x_ref, ho_ref, ht_ref, wo_ref, w1_ref, w2_ref, gain_ref, bias_ref, x1_ref, u_ref, ut_ref, tall):
        x1 = x_ref[0, 0].astype(F32) + mm(ho_ref[...], wo_ref[...])
        x1 += mm(ht_ref[:, :half], w1_ref[...]) + mm(ht_ref[:, half:], w2_ref[...])
        x1_ref[...] = x1
        hat, _ = normalize(x1)
        u = (hat * gain_ref[...] + bias_ref[...]).astype(BF16)
        u_ref[...] = u
        tall[...] = u.T
        place_rows(where_ref, tall, ut_ref, count)

    row = lambda i, w: (i, 0)
    return pl.pallas_call(
        kernel,
        grid_spec=pltpu.PrefetchScalarGridSpec(
            num_scalar_prefetch=1,
            grid=(length // step,),
            in_specs=[
                pl.BlockSpec((1, 1, step, width), lambda i, w: (w[0], 0, i, 0)),
                pl.BlockSpec((step, group), row),
                pl.BlockSpec((step, group), row),
                whole_block((group, width)),
                whole_block((half, width)),
                whole_block((half, width)),
                whole_block((1, width)),
                whole_block((1, width)),
            ],
            out_specs=[
                pl.BlockSpec((step, width), row),
                pl.BlockSpec((step, width), row),
                pl.BlockSpec((width, step), lambda i, w: (0, i)),
            ],
            scratch_shapes=[pltpu.VMEM((width, step), BF16)],
        ),
        out_shape=[
            jax.ShapeDtypeStruct((length, width), F32),
            jax.ShapeDtypeStruct((length, width), BF16),
            jax.ShapeDtypeStruct((width, length), BF16),
        ],
        compiler_params=roomy(),
        cost_estimate=brief(),
        name="attention_out",
    )(where, layer_in, heads_own, heads_other, out_own, out_first, out_second, gain, bias)


TALL = 256
STEP = 512


def chunks(length):
    return [slice(i, i + TALL) for i in range(0, length, TALL)]


def gelu_pair(pre):
    root = math.sqrt(2.0 / math.pi)
    straight = root * pre
    inner = straight * (1.0 + 0.044715 * (pre * pre))
    bend = jnp.tanh(inner)
    lean = 1.5 * inner - straight
    half = 0.5 * pre
    hid = half + half * bend
    slope = (0.5 + lean) + bend * (0.5 - lean * bend)
    return hid.astype(BF16), slope.astype(BF16)


def hidden_forward(u2, dy_rows, up, before):
    length, width = u2.shape
    half = width // 2
    gathered = up.ndim == 4
    steps = 2 * width // STEP
    first = 0 if before is None else steps

    def kernel(u_ref, dy_ref, up_ref, *refs):
        hid_ref, slope_ref, sent_ref, kept_ref = refs[-4:]
        weight = up_ref[...].reshape(width, STEP)
        for rows in chunks(length):
            hid, slope = gelu_pair(mm(u_ref[rows, :], weight))
            hid_ref[rows, :] = hid
            slope_ref[rows, :] = slope
        hid = hid_ref[...]
        for rows in chunks(half):
            sent_ref[rows, :] = mm(dy_ref[half + rows.start : half + rows.stop, :], hid).astype(BF16)
        for rows in chunks(half):
            kept_ref[rows, :] = mm(dy_ref[rows, :], hid).astype(BF16)

    if gathered:
        up_spec = pl.BlockSpec((up.shape[0], 1, up.shape[2], STEP), lambda j: (0, j // 2, 0, lax.rem(j, 2)))
    else:
        up_spec = pl.BlockSpec((width, STEP), lambda j: (0, j))
    tile = pl.BlockSpec((length, STEP), lambda j: (0, first + j))
    part = pl.BlockSpec((half, STEP), lambda j: (0, j))
    wide = jax.ShapeDtypeStruct((length, 2 * steps * STEP), BF16)
    return pl.pallas_call(
        kernel,
        grid=(steps,),
        in_specs=[whole_block((length, width)), whole_block((width, length)), up_spec]
        + ([] if before is None else [pl.BlockSpec(memory_space=pl.ANY)] * 2),
        out_specs=[tile, tile, part, part],
        out_shape=[wide, wide] + [jax.ShapeDtypeStruct((half, steps * STEP), BF16)] * 2,
        input_output_aliases={} if before is None else {3: 0, 4: 1},
        compiler_params=roomy(),
        cost_estimate=brief(),
        name="hidden_forward",
    )(u2, dy_rows, up, *(before or ()))


def hidden_backward(where, cotangent, hid, slope, down_own, buffer, u2_rows, x1):
    length, width = x1.shape
    half = width // 2
    pieces, _, rows_each, _ = buffer.shape
    side = 2 * width // STEP
    steps = 2 * side

    def kernel(
        where_ref, dy_ref, hid_ref, slope_ref, down_ref, down2_ref, ut_ref, x1_ref,
        layer_ref, dpre_ref, sent_ref, kept_ref,
        down_s, mix_s, x1_s, sem,
    ):
        j = pl.program_id(0)
        fetch = pltpu.make_async_copy(x1_ref, x1_s, sem)

        @pl.when(j == 0)
        def _():
            fetch.start()
            mix_s[...] = jnp.zeros_like(mix_s)

        @pl.when(j < side)
        def _():
            down_s[...] = down_ref[...]

        @pl.when(j >= side)
        def _():
            down_s[...] = down2_ref[...].reshape(STEP, width)

        for rows in chunks(length):
            dhid = mm_nt(dy_ref[0, 0, rows, :], down_s[...])
            dpre_ref[rows, :] = (dhid * slope_ref[rows, :].astype(F32)).astype(BF16)
        for rows in chunks(length):
            mix_s[rows, :] += mm(hid_ref[rows, :], down_s[...])
        dpre = dpre_ref[...]
        for rows in chunks(half):
            sent_ref[rows, :] = mm(ut_ref[half + rows.start : half + rows.stop, :], dpre).astype(BF16)
        for rows in chunks(half):
            kept_ref[rows, :] = mm(ut_ref[rows, :], dpre).astype(BF16)

        @pl.when(j == steps - 1)
        def _():
            fetch.wait()
            for rows in chunks(length):
                layer_ref[rows, :] = (x1_s[rows, :] + mix_s[rows, :]).astype(BF16)

    low = lambda j: jnp.minimum(j, side - 1)
    high = lambda j: jnp.maximum(j - side, 0)
    tile = pl.BlockSpec((length, STEP), lambda j, w: (0, j))
    part = pl.BlockSpec((half, STEP), lambda j, w: (0, j))
    return pl.pallas_call(
        kernel,
        grid_spec=pltpu.PrefetchScalarGridSpec(
            num_scalar_prefetch=1,
            grid=(steps,),
            in_specs=[
                pl.BlockSpec((1, 1, length, width), lambda j, w: (w[0], 0, 0, 0), pipeline_mode=pl.Buffered(1)),
                tile,
                tile,
                pl.BlockSpec((STEP, width), lambda j, w: (low(j), 0)),
                pl.BlockSpec((pieces // side, 2, rows_each, width), lambda j, w: (high(j), 1, 0, 0)),
                whole_block((width, length)),
                pl.BlockSpec(memory_space=pl.ANY),
            ],
            out_specs=[whole_block((length, width)), tile, part, part],
            scratch_shapes=[
                pltpu.VMEM((STEP, width), BF16),
                pltpu.VMEM((length, width), F32),
                pltpu.VMEM((length, width), F32),
                pltpu.SemaphoreType.DMA,
            ],
        ),
        out_shape=[
            jax.ShapeDtypeStruct((length, width), BF16),
            jax.ShapeDtypeStruct((length, steps * STEP), BF16),
            jax.ShapeDtypeStruct((half, steps * STEP), BF16),
            jax.ShapeDtypeStruct((half, steps * STEP), BF16),
        ],
        compiler_params=roomy(),
        cost_estimate=brief(),
        name="hidden_backward",
    )(where, cotangent, hid, slope, down_own, buffer, u2_rows, x1)


def second_norm_backward(where, cotangent, dpre, up_own, buffer, x1, gain, out_own, out_first, out_second, count):
    length, width = x1.shape
    group = out_own.shape[0]
    pieces, _, rows_each, _ = buffer.shape
    side = 2
    tiles = 2 * side
    steps = tiles + 2
    chunk = 128

    def kernel(
        where_ref, dpre_ref, up_ref, up2_ref, dy_ref, x1_ref, gain_ref, wo_ref, w1_ref, w2_ref,
        dattn_ref, turned_ref, dheads_ref, sums_ref,
        up_s, out_s, grad_s, tall, dy_s, x1_s, sems,
    ):
        j = pl.program_id(0)
        fetches = [
            pltpu.make_async_copy(x1_ref, x1_s, sems.at[0]),
            pltpu.make_async_copy(dy_ref.at[where_ref[0], 0], dy_s, sems.at[1]),
        ]

        @pl.when(j == 0)
        def _():
            for fetch in fetches:
                fetch.start()
            grad_s[...] = jnp.zeros_like(grad_s)
            sums_ref[...] = jnp.zeros_like(sums_ref)

        @pl.when(j < side)
        def _():
            up_s[...] = up_ref[...]

        @pl.when(jnp.logical_and(j >= side, j < tiles))
        def _():
            up_s[...] = up2_ref[...].reshape(width, width)

        @pl.when(j < tiles)
        def _():
            for rows in chunks(length):
                grad_s[rows, :] += mm_nt(dpre_ref[rows, :], up_s[...])

        @pl.when(j == tiles - 1)
        def _():
            for fetch in fetches:
                fetch.wait()

            @pl.loop(0, length // chunk)
            def _(i):
                rows = pl.ds(pl.multiple_of(i * chunk, chunk), chunk)
                du = grad_s[rows, :]
                hat, rstd = normalize(x1_s[rows, :])
                sums_ref[0:1, :] += jnp.sum(du * hat, axis=0, keepdims=True)
                sums_ref[1:2, :] += jnp.sum(du, axis=0, keepdims=True)
                out = dy_s[rows, :].astype(F32) + normalize_backward(du, hat, rstd, gain_ref[...])
                out = out.astype(BF16)
                dattn_ref[rows, :] = out
                tall[:, rows] = out.T

            place_rows(where_ref, tall, turned_ref, count)

        @pl.when(j == tiles)
        def _():
            out_s[...] = wo_ref[...]

        @pl.when(j == tiles + 1)
        def _():
            out_s[: group // 2, :] = w1_ref[...]
            out_s[group // 2 :, :] = w2_ref[...]

        @pl.when(j >= tiles)
        def _():
            for rows in chunks(length):
                dheads_ref[0, rows, :] = mm_nt(dattn_ref[rows, :], out_s[...]).astype(BF16)

    low = lambda j: jnp.minimum(j, side - 1)
    high = lambda j: jnp.clip(j - side, 0, side - 1)
    return pl.pallas_call(
        kernel,
        grid_spec=pltpu.PrefetchScalarGridSpec(
            num_scalar_prefetch=1,
            grid=(steps,),
            in_specs=[
                pl.BlockSpec((length, width), lambda j, w: (0, jnp.minimum(j, tiles - 1))),
                pl.BlockSpec((width, width), lambda j, w: (0, low(j))),
                pl.BlockSpec((pieces, 1, rows_each, width), lambda j, w: (0, high(j), 0, 0)),
                pl.BlockSpec(memory_space=pl.ANY),
                pl.BlockSpec(memory_space=pl.ANY),
                whole_block((1, width)),
                whole_block((group, width)),
                whole_block((group // 2, width)),
                whole_block((group // 2, width)),
            ],
            out_specs=[
                whole_block((length, width)),
                whole_block((width, length)),
                pl.BlockSpec((1, length, group), lambda j, w: (jnp.maximum(j - tiles, 0), 0, 0)),
                whole_block((2, width)),
            ],
            scratch_shapes=[
                pltpu.VMEM((width, width), BF16),
                pltpu.VMEM((group, width), BF16),
                pltpu.VMEM((length, width), F32),
                pltpu.VMEM((width, length), BF16),
                pltpu.VMEM((length, width), BF16),
                pltpu.VMEM((length, width), F32),
                pltpu.SemaphoreType.DMA((2,)),
            ],
        ),
        out_shape=[
            jax.ShapeDtypeStruct((length, width), BF16),
            jax.ShapeDtypeStruct((width, length), BF16),
            jax.ShapeDtypeStruct((2, length, group), BF16),
            jax.ShapeDtypeStruct((2, width), F32),
        ],
        compiler_params=roomy(),
        cost_estimate=brief(),
        name="second_norm_backward",
    )(where, dpre, up_own, buffer, cotangent, x1, gain, out_own, out_first, out_second)


def projection_rows(u1_rows, context_turned, dqkv, dckv, dattn_rows, heads):
    width, length = u1_rows.shape
    half = width // 2
    group = heads.shape[1]

    def kernel(ut_ref, cut_ref, grad_ref, cgrad_ref, dt_ref, heads_ref, sent_ref, kept_ref):
        s = pl.program_id(0)

        @pl.when(s < 3)
        def _():
            grad = grad_ref[0]
            cgrad = jnp.where(s > 0, cgrad_ref[0], jnp.zeros_like(cgrad_ref[0]))
            for ref, start in ((sent_ref, half), (kept_ref, 0)):
                for rows in chunks(half):
                    here = slice(start + rows.start, start + rows.stop)
                    ref[rows, :] = (mm(ut_ref[here, :], grad) + mm(cut_ref[here, :], cgrad)).astype(BF16)

        @pl.when(s == 3)
        def _():
            heads = heads_ref[...]
            for ref, start in ((sent_ref, half), (kept_ref, 0)):
                for rows in chunks(half):
                    here = slice(start + rows.start, start + rows.stop)
                    ref[rows, :] = mm(dt_ref[here, :], heads).astype(BF16)

    part = pl.BlockSpec((half, group), lambda s: (0, s))
    return pl.pallas_call(
        kernel,
        grid=(4,),
        in_specs=[
            whole_block((width, length)),
            whole_block((width, CTX)),
            pl.BlockSpec((1, length, group), lambda s: (jnp.minimum(s, 2), 0, 0)),
            pl.BlockSpec((1, CTX, group), lambda s: (jnp.clip(s - 1, 0, 1), 0, 0)),
            whole_block((width, length)),
            whole_block((length, group)),
        ],
        out_specs=[part, part],
        out_shape=[jax.ShapeDtypeStruct((half, 4 * group), BF16)] * 2,
        compiler_params=roomy(),
        cost_estimate=brief(),
        name="projection_rows",
    )(u1_rows, context_turned, dqkv, dckv, dattn_rows, heads)


def inputs_backward(where, dsides, qkv_own, qkv_first, qkv_second, u1, coef, skip, state, layer_in, dattn, gain):
    length, width = layer_in.shape[2:]
    group = qkv_own.shape[2]
    steps = 6
    chunk = 128
    before = BLK // CH - 1

    def kernel(
        where_ref, do_ref, dt_ref, co_ref, ct_ref, own_ref, w1_ref, w2_ref, v_ref, rates_ref,
        norms_ref, coef_ref, skip_ref, state_ref, x_ref, dx_ref, gain_ref,
        out_ref, sums_ref, small_ref,
        grad_s, cgrad_s, weight_s, total, ctotal, within,
    ):
        j = pl.program_id(0)

        @pl.when(j == 0)
        def _():
            total[...] = jnp.zeros_like(total)
            ctotal[...] = jnp.zeros_like(ctotal)
            sums_ref[...] = jnp.zeros_like(sums_ref)
            for n in range(NS):
                within[n] = decay_within(n, True)

        @pl.when(j < 3)
        def _():
            grad_s[...] = do_ref[0]
            cgrad_s[...] = co_ref[0]
            weight_s[...] = own_ref[0]

        @pl.when(j >= 3)
        def _():
            grad_s[...] = dt_ref[0]
            cgrad_s[...] = ct_ref[0]
            weight_s[:, : group // 2] = w1_ref[0]
            weight_s[:, group // 2 :] = w2_ref[0]

        @pl.when(lax.rem(j, 3) == 0)
        def _():
            cgrad_s[...] = jnp.zeros_like(cgrad_s)

        for rows in chunks(length):
            total[rows, :] += mm_nt(grad_s[rows, :], weight_s[...])
        ctotal[...] += mm_nt(cgrad_s[...], weight_s[...])

        @pl.when(j == steps - 1)
        def _():
            carry_in, carry_out, whole = decay_vectors(rates_ref[...], norms_ref[...])

            @pl.loop(0, width // 256)
            def _(c):
                here = pl.ds(pl.multiple_of(c * 256, 256), 256)
                rows = v_ref[:, here].astype(F32)
                grad = ctotal[:, here].astype(BF16)
                wide = grad.astype(F32)
                du = skip_ref[:, here] * wide
                reach = jnp.dot(carry_in, wide, precision=HIGHEST, preferred_element_type=F32)
                for n in range(NS):
                    back = mm(within[n], grad)
                    du += coef_ref[n : n + 1, here] * back
                    small_ref[n : n + 1, here] = (
                        jnp.sum(rows * back, axis=0, keepdims=True) + state_ref[n : n + 1, here] * reach[n : n + 1, :]
                    )
                small_ref[NS : NS + 1, here] = jnp.sum(rows * wide, axis=0, keepdims=True)
                total[before * CH : (before + 1) * CH, here] += du
                carried = coef_ref[:, here] * reach
                for k in reversed(range(before)):
                    total[k * CH : (k + 1) * CH, here] += lax.dot_general(
                        carry_out.astype(F32),
                        carried,
                        (((0,), (0,)), ((), ())),
                        precision=HIGHEST,
                        preferred_element_type=F32,
                    )
                    carried = whole * carried

            @pl.loop(0, length // chunk)
            def _(i):
                rows = pl.ds(pl.multiple_of(i * chunk, chunk), chunk)
                du = total[rows, :]
                hat, rstd = normalize(x_ref[0, 0, rows, :].astype(F32))
                sums_ref[0:1, :] += jnp.sum(du * hat, axis=0, keepdims=True)
                sums_ref[1:2, :] += jnp.sum(du, axis=0, keepdims=True)
                out = dx_ref[rows, :].astype(F32) + normalize_backward(du, hat, rstd, gain_ref[...])
                out_ref[rows, :] = out.astype(BF16)

    low = lambda j: jnp.minimum(j, 2)
    high = lambda j: jnp.maximum(j - 3, 0)
    back = lambda s: jnp.maximum(s - 1, 0)
    mine = pl.BlockSpec((1, 1, length, width), lambda j, w: (w[0], 0, 0, 0), pipeline_mode=pl.Buffered(1))
    (dqkv_own, dckv_own), (dqkv_other, dckv_other) = dsides
    return pl.pallas_call(
        kernel,
        grid_spec=pltpu.PrefetchScalarGridSpec(
            num_scalar_prefetch=1,
            grid=(steps,),
            in_specs=[
                pl.BlockSpec((1, length, group), lambda j, w: (low(j), 0, 0)),
                pl.BlockSpec((1, length, group), lambda j, w: (high(j), 0, 0)),
                pl.BlockSpec((1, CTX, group), lambda j, w: (back(low(j)), 0, 0)),
                pl.BlockSpec((1, CTX, group), lambda j, w: (back(high(j)), 0, 0)),
                pl.BlockSpec((1, width, group), lambda j, w: (low(j), 0, 0)),
                pl.BlockSpec((1, width, group // 2), lambda j, w: (high(j), 0, 0)),
                pl.BlockSpec((1, width, group // 2), lambda j, w: (high(j), 0, 0)),
                pl.BlockSpec((CH, width), lambda j, w: (before, 0)),
                whole_block((NS, 1)),
                whole_block((NS, 1)),
                whole_block((NS, width)),
                whole_block((1, width)),
                whole_block((NS, width)),
                mine,
                whole_block((length, width)),
                whole_block((1, width)),
            ],
            out_specs=[
                whole_block((length, width)),
                whole_block((2, width)),
                whole_block((NS + 1, width)),
            ],
            scratch_shapes=[
                pltpu.VMEM((length, group), BF16),
                pltpu.VMEM((CTX, group), BF16),
                pltpu.VMEM((width, group), BF16),
                pltpu.VMEM((length, width), F32),
                pltpu.VMEM((CTX, width), F32),
                pltpu.VMEM((NS, CH, CH), BF16),
            ],
        ),
        out_shape=[
            jax.ShapeDtypeStruct((length, width), BF16),
            jax.ShapeDtypeStruct((2, width), F32),
            jax.ShapeDtypeStruct((NS + 1, width), F32),
        ],
        compiler_params=roomy(),
        cost_estimate=brief(),
        name="inputs_backward",
    )(
        where, dqkv_own, dqkv_other, dckv_own, dckv_other, qkv_own, qkv_first, qkv_second,
        u1, *decay_arrays(), coef, skip, state, layer_in, dattn, gain,
    )


def join(where, kept, got, group, above, below, bit):
    rows, columns = kept.shape
    width = group or 2 * STEP
    shape = (above, 2, below, columns)

    def kernel(where_ref, kept_ref, got_ref, keep_ref, send_ref):
        mine = (where_ref[1] >> bit) & 1
        for out_ref, index in ((keep_ref, mine), (send_ref, 1 - mine)):
            come = got_ref[:, pl.ds(index, 1)][:, 0].astype(F32)
            if group:
                come = jnp.concatenate([come[..., group // 2 :], come[..., : group // 2]], axis=-1)
            out_ref[...] = (kept_ref[:, pl.ds(index, 1)][:, 0].astype(F32) + come).astype(BF16)

    tile = pl.BlockSpec((above, 2, below, width), lambda j, w: (0, 0, 0, j))
    out = pl.BlockSpec((above, below, width), lambda j, w: (0, 0, j))
    keep, send = pl.pallas_call(
        kernel,
        grid_spec=pltpu.PrefetchScalarGridSpec(
            num_scalar_prefetch=1, grid=(columns // width,), in_specs=[tile, tile], out_specs=[out, out]
        ),
        out_shape=[jax.ShapeDtypeStruct((above, below, columns), BF16)] * 2,
        compiler_params=roomy(),
        cost_estimate=brief(),
        name="join",
    )(where, kept.reshape(shape), got.reshape(shape))
    return keep.reshape(rows // 2, columns), send.reshape(rows // 2, columns)


def add_pairs(where, *pairs):
    rows, columns = pairs[0][0].shape
    width = min(columns, 4 * STEP)
    tiles = columns // width

    def kernel(where_ref, *refs):
        out_ref = refs[-1]
        for k in range(len(pairs)):

            @pl.when(pl.program_id(0) // tiles == k)
            def _(left=refs[2 * k], right=refs[2 * k + 1]):
                out_ref[...] = (left[...].astype(F32) + right[...].astype(F32)).astype(BF16)

    def spec(k):
        return pl.BlockSpec((rows, width), lambda j, w: (0, jnp.clip(j - k * tiles, 0, tiles - 1)))

    return pl.pallas_call(
        kernel,
        grid_spec=pltpu.PrefetchScalarGridSpec(
            num_scalar_prefetch=1,
            grid=(len(pairs) * tiles,),
            in_specs=[spec(k) for k in range(len(pairs)) for _ in range(2)],
            out_specs=pl.BlockSpec((rows, width), lambda j, w: (0, j)),
        ),
        out_shape=jax.ShapeDtypeStruct((rows, len(pairs) * columns), BF16),
        cost_estimate=brief(37),
        name="add_pairs",
    )(where, *[value for pair in pairs for value in pair])


def both_parts(where, own, pieces, kind):
    length, width = own.shape
    step = min(piece.shape[0] for piece in pieces)
    counts = [piece.shape[0] // step for piece in pieces]
    starts = [sum(counts[:k]) for k in range(len(counts))]

    def kernel(where_ref, own_ref, *refs):
        out_ref = refs[-1]
        m, i = pl.program_id(0), pl.program_id(1)
        here = m == where_ref[0]

        @pl.when(here)
        def _():
            out_ref[0, 0] = own_ref[...].astype(kind)

        for ref, start, count in zip(refs, starts, counts):

            @pl.when(jnp.logical_not(here) & (i >= start) & (i < start + count))
            def _(ref=ref):
                out_ref[0, 0] = ref[...].astype(kind)

    def spec(start, count):
        return pl.BlockSpec((step, width), lambda m, i, w: (jnp.clip(i - start, 0, count - 1), 0))

    return pl.pallas_call(
        kernel,
        grid_spec=pltpu.PrefetchScalarGridSpec(
            num_scalar_prefetch=1,
            grid=(2, length // step),
            in_specs=[pl.BlockSpec((step, width), lambda m, i, w: (i, 0))]
            + [spec(start, count) for start, count in zip(starts, counts)],
            out_specs=pl.BlockSpec((1, 1, step, width), lambda m, i, w: (m, 0, i, 0)),
        ),
        out_shape=jax.ShapeDtypeStruct((2, 1, length, width), kind),
        cost_estimate=brief(37),
        name="both_parts",
    )(where, own, *pieces)


def swap_halves(values, width):
    half = width // 2
    order = [start + half * k for start in range(0, values.shape[1], width) for k in (1, 0)]
    return jnp.concatenate([values[:, i : i + half] for i in order], axis=1)


def shards(
    dp_count,
    layer_in,
    ln1_gain,
    ln1_bias,
    qkv_weight,
    out_weight,
    ssm_coef,
    ssm_skip,
    ln2_gain,
    ln2_bias,
    up_weight,
    down_weight,
    cotangent,
):
    width = layer_in.shape[3]
    group = qkv_weight.shape[2]
    mine = lax.axis_index("tensor")
    place = lax.axis_index("dp")
    where = jnp.stack([mine, place]).astype(jnp.int32)
    rows_each = width // dp_count
    gain1, bias1, gain2, bias2 = ln1_gain[None], ln1_bias[None], ln2_gain[None], ln2_bias[None]

    over_x = lambda v: swap(v, "tensor", 1, 2)
    over = lambda v, bit: swap(v, "dp", 1 << bit, dp_count)
    core = place & 1

    def scatter(values, depth):
        groups = [[(k << depth) | low for k in range(dp_count >> depth)] for low in range(1 << depth)]
        return lax.psum_scatter(values, "dp", scatter_dimension=0, axis_index_groups=groups, tiled=True)

    bits = dp_count.bit_length() - 1

    class Halvings:
        def __init__(self, keep, send, bit):
            self.left = [b for b in reversed(range(1, bits)) if b != bit]
            self.total, self.got = keep, over(send, bit)

        def step(self, bit, *deps):
            if bit not in self.left:
                return self.got
            total = (self.total.astype(F32) + tie(self.got, *deps)).astype(BF16)
            axis = self.left.index(bit)
            rows, columns = total.shape
            spread = total.reshape((1 << axis, 2, rows // (2 << axis), columns))
            mybit = (place >> bit) & 1
            pick = lambda index: lax.dynamic_index_in_dim(spread, index, 1, keepdims=False).reshape(-1, columns)
            self.left.remove(bit)
            self.total, send = pick(mybit), pick(1 - mybit)
            self.got = over(send, bit)
            return send

        def last(self, *deps):
            while self.left:
                self.step(self.left[-1])
            return self.total.astype(F32) + tie(self.got, *deps)

    def part_of(weight, axis, index, count):
        size = weight.shape[axis] // count
        return lax.dynamic_slice_in_dim(weight, index * size, size, axis)

    up_mine = part_of(up_weight, 0, place, dp_count)
    feed = jnp.concatenate([up_mine[:, :width], up_mine[:, width:], part_of(down_weight, 0, place, dp_count)], axis=0)
    feed = over_x(feed)
    qkv_first = over_x(part_of(qkv_weight, 2, core, 2))
    small = over_x(jnp.concatenate([ssm_coef, ssm_skip[None]], axis=0))
    out_first = over_x(part_of(out_weight, 0, core, 2))

    def in_order(own, other, axis):
        return jnp.where(
            mine == 0, jnp.concatenate([own, other], axis=axis), jnp.concatenate([other, own], axis=axis)
        )

    coef = in_order(ssm_coef, small[:NS], 1)
    skip = in_order(ssm_skip[None], small[NS:], 1)

    dy_rows = turn_rows(where, cotangent, dp_count)
    feed = tie(feed, dy_rows, small)
    buffer = lax.all_gather(feed, "dp", axis=0, tiled=True).reshape(dp_count, 4, rows_each, width)
    u1, u1_rows = first_norm(tie(where, feed), layer_in, gain1, bias1, dp_count)
    context, state = ssm_forward(u1, coef, skip)
    context_turned = context_rows(tie(where, context), context, dp_count)
    qkv_own, ckv_own = project(u1, tie(context, context_turned), (qkv_weight,))
    heads_own, lse_own = attend_forward(qkv_own, ckv_own)
    qkv_first = tie(qkv_first, heads_own)
    qkv_second = over(qkv_first, 0)
    qkv_other, ckv_other = project(tie(u1, heads_own), context, (qkv_first, qkv_second))
    out_first = tie(out_first, qkv_other)
    out_second = over(out_first, 0)
    heads_other, lse_other = attend_forward(qkv_other, tie(ckv_other, out_first))
    out_second = tie(out_second, heads_other)
    x1, u2, u2_rows = attention_out(
        where, layer_in, heads_own, heads_other, out_weight, out_first, out_second, gain2, bias2, dp_count
    )
    hid, slope, sent, kept_own = hidden_forward(u2, dy_rows, up_weight, None)
    got_own = over(sent, 0)
    hid, slope, sent, kept_other = hidden_forward(u2, dy_rows, buffer, (hid, slope))
    got_other = over(sent, 0)

    split_y = (dp_count // 4, rows_each, 1)
    down_keep_own, down_send_own = join(tie(where, sent), kept_own, got_own, 0, *split_y)
    down_got_own = over(down_send_own, 1)
    down_keep_other, down_send_other = join(tie(where, down_send_own), kept_other, got_other, 0, *split_y)
    down_got_other = over(down_send_other, 1)
    layer_out, dpre, up_sent, up_kept = hidden_backward(
        tie(where, down_send_other), cotangent, hid, slope, down_weight, buffer, u2_rows, x1
    )
    up_got = over(up_sent, 0)
    layer_come = over_x(layer_out)
    down_sum = add_pairs(
        tie(where, layer_out), (down_keep_own, down_got_own), (down_keep_other, down_got_other)
    )
    up_keep, up_send = join(tie(where, down_sum), up_kept, up_got, 0, *split_y)
    down_sum = scatter(down_sum, 2)
    up_got = over(up_send, 1)
    dattn, dattn_rows, dheads, sums2 = second_norm_backward(
        tie(where, up_send),
        cotangent,
        dpre,
        up_weight,
        buffer,
        x1,
        gain2,
        out_weight,
        out_first,
        out_second,
        dp_count,
    )
    dqkv_other, dckv_other = attend_backward(qkv_other, ckv_other, dheads, 1, lse_other)
    other_sent, other_kept = projection_rows(
        u1_rows, context_turned, dqkv_other, dckv_other, dattn_rows, heads_other
    )
    other_got = over(other_sent, 0)
    layer_come = tie(layer_come, other_sent)
    up_sum = add_pairs(tie(where, other_sent), (up_keep, up_got))
    dqkv_own, dckv_own = attend_backward(qkv_own, ckv_own, tie(dheads, up_sum, layer_come), 0, lse_own)
    up_sum = scatter(up_sum, 2)
    other_keep, other_send = join(
        tie(where, dqkv_own), other_kept, tie(other_got, dqkv_own), group, *split_y
    )
    other_got = over(other_send, 1)
    own_sent, own_kept = projection_rows(
        tie(u1_rows, other_send), context_turned, dqkv_own, dckv_own, dattn_rows, heads_own
    )
    own_got = over(own_sent, 0)
    down_sum = tie(down_sum, own_sent)
    grad_in, sums1, small_ssm = inputs_backward(
        tie(where, own_sent, down_sum),
        ((dqkv_own, dckv_own), (dqkv_other, dckv_other)),
        qkv_weight,
        qkv_first,
        qkv_second,
        u1,
        coef,
        skip,
        state,
        layer_in,
        dattn,
        gain1,
    )

    small_all = jnp.concatenate([small_ssm, sums2, sums1], axis=0)
    grad_first = over_x(grad_in[: grad_in.shape[0] // 2])
    up_sum = tie(up_sum, grad_in)
    other_sum = add_pairs(tie(where, grad_in, own_got, up_sum), (other_keep, other_got))
    own_keep, own_send = join(tie(where, other_sum), own_kept, own_got, 0, *split_y)
    own_rows = Halvings(own_keep, own_send, 1)
    other_sum = scatter(other_sum, 2)
    layer_pair = both_parts(tie(where, own_send), layer_out, (layer_come,), BF16)

    def meet(chains, *others):
        done = lax.optimization_barrier((*(c.got for c in chains), *others))
        for chain, got in zip(chains, done):
            chain.got = got
        return done[len(chains) :]

    small_got = over_x(small_all)
    small_got, grad_first = meet((own_rows,), small_got, grad_first, layer_pair)[:2]
    own_rows.step(2)
    small_all = small_all + small_got
    grad_second = over_x(tie(grad_in[grad_in.shape[0] // 2 :], grad_first))
    small_got = over(small_all, 0)
    cross = lambda values: over_x(values[:, values.shape[1] // 2 :]).astype(F32)
    down_come, up_come = cross(down_sum), cross(up_sum)
    small_got, other_sum, down_come, up_come = meet((own_rows,), small_got, other_sum, down_come, up_come)
    other_come = over_x(other_sum).astype(F32)
    own_rows.step(3)
    small_all = small_all + small_got
    small_got = over(small_all, 1)
    small_got, grad_second = meet((own_rows,), small_got, grad_second)
    small_all = small_all + small_got
    for bit in range(2, bits):
        small_all = small_all + over(small_all, bit)
    own_total = own_rows.last()
    here = lax.dynamic_slice_in_dim(small_all[: NS + 1], mine * group, group, 1)
    grad_pair = both_parts(where, grad_in, (grad_first, grad_second), F32)

    def ordered(values):
        return jnp.where(core == 1, swap_halves(values, group), values)

    hidden = up_weight.shape[1]
    grad_down = down_sum[:, :hidden].astype(F32) + down_come
    grad_up = up_sum[:, :hidden].astype(F32) + up_come
    grad_qkv_out = own_total + ordered(other_come)
    grad_qkv, grad_out = grad_qkv_out[:, : 3 * group], grad_qkv_out[:, 3 * group :]

    return (
        layer_pair,
        grad_pair,
        small_all[NS + 3],
        small_all[NS + 4],
        grad_qkv.reshape(rows_each, 3, group).swapaxes(0, 1),
        grad_out.T,
        here[:NS],
        here[NS],
        small_all[NS + 1],
        small_all[NS + 2],
        grad_up,
        grad_down.T,
    )


def solution(mesh):
    in_specs = (
        P(None, "dp", None, None),
        P(),
        P(),
        P(None, None, "tensor"),
        P("tensor", None),
        P(None, "tensor"),
        P("tensor"),
        P(),
        P(),
        P(None, "tensor"),
        P("tensor", None),
        P(None, "dp", None, None),
    )
    out_specs = (
        P(None, "dp", None, None),
        P(None, "dp", None, None),
        P(),
        P(),
        P(None, "dp", "tensor"),
        P("tensor", "dp"),
        P(None, "tensor"),
        P("tensor"),
        P(),
        P(),
        P("dp", "tensor"),
        P("tensor", "dp"),
    )
    body = functools.partial(shards, mesh.shape["dp"])
    return jax.shard_map(body, mesh=mesh, in_specs=in_specs, out_specs=out_specs, check_vma=False)
```

```python
import functools
import math

import jax
import jax.numpy as jnp
from jax import lax
from jax.experimental import pallas as pl
from jax.experimental.pallas import tpu as pltpu
from jax.sharding import PartitionSpec as P
import numpy as np

HD = 128
NS = 16
BLK = 512
CTX = 128
CH = 128
TILE = 256
EPS = 1e-05
F32 = jnp.float32
BF16 = jnp.bfloat16
HIGHEST = lax.Precision.HIGHEST
SCALE = HD**-0.5
LOG2 = SCALE * math.log2(math.e)


def swap(value, axis, mask, count):
    return lax.ppermute(value, axis, [(i, i ^ mask) for i in range(count)])


def tie(value, *deps):
    return lax.optimization_barrier((value, *deps))[0] if deps else value


def mm(left, right):
    return lax.dot_general(left, right, (((1,), (0,)), ((), ())), preferred_element_type=F32)


def mm_nt(left, right):
    return lax.dot_general(left, right, (((1,), (1,)), ((), ())), preferred_element_type=F32)


def mm_tn(left, right):
    return lax.dot_general(left, right, (((0,), (0,)), ((), ())), preferred_element_type=F32)


def decay_constants():
    rates = 4.0 / CH * np.exp2(-8.0 * np.arange(NS, dtype=np.float64) / (NS - 1))
    return rates, np.sqrt(-np.expm1(-2.0 * rates))


RATES, NORMS = decay_constants()


def decay_within(n, transposed):
    rows = lax.broadcasted_iota(jnp.int32, (CH, CH), 0)
    columns = lax.broadcasted_iota(jnp.int32, (CH, CH), 1)
    offset = columns - rows if transposed else rows - columns
    powers = jnp.exp(offset.astype(F32) * -float(RATES[n]))
    return jnp.where(offset >= 0, float(NORMS[n]) * powers, 0.0).astype(BF16)


def decay_vectors(rates, norms):
    steps = lax.broadcasted_iota(jnp.int32, (NS, CH), 1).astype(F32)
    carry_in = jnp.exp(-rates * (steps + 1.0))
    carry_out = (norms * jnp.exp(-rates * (CH - 1.0 - steps))).astype(BF16)
    return carry_in, carry_out, jnp.exp(-rates * CH)


def ssm_forward_kernel(v_ref, rates_ref, norms_ref, coef_ref, skip_ref, out_ref, state_ref, within_ref):
    @pl.when(pl.program_id(0) == 0)
    def _():
        for n in range(NS):
            within_ref[n] = decay_within(n, False)

    carry_in, carry_out, whole = decay_vectors(rates_ref[...], norms_ref[...])
    before = BLK // CH - 1
    state = jnp.zeros(state_ref.shape, F32)
    for k in range(before):
        state = whole * state + mm(carry_out, v_ref[k * CH : (k + 1) * CH, :])
    state_ref[...] = state
    rows = v_ref[before * CH :, :]
    total = skip_ref[...] * rows.astype(F32)
    total += lax.dot_general(
        carry_in, coef_ref[...] * state, (((0,), (0,)), ((), ())), precision=HIGHEST, preferred_element_type=F32
    )
    for n in range(NS):
        total += coef_ref[n : n + 1, :] * mm(within_ref[n], rows)
    out_ref[...] = total.astype(BF16)


def decay_arrays():
    return jnp.asarray(RATES[:, None], F32), jnp.asarray(NORMS[:, None], F32)


def ssm_forward(rows, coef, skip):
    width = rows.shape[1]
    step = 256
    column = lambda c: (0, c)
    fixed = pl.BlockSpec((NS, 1), lambda c: (0, 0))
    return pl.pallas_call(
        ssm_forward_kernel,
        grid=(width // step,),
        in_specs=[
            pl.BlockSpec((BLK, step), column),
            fixed,
            fixed,
            pl.BlockSpec((NS, step), column),
            pl.BlockSpec((1, step), column),
        ],
        out_specs=[pl.BlockSpec((CH, step), column), pl.BlockSpec((NS, step), column)],
        out_shape=[jax.ShapeDtypeStruct((CH, width), BF16), jax.ShapeDtypeStruct((NS, width), F32)],
        scratch_shapes=[pltpu.VMEM((NS, CH, CH), BF16)],
        cost_estimate=brief(31),
        name="ssm_forward",
    )(rows, *decay_arrays(), coef, skip)


def key_parts(block, tile, k_ref, v_ref, ck_ref, cv_ref):
    parts = []
    if block > 0:
        parts.append((None, ck_ref[0], cv_ref[0], False))
    for piece in range(tile + 1):
        where = slice(block * BLK + piece * TILE, block * BLK + (piece + 1) * TILE)
        parts.append((piece, k_ref[0, where, :], v_ref[0, where, :], piece == tile))
    return parts


def tile_scores(keys, query, masked):
    scores = mm_nt(keys, query)
    if masked:
        key_ids = lax.broadcasted_iota(jnp.int32, scores.shape, 0)
        query_ids = lax.broadcasted_iota(jnp.int32, scores.shape, 1)
        scores = jnp.where(key_ids <= query_ids, scores, -1e30)
    return scores


def attend_forward_kernel(q_ref, k_ref, v_ref, ck_ref, cv_ref, out_ref, lse_ref):
    for block in range(2):
        for tile in range(BLK // TILE):
            base = block * BLK + tile * TILE
            query = q_ref[0, base : base + TILE, :]
            parts = key_parts(block, tile, k_ref, v_ref, ck_ref, cv_ref)
            scores = [tile_scores(keys, query, masked) for _, keys, _, masked in parts]
            top = functools.reduce(jnp.maximum, [jnp.max(s, axis=0, keepdims=True) for s in scores]) * LOG2
            exps = [jnp.exp2(s * LOG2 - top) for s in scores]
            total = functools.reduce(jnp.add, [jnp.sum(e, axis=0, keepdims=True) for e in exps])
            inverse = 1.0 / total
            out = functools.reduce(
                jnp.add,
                [mm_tn(values, (e * inverse).astype(BF16)) for (_, _, values, _), e in zip(parts, exps)],
            )
            out_ref[base : base + TILE, :] = out.T.astype(BF16)
            lse_ref[0, :, base : base + TILE] = top + jnp.log2(total)


def attend_forward(qkv, ckv):
    length, width = qkv.shape[1], qkv.shape[2]
    heads = width // HD
    pick = lambda s: pl.BlockSpec((1, length, HD), lambda h: (s, 0, h))
    pick_context = lambda s: pl.BlockSpec((1, CTX, HD), lambda h: (s, 0, h))
    return pl.pallas_call(
        attend_forward_kernel,
        grid=(heads,),
        in_specs=[pick(0), pick(1), pick(2), pick_context(0), pick_context(1)],
        out_specs=[
            pl.BlockSpec((length, HD), lambda h: (0, h)),
            pl.BlockSpec((1, 1, length), lambda h: (h, 0, 0)),
        ],
        out_shape=[
            jax.ShapeDtypeStruct((length, width), BF16),
            jax.ShapeDtypeStruct((heads, 1, length), F32),
        ],
        cost_estimate=brief(31),
        name="attend_forward",
    )(qkv, qkv, qkv, ckv, ckv)


def attend_backward_kernel(q_ref, k_ref, v_ref, ck_ref, cv_ref, dout_ref, lse_ref, grad_ref, cgrad_ref):
    for block in range(2):
        grads = {}
        for tile in range(BLK // TILE):
            base = block * BLK + tile * TILE
            query = q_ref[0, base : base + TILE, :]
            dout = dout_ref[0, base : base + TILE, :]
            lse = lse_ref[0, :, base : base + TILE]
            parts = key_parts(block, tile, k_ref, v_ref, ck_ref, cv_ref)
            probs = [jnp.exp2(tile_scores(keys, query, masked) * LOG2 - lse) for _, keys, _, masked in parts]
            dprobs = [mm_nt(values, dout) for _, _, values, _ in parts]
            inner = functools.reduce(
                jnp.add, [jnp.sum(p * d, axis=0, keepdims=True) for p, d in zip(probs, dprobs)]
            )
            dquery = None
            for (name, keys, _, _), p, d in zip(parts, probs, dprobs):
                dscore = (p * (d - inner)).astype(BF16)
                term = mm_tn(keys, dscore)
                dquery = term if dquery is None else dquery + term
                dkey, dvalue = mm(dscore, query), mm(p.astype(BF16), dout)
                if name in grads:
                    grads[name] = (grads[name][0] + dkey, grads[name][1] + dvalue)
                else:
                    grads[name] = (dkey, dvalue)
            grad_ref[0, base : base + TILE, :] = (dquery.T * SCALE).astype(BF16)
        for name, (dkey, dvalue) in grads.items():
            dkey, dvalue = (dkey * SCALE).astype(BF16), dvalue.astype(BF16)
            if name is None:
                cgrad_ref[0] = dkey
                cgrad_ref[1] = dvalue
            else:
                where = slice(block * BLK + name * TILE, block * BLK + (name + 1) * TILE)
                grad_ref[1, where, :] = dkey
                grad_ref[2, where, :] = dvalue


def attend_backward(qkv, ckv, dheads, side, lse):
    length, width = qkv.shape[1], qkv.shape[2]
    heads = width // HD
    pick = lambda s: pl.BlockSpec((1, length, HD), lambda h: (s, 0, h))
    pick_context = lambda s: pl.BlockSpec((1, CTX, HD), lambda h: (s, 0, h))
    return pl.pallas_call(
        attend_backward_kernel,
        grid=(heads,),
        in_specs=[
            pick(0),
            pick(1),
            pick(2),
            pick_context(0),
            pick_context(1),
            pl.BlockSpec((1, length, HD), lambda h: (side, 0, h)),
            pl.BlockSpec((1, 1, length), lambda h: (h, 0, 0)),
        ],
        out_specs=[
            pl.BlockSpec((3, length, HD), lambda h: (0, 0, h)),
            pl.BlockSpec((2, CTX, HD), lambda h: (0, 0, h)),
        ],
        out_shape=[
            jax.ShapeDtypeStruct((3, length, width), BF16),
            jax.ShapeDtypeStruct((2, CTX, width), BF16),
        ],
        cost_estimate=brief(),
        name="attend_backward",
    )(qkv, qkv, qkv, ckv, ckv, dheads, lse)


def brief(power=32):
    return pl.CostEstimate(flops=1 << power, bytes_accessed=1 << 16, transcendentals=0)


def roomy():
    return pltpu.CompilerParams(vmem_limit_bytes=56 << 20)


def place_rows(where_ref, tall_ref, out_ref, count):
    size = tall_ref.shape[0] // count
    core = where_ref[1] & 1
    for p in range(count):
        start = pl.multiple_of((p % (count // 2) * 2 + (core ^ (p // (count // 2)))) * size, size)
        out_ref[p * size : (p + 1) * size, :] = tall_ref[pl.ds(start, size), :]


def whole_block(shape):
    return pl.BlockSpec(shape, lambda *_: (0,) * len(shape), pipeline_mode=pl.Buffered(1))


def normalize(values):
    center = values - jnp.mean(values, axis=-1, keepdims=True)
    rstd = lax.rsqrt(jnp.mean(center * center, axis=-1, keepdims=True) + EPS)
    return center * rstd, rstd


def normalize_backward(grad, hat, rstd, gain):
    dn = grad * gain
    return rstd * (dn - jnp.mean(dn, axis=-1, keepdims=True) - hat * jnp.mean(dn * hat, axis=-1, keepdims=True))


def turn_rows(where, values, count):
    length, width = values.shape[2:]
    step = 256

    def kernel(where_ref, x_ref, out_ref, tall):
        tall[...] = x_ref[0, 0].T
        place_rows(where_ref, tall, out_ref, count)

    return pl.pallas_call(
        kernel,
        grid_spec=pltpu.PrefetchScalarGridSpec(
            num_scalar_prefetch=1,
            grid=(length // step,),
            in_specs=[pl.BlockSpec((1, 1, step, width), lambda i, w: (w[0], 0, i, 0))],
            out_specs=pl.BlockSpec((width, step), lambda i, w: (0, i)),
            scratch_shapes=[pltpu.VMEM((width, step), BF16)],
        ),
        out_shape=jax.ShapeDtypeStruct((width, length), BF16),
        cost_estimate=brief(),
        name="turn_rows",
    )(where, values)


def first_norm(where, layer_in, gain, bias, count):
    length, width = layer_in.shape[2:]
    step = 256

    def kernel(where_ref, x_ref, gain_ref, bias_ref, u_ref, ut_ref, tall):
        hat, _ = normalize(x_ref[0, 0].astype(F32))
        u = (hat * gain_ref[...] + bias_ref[...]).astype(BF16)
        u_ref[...] = u
        tall[...] = u.T
        place_rows(where_ref, tall, ut_ref, count)

    return pl.pallas_call(
        kernel,
        grid_spec=pltpu.PrefetchScalarGridSpec(
            num_scalar_prefetch=1,
            grid=(length // step,),
            in_specs=[
                pl.BlockSpec((1, 1, step, width), lambda i, w: (w[0], 0, i, 0)),
                whole_block((1, width)),
                whole_block((1, width)),
            ],
            out_specs=[
                pl.BlockSpec((step, width), lambda i, w: (i, 0)),
                pl.BlockSpec((width, step), lambda i, w: (0, i)),
            ],
            scratch_shapes=[pltpu.VMEM((width, step), BF16)],
        ),
        out_shape=[
            jax.ShapeDtypeStruct((length, width), BF16),
            jax.ShapeDtypeStruct((width, length), BF16),
        ],
        cost_estimate=brief(),
        name="first_norm",
    )(where, layer_in, gain, bias)


def context_rows(where, context, count):
    def kernel(where_ref, c_ref, out_ref, tall):
        tall[...] = c_ref[...].T
        place_rows(where_ref, tall, out_ref, count)

    rows, width = context.shape
    return pl.pallas_call(
        kernel,
        in_specs=[pl.BlockSpec(memory_space=pltpu.SMEM), pl.BlockSpec(memory_space=pltpu.VMEM)],
        out_specs=pl.BlockSpec(memory_space=pltpu.VMEM),
        out_shape=jax.ShapeDtypeStruct((width, rows), BF16),
        scratch_shapes=[pltpu.VMEM((width, rows), BF16)],
        cost_estimate=brief(31),
        name="context_rows",
    )(where, context)


def project(u1, context, weights):
    length, width = u1.shape
    rows = context.shape[0]
    sizes = [w.shape[2] for w in weights]
    group = sum(sizes)

    def kernel(u_ref, c_ref, *refs):
        qkv_ref, ckv_ref, weight_s = refs[len(weights) :]
        start = 0
        for ref, size in zip(refs, sizes):
            weight_s[:, start : start + size] = ref[0]
            start += size
        for part in chunks(length):
            qkv_ref[0, part, :] = mm(u_ref[part, :], weight_s[...]).astype(BF16)

        @pl.when(pl.program_id(0) > 0)
        def _():
            ckv_ref[0] = mm(c_ref[...], weight_s[...]).astype(BF16)

    return pl.pallas_call(
        kernel,
        grid=(3,),
        in_specs=[whole_block((length, width)), whole_block((rows, width))]
        + [pl.BlockSpec((1, width, size), lambda s: (s, 0, 0)) for size in sizes],
        out_specs=[
            pl.BlockSpec((1, length, group), lambda s: (s, 0, 0)),
            pl.BlockSpec((1, rows, group), lambda s: (jnp.maximum(s - 1, 0), 0, 0)),
        ],
        out_shape=[
            jax.ShapeDtypeStruct((3, length, group), BF16),
            jax.ShapeDtypeStruct((2, rows, group), BF16),
        ],
        scratch_shapes=[pltpu.VMEM((width, group), BF16)],
        compiler_params=roomy(),
        cost_estimate=brief(31),
        name="project",
    )(u1, context, *weights)


def attention_out(where, layer_in, heads_own, heads_other, out_own, out_first, out_second, gain, bias, count):
    length, width = layer_in.shape[2:]
    group = heads_own.shape[1]
    half = group // 2
    step = 256

    def kernel(where_ref, x_ref, ho_ref, ht_ref, wo_ref, w1_ref, w2_ref, gain_ref, bias_ref, x1_ref, u_ref, ut_ref, tall):
        x1 = x_ref[0, 0].astype(F32) + mm(ho_ref[...], wo_ref[...])
        x1 += mm(ht_ref[:, :half], w1_ref[...]) + mm(ht_ref[:, half:], w2_ref[...])
        x1_ref[...] = x1
        hat, _ = normalize(x1)
        u = (hat * gain_ref[...] + bias_ref[...]).astype(BF16)
        u_ref[...] = u
        tall[...] = u.T
        place_rows(where_ref, tall, ut_ref, count)

    row = lambda i, w: (i, 0)
    return pl.pallas_call(
        kernel,
        grid_spec=pltpu.PrefetchScalarGridSpec(
            num_scalar_prefetch=1,
            grid=(length // step,),
            in_specs=[
                pl.BlockSpec((1, 1, step, width), lambda i, w: (w[0], 0, i, 0)),
                pl.BlockSpec((step, group), row),
                pl.BlockSpec((step, group), row),
                whole_block((group, width)),
                whole_block((half, width)),
                whole_block((half, width)),
                whole_block((1, width)),
                whole_block((1, width)),
            ],
            out_specs=[
                pl.BlockSpec((step, width), row),
                pl.BlockSpec((step, width), row),
                pl.BlockSpec((width, step), lambda i, w: (0, i)),
            ],
            scratch_shapes=[pltpu.VMEM((width, step), BF16)],
        ),
        out_shape=[
            jax.ShapeDtypeStruct((length, width), F32),
            jax.ShapeDtypeStruct((length, width), BF16),
            jax.ShapeDtypeStruct((width, length), BF16),
        ],
        compiler_params=roomy(),
        cost_estimate=brief(),
        name="attention_out",
    )(where, layer_in, heads_own, heads_other, out_own, out_first, out_second, gain, bias)


TALL = 256
STEP = 512


def chunks(length):
    return [slice(i, i + TALL) for i in range(0, length, TALL)]


def gelu_pair(pre):
    root = math.sqrt(2.0 / math.pi)
    straight = root * pre
    inner = straight * (1.0 + 0.044715 * (pre * pre))
    bend = jnp.tanh(inner)
    lean = 1.5 * inner - straight
    half = 0.5 * pre
    hid = half + half * bend
    slope = (0.5 + lean) + bend * (0.5 - lean * bend)
    return hid.astype(BF16), slope.astype(BF16)


def hidden_forward(u2, dy_rows, up, before):
    length, width = u2.shape
    half = width // 2
    gathered = up.ndim == 4
    steps = 2 * width // STEP
    first = 0 if before is None else steps

    def kernel(u_ref, dy_ref, up_ref, *refs):
        hid_ref, slope_ref, sent_ref, kept_ref = refs[-4:]
        weight = up_ref[...].reshape(width, STEP)
        for rows in chunks(length):
            hid, slope = gelu_pair(mm(u_ref[rows, :], weight))
            hid_ref[rows, :] = hid
            slope_ref[rows, :] = slope
        hid = hid_ref[...]
        for rows in chunks(half):
            sent_ref[rows, :] = mm(dy_ref[half + rows.start : half + rows.stop, :], hid).astype(BF16)
        for rows in chunks(half):
            kept_ref[rows, :] = mm(dy_ref[rows, :], hid).astype(BF16)

    if gathered:
        up_spec = pl.BlockSpec((up.shape[0], 1, up.shape[2], STEP), lambda j: (0, j // 2, 0, lax.rem(j, 2)))
    else:
        up_spec = pl.BlockSpec((width, STEP), lambda j: (0, j))
    tile = pl.BlockSpec((length, STEP), lambda j: (0, first + j))
    part = pl.BlockSpec((half, STEP), lambda j: (0, j))
    wide = jax.ShapeDtypeStruct((length, 2 * steps * STEP), BF16)
    return pl.pallas_call(
        kernel,
        grid=(steps,),
        in_specs=[whole_block((length, width)), whole_block((width, length)), up_spec]
        + ([] if before is None else [pl.BlockSpec(memory_space=pl.ANY)] * 2),
        out_specs=[tile, tile, part, part],
        out_shape=[wide, wide] + [jax.ShapeDtypeStruct((half, steps * STEP), BF16)] * 2,
        input_output_aliases={} if before is None else {3: 0, 4: 1},
        compiler_params=roomy(),
        cost_estimate=brief(37),
        name="hidden_forward",
    )(u2, dy_rows, up, *(before or ()))


def hidden_backward(where, cotangent, hid, slope, down_own, buffer, u2_rows, x1):
    length, width = x1.shape
    half = width // 2
    pieces, _, rows_each, _ = buffer.shape
    side = 2 * width // STEP
    steps = 2 * side

    def kernel(
        where_ref, dy_ref, hid_ref, slope_ref, down_ref, down2_ref, ut_ref, x1_ref,
        layer_ref, dpre_ref, sent_ref, kept_ref,
        down_s, mix_s, x1_s, sem,
    ):
        j = pl.program_id(0)
        fetch = pltpu.make_async_copy(x1_ref, x1_s, sem)

        @pl.when(j == 0)
        def _():
            fetch.start()
            mix_s[...] = jnp.zeros_like(mix_s)

        @pl.when(j < side)
        def _():
            down_s[...] = down_ref[...]

        @pl.when(j >= side)
        def _():
            down_s[...] = down2_ref[...].reshape(STEP, width)

        for rows in chunks(length):
            dhid = mm_nt(dy_ref[0, 0, rows, :], down_s[...])
            dpre_ref[rows, :] = (dhid * slope_ref[rows, :].astype(F32)).astype(BF16)
        for rows in chunks(length):
            mix_s[rows, :] += mm(hid_ref[rows, :], down_s[...])
        dpre = dpre_ref[...]
        for rows in chunks(half):
            sent_ref[rows, :] = mm(ut_ref[half + rows.start : half + rows.stop, :], dpre).astype(BF16)
        for rows in chunks(half):
            kept_ref[rows, :] = mm(ut_ref[rows, :], dpre).astype(BF16)

        @pl.when(j == steps - 1)
        def _():
            fetch.wait()
            for rows in chunks(length):
                layer_ref[rows, :] = (x1_s[rows, :] + mix_s[rows, :]).astype(BF16)

    low = lambda j: jnp.minimum(j, side - 1)
    high = lambda j: jnp.maximum(j - side, 0)
    tile = pl.BlockSpec((length, STEP), lambda j, w: (0, j))
    part = pl.BlockSpec((half, STEP), lambda j, w: (0, j))
    return pl.pallas_call(
        kernel,
        grid_spec=pltpu.PrefetchScalarGridSpec(
            num_scalar_prefetch=1,
            grid=(steps,),
            in_specs=[
                pl.BlockSpec((1, 1, length, width), lambda j, w: (w[0], 0, 0, 0), pipeline_mode=pl.Buffered(1)),
                tile,
                tile,
                pl.BlockSpec((STEP, width), lambda j, w: (low(j), 0)),
                pl.BlockSpec((pieces // side, 2, rows_each, width), lambda j, w: (high(j), 1, 0, 0)),
                whole_block((width, length)),
                pl.BlockSpec(memory_space=pl.ANY),
            ],
            out_specs=[whole_block((length, width)), tile, part, part],
            scratch_shapes=[
                pltpu.VMEM((STEP, width), BF16),
                pltpu.VMEM((length, width), F32),
                pltpu.VMEM((length, width), F32),
                pltpu.SemaphoreType.DMA,
            ],
        ),
        out_shape=[
            jax.ShapeDtypeStruct((length, width), BF16),
            jax.ShapeDtypeStruct((length, steps * STEP), BF16),
            jax.ShapeDtypeStruct((half, steps * STEP), BF16),
            jax.ShapeDtypeStruct((half, steps * STEP), BF16),
        ],
        compiler_params=roomy(),
        cost_estimate=brief(),
        name="hidden_backward",
    )(where, cotangent, hid, slope, down_own, buffer, u2_rows, x1)


def second_norm_backward(where, cotangent, dpre, up_own, buffer, x1, gain, out_own, out_first, out_second, count):
    length, width = x1.shape
    group = out_own.shape[0]
    pieces, _, rows_each, _ = buffer.shape
    side = 2
    tiles = 2 * side
    steps = tiles + 2
    chunk = 128

    def kernel(
        where_ref, dpre_ref, up_ref, up2_ref, dy_ref, x1_ref, gain_ref, wo_ref, w1_ref, w2_ref,
        dattn_ref, turned_ref, dheads_ref, sums_ref,
        up_s, out_s, grad_s, tall, dy_s, x1_s, sems,
    ):
        j = pl.program_id(0)
        fetches = [
            pltpu.make_async_copy(x1_ref, x1_s, sems.at[0]),
            pltpu.make_async_copy(dy_ref.at[where_ref[0], 0], dy_s, sems.at[1]),
        ]

        @pl.when(j == 0)
        def _():
            for fetch in fetches:
                fetch.start()
            grad_s[...] = jnp.zeros_like(grad_s)
            sums_ref[...] = jnp.zeros_like(sums_ref)

        @pl.when(j < side)
        def _():
            up_s[...] = up_ref[...]

        @pl.when(jnp.logical_and(j >= side, j < tiles))
        def _():
            up_s[...] = up2_ref[...].reshape(width, width)

        @pl.when(j < tiles)
        def _():
            for rows in chunks(length):
                grad_s[rows, :] += mm_nt(dpre_ref[rows, :], up_s[...])

        @pl.when(j == tiles - 1)
        def _():
            for fetch in fetches:
                fetch.wait()

            @pl.loop(0, length // chunk)
            def _(i):
                rows = pl.ds(pl.multiple_of(i * chunk, chunk), chunk)
                du = grad_s[rows, :]
                hat, rstd = normalize(x1_s[rows, :])
                sums_ref[0:1, :] += jnp.sum(du * hat, axis=0, keepdims=True)
                sums_ref[1:2, :] += jnp.sum(du, axis=0, keepdims=True)
                out = dy_s[rows, :].astype(F32) + normalize_backward(du, hat, rstd, gain_ref[...])
                out = out.astype(BF16)
                dattn_ref[rows, :] = out
                tall[:, rows] = out.T

            place_rows(where_ref, tall, turned_ref, count)

        @pl.when(j == tiles)
        def _():
            out_s[...] = wo_ref[...]

        @pl.when(j == tiles + 1)
        def _():
            out_s[: group // 2, :] = w1_ref[...]
            out_s[group // 2 :, :] = w2_ref[...]

        @pl.when(j >= tiles)
        def _():
            for rows in chunks(length):
                dheads_ref[0, rows, :] = mm_nt(dattn_ref[rows, :], out_s[...]).astype(BF16)

    low = lambda j: jnp.minimum(j, side - 1)
    high = lambda j: jnp.clip(j - side, 0, side - 1)
    return pl.pallas_call(
        kernel,
        grid_spec=pltpu.PrefetchScalarGridSpec(
            num_scalar_prefetch=1,
            grid=(steps,),
            in_specs=[
                pl.BlockSpec((length, width), lambda j, w: (0, jnp.minimum(j, tiles - 1))),
                pl.BlockSpec((width, width), lambda j, w: (0, low(j))),
                pl.BlockSpec((pieces, 1, rows_each, width), lambda j, w: (0, high(j), 0, 0)),
                pl.BlockSpec(memory_space=pl.ANY),
                pl.BlockSpec(memory_space=pl.ANY),
                whole_block((1, width)),
                whole_block((group, width)),
                whole_block((group // 2, width)),
                whole_block((group // 2, width)),
            ],
            out_specs=[
                whole_block((length, width)),
                whole_block((width, length)),
                pl.BlockSpec((1, length, group), lambda j, w: (jnp.maximum(j - tiles, 0), 0, 0)),
                whole_block((2, width)),
            ],
            scratch_shapes=[
                pltpu.VMEM((width, width), BF16),
                pltpu.VMEM((group, width), BF16),
                pltpu.VMEM((length, width), F32),
                pltpu.VMEM((width, length), BF16),
                pltpu.VMEM((length, width), BF16),
                pltpu.VMEM((length, width), F32),
                pltpu.SemaphoreType.DMA((2,)),
            ],
        ),
        out_shape=[
            jax.ShapeDtypeStruct((length, width), BF16),
            jax.ShapeDtypeStruct((width, length), BF16),
            jax.ShapeDtypeStruct((2, length, group), BF16),
            jax.ShapeDtypeStruct((2, width), F32),
        ],
        compiler_params=roomy(),
        cost_estimate=brief(),
        name="second_norm_backward",
    )(where, dpre, up_own, buffer, cotangent, x1, gain, out_own, out_first, out_second)


def projection_rows(u1_rows, context_turned, dqkv, dckv, dattn_rows, heads):
    width, length = u1_rows.shape
    half = width // 2
    group = heads.shape[1]

    def kernel(ut_ref, cut_ref, grad_ref, cgrad_ref, dt_ref, heads_ref, kept_ref, *sent_refs):
        s = pl.program_id(0)

        def emit(product):
            for rows in chunks(half):
                kept_ref[rows, :] = product(rows.start).astype(BF16)
            for rows in chunks(half):
                sent = product(half + rows.start).astype(BF16)
                for k, ref in enumerate(sent_refs):

                    @pl.when(s == k)
                    def _(ref=ref, rows=rows, sent=sent):
                        ref[rows, :] = sent

        @pl.when(s < 3)
        def _():
            grad = grad_ref[0]
            cgrad = jnp.where(s > 0, cgrad_ref[0], jnp.zeros_like(cgrad_ref[0]))

            def product(start):
                here = slice(start, start + TALL)
                return mm(ut_ref[here, :], grad) + mm(cut_ref[here, :], cgrad)

            emit(product)

        @pl.when(s == 3)
        def _():
            heads = heads_ref[...]
            emit(lambda start: mm(dt_ref[start : start + TALL, :], heads))

    part = pl.BlockSpec((half, group), lambda s: (0, s))
    return pl.pallas_call(
        kernel,
        grid=(4,),
        in_specs=[
            whole_block((width, length)),
            whole_block((width, CTX)),
            pl.BlockSpec((1, length, group), lambda s: (jnp.minimum(s, 2), 0, 0)),
            pl.BlockSpec((1, CTX, group), lambda s: (jnp.clip(s - 1, 0, 1), 0, 0)),
            whole_block((width, length)),
            whole_block((length, group)),
        ],
        out_specs=[part] + [whole_block((half, group))] * 4,
        out_shape=[jax.ShapeDtypeStruct((half, 4 * group), BF16)]
        + [jax.ShapeDtypeStruct((half, group), BF16)] * 4,
        compiler_params=roomy(),
        cost_estimate=brief(),
        name="projection_rows",
    )(u1_rows, context_turned, dqkv, dckv, dattn_rows, heads)


def inputs_backward(part, where, dsides, qkv_own, qkv_first, qkv_second, u1, coef, skip, state, layer_in, dattn, gain):
    length, width = layer_in.shape[2] // 2, layer_in.shape[3]
    group = qkv_own.shape[2]
    steps = 6
    chunk = 128
    before = BLK // CH - 1

    def kernel(
        where_ref, do_ref, dt_ref, co_ref, ct_ref, own_ref, w1_ref, w2_ref, v_ref, rates_ref,
        norms_ref, coef_ref, skip_ref, state_ref, x_ref, dx_ref, gain_ref,
        out_ref, sums_ref, *rest,
    ):
        grad_s, cgrad_s, weight_s, total, ctotal, within = rest[-6:]
        small_ref = rest[0]
        j = pl.program_id(0)

        @pl.when(j == 0)
        def _():
            total[...] = jnp.zeros_like(total)
            ctotal[...] = jnp.zeros_like(ctotal)
            sums_ref[...] = jnp.zeros_like(sums_ref)
            if part == 0:
                for n in range(NS):
                    within[n] = decay_within(n, True)

        @pl.when(j < 3)
        def _():
            grad_s[...] = do_ref[0]
            cgrad_s[...] = co_ref[0]
            weight_s[...] = own_ref[0]

        @pl.when(j >= 3)
        def _():
            grad_s[...] = dt_ref[0]
            cgrad_s[...] = ct_ref[0]
            weight_s[:, : group // 2] = w1_ref[0]
            weight_s[:, group // 2 :] = w2_ref[0]

        @pl.when(lax.rem(j, 3) == 0)
        def _():
            cgrad_s[...] = jnp.zeros_like(cgrad_s)

        for rows in chunks(length):
            total[rows, :] += mm_nt(grad_s[rows, :], weight_s[...])
        if part == 0:
            ctotal[...] += mm_nt(cgrad_s[...], weight_s[...])

        def state_space():
            carry_in, carry_out, whole = decay_vectors(rates_ref[...], norms_ref[...])

            @pl.loop(0, width // 256)
            def _(c):
                here = pl.ds(pl.multiple_of(c * 256, 256), 256)
                rows = v_ref[:, here].astype(F32)
                grad = ctotal[:, here].astype(BF16)
                wide = grad.astype(F32)
                du = skip_ref[:, here] * wide
                reach = jnp.dot(carry_in, wide, precision=HIGHEST, preferred_element_type=F32)
                for n in range(NS):
                    back = mm(within[n], grad)
                    du += coef_ref[n : n + 1, here] * back
                    small_ref[n : n + 1, here] = (
                        jnp.sum(rows * back, axis=0, keepdims=True) + state_ref[n : n + 1, here] * reach[n : n + 1, :]
                    )
                small_ref[NS : NS + 1, here] = jnp.sum(rows * wide, axis=0, keepdims=True)
                total[before * CH : (before + 1) * CH, here] += du
                carried = coef_ref[:, here] * reach
                for k in reversed(range(before)):
                    total[k * CH : (k + 1) * CH, here] += lax.dot_general(
                        carry_out.astype(F32),
                        carried,
                        (((0,), (0,)), ((), ())),
                        precision=HIGHEST,
                        preferred_element_type=F32,
                    )
                    carried = whole * carried

        @pl.when(j == steps - 1)
        def _():
            if part == 0:
                state_space()

            @pl.loop(0, length // chunk)
            def _(i):
                rows = pl.ds(pl.multiple_of(i * chunk, chunk), chunk)
                du = total[rows, :]
                hat, rstd = normalize(x_ref[0, 0, rows, :].astype(F32))
                sums_ref[0:1, :] += jnp.sum(du * hat, axis=0, keepdims=True)
                sums_ref[1:2, :] += jnp.sum(du, axis=0, keepdims=True)
                out = dx_ref[rows, :].astype(F32) + normalize_backward(du, hat, rstd, gain_ref[...])
                out_ref[rows, :] = out.astype(BF16)

    low = lambda j: jnp.minimum(j, 2)
    high = lambda j: jnp.maximum(j - 3, 0)
    back = lambda s: jnp.maximum(s - 1, 0)
    mine = pl.BlockSpec((1, 1, length, width), lambda j, w: (w[0], 0, part, 0), pipeline_mode=pl.Buffered(1))
    (dqkv_own, dckv_own), (dqkv_other, dckv_other) = dsides
    return pl.pallas_call(
        kernel,
        grid_spec=pltpu.PrefetchScalarGridSpec(
            num_scalar_prefetch=1,
            grid=(steps,),
            in_specs=[
                pl.BlockSpec((1, length, group), lambda j, w: (low(j), part, 0)),
                pl.BlockSpec((1, length, group), lambda j, w: (high(j), part, 0)),
                pl.BlockSpec((1, CTX, group), lambda j, w: (back(low(j)), 0, 0)),
                pl.BlockSpec((1, CTX, group), lambda j, w: (back(high(j)), 0, 0)),
                pl.BlockSpec((1, width, group), lambda j, w: (low(j), 0, 0)),
                pl.BlockSpec((1, width, group // 2), lambda j, w: (high(j), 0, 0)),
                pl.BlockSpec((1, width, group // 2), lambda j, w: (high(j), 0, 0)),
                pl.BlockSpec((CH, width), lambda j, w: (before, 0)),
                whole_block((NS, 1)),
                whole_block((NS, 1)),
                whole_block((NS, width)),
                whole_block((1, width)),
                whole_block((NS, width)),
                mine,
                pl.BlockSpec((length, width), lambda j, w: (part, 0), pipeline_mode=pl.Buffered(1)),
                whole_block((1, width)),
            ],
            out_specs=[
                whole_block((length, width)),
                whole_block((2, width)),
                *([whole_block((NS + 1, width))] if part == 0 else []),
            ],
            scratch_shapes=[
                pltpu.VMEM((length, group), BF16),
                pltpu.VMEM((CTX, group), BF16),
                pltpu.VMEM((width, group), BF16),
                pltpu.VMEM((length, width), F32),
                pltpu.VMEM((CTX, width), F32),
                pltpu.VMEM((NS, CH, CH), BF16),
            ],
        ),
        out_shape=[
            jax.ShapeDtypeStruct((length, width), BF16),
            jax.ShapeDtypeStruct((2, width), F32),
            *([jax.ShapeDtypeStruct((NS + 1, width), F32)] if part == 0 else []),
        ],
        compiler_params=roomy(),
        cost_estimate=brief(),
        name="inputs_backward",
    )(
        where, dqkv_own, dqkv_other, dckv_own, dckv_other, qkv_own, qkv_first, qkv_second,
        u1, *decay_arrays(), coef, skip, state, layer_in, dattn, gain,
    )


def join(where, kept, got, swap, above, below, bit, power=32):
    rows, columns = kept.shape
    pieces = list(got) if isinstance(got, (list, tuple)) else [got]
    width = columns // len(pieces) if len(pieces) > 1 else 2 * STEP
    shape = (above, 2, below)

    def kernel(where_ref, kept_ref, *refs):
        keep_ref, send_ref = refs[-2:]
        mine = (where_ref[1] >> bit) & 1

        def emit(got_ref):
            for out_ref, index in ((keep_ref, mine), (send_ref, 1 - mine)):
                come = got_ref[:, pl.ds(index, 1)][:, 0].astype(F32)
                if swap:
                    come = jnp.concatenate([come[..., width // 2 :], come[..., : width // 2]], axis=-1)
                out_ref[...] = (kept_ref[:, pl.ds(index, 1)][:, 0].astype(F32) + come).astype(BF16)

        if len(pieces) == 1:
            emit(refs[0])
        else:
            for k in range(len(pieces)):

                @pl.when(pl.program_id(0) == k)
                def _(ref=refs[k]):
                    emit(ref)

    tile = pl.BlockSpec((above, 2, below, width), lambda j, w: (0, 0, 0, j))
    out = pl.BlockSpec((above, below, width), lambda j, w: (0, 0, j))
    many = [tile] if len(pieces) == 1 else [whole_block((*shape, width))] * len(pieces)
    keep, send = pl.pallas_call(
        kernel,
        grid_spec=pltpu.PrefetchScalarGridSpec(
            num_scalar_prefetch=1, grid=(columns // width,), in_specs=[tile, *many], out_specs=[out, out]
        ),
        out_shape=[jax.ShapeDtypeStruct((above, below, columns), BF16)] * 2,
        compiler_params=roomy(),
        cost_estimate=brief(power),
        name="join",
    )(where, kept.reshape(*shape, columns), *[piece.reshape(*shape, -1) for piece in pieces])
    return keep.reshape(rows // 2, columns), send.reshape(rows // 2, columns)


def add_pairs(where, *pairs, power=37):
    rows, columns = pairs[0][0].shape
    width = min(columns, 4 * STEP)
    tiles = columns // width

    def kernel(where_ref, *refs):
        out_ref = refs[-1]
        for k in range(len(pairs)):

            @pl.when(pl.program_id(0) // tiles == k)
            def _(left=refs[2 * k], right=refs[2 * k + 1]):
                out_ref[...] = (left[...].astype(F32) + right[...].astype(F32)).astype(BF16)

    def spec(k):
        return pl.BlockSpec((rows, width), lambda j, w: (0, jnp.clip(j - k * tiles, 0, tiles - 1)))

    return pl.pallas_call(
        kernel,
        grid_spec=pltpu.PrefetchScalarGridSpec(
            num_scalar_prefetch=1,
            grid=(len(pairs) * tiles,),
            in_specs=[spec(k) for k in range(len(pairs)) for _ in range(2)],
            out_specs=pl.BlockSpec((rows, width), lambda j, w: (0, j)),
        ),
        out_shape=jax.ShapeDtypeStruct((rows, len(pairs) * columns), BF16),
        cost_estimate=brief(power),
        name="add_pairs",
    )(where, *[value for pair in pairs for value in pair])


def both_parts(where, own, come, kind, power):
    step = min(piece.shape[0] for piece in own + come)
    width = own[0].shape[1]
    steps = sum(piece.shape[0] for piece in own) // step
    def kernel(where_ref, *refs):
        out_ref = refs[-1]
        here = pl.program_id(0) == where_ref[0]
        for side, pieces in enumerate((refs[: len(own)], refs[len(own) : -1])):
            mine = jnp.logical_not(here) if side else here
            at = 0
            for ref in pieces:
                for start in range(0, ref.shape[0], step):

                    @pl.when(mine & (pl.program_id(1) == at))
                    def _(ref=ref, start=start):
                        out_ref[0, 0] = ref[start : start + step, :].astype(kind)

                    at += 1

    return pl.pallas_call(
        kernel,
        grid_spec=pltpu.PrefetchScalarGridSpec(
            num_scalar_prefetch=1,
            grid=(2, steps),
            in_specs=[whole_block(piece.shape) for piece in own + come],
            out_specs=pl.BlockSpec((1, 1, step, width), lambda m, i, w: (m, 0, i, 0)),
        ),
        out_shape=jax.ShapeDtypeStruct((2, 1, steps * step, width), kind),
        compiler_params=roomy(),
        cost_estimate=brief(power),
        name="both_parts",
    )(where, *own, *come)


def swap_halves(values, width):
    half = width // 2
    order = [start + half * k for start in range(0, values.shape[1], width) for k in (1, 0)]
    return jnp.concatenate([values[:, i : i + half] for i in order], axis=1)


def shards(
    dp_count,
    layer_in,
    ln1_gain,
    ln1_bias,
    qkv_weight,
    out_weight,
    ssm_coef,
    ssm_skip,
    ln2_gain,
    ln2_bias,
    up_weight,
    down_weight,
    cotangent,
):
    width = layer_in.shape[3]
    group = qkv_weight.shape[2]
    mine = lax.axis_index("tensor")
    place = lax.axis_index("dp")
    where = jnp.stack([mine, place]).astype(jnp.int32)
    rows_each = width // dp_count
    gain1, bias1, gain2, bias2 = ln1_gain[None], ln1_bias[None], ln2_gain[None], ln2_bias[None]

    over_x = lambda v: swap(v, "tensor", 1, 2)
    over = lambda v, bit: swap(v, "dp", 1 << bit, dp_count)
    core = place & 1

    def scatter(values, depth):
        groups = [[(k << depth) | low for k in range(dp_count >> depth)] for low in range(1 << depth)]
        return lax.psum_scatter(values, "dp", scatter_dimension=0, axis_index_groups=groups, tiled=True)

    bits = dp_count.bit_length() - 1

    def part_of(weight, axis, index, count):
        size = weight.shape[axis] // count
        return lax.dynamic_slice_in_dim(weight, index * size, size, axis)

    up_mine = part_of(up_weight, 0, place, dp_count)
    feed = jnp.concatenate([up_mine[:, :width], up_mine[:, width:], part_of(down_weight, 0, place, dp_count)], axis=0)
    feed = over_x(feed)
    qkv_first = over_x(part_of(qkv_weight, 2, core, 2))
    small = over_x(jnp.concatenate([ssm_coef, ssm_skip[None]], axis=0))
    out_first = over_x(part_of(out_weight, 0, core, 2))

    def in_order(own, other, axis):
        return jnp.where(
            mine == 0, jnp.concatenate([own, other], axis=axis), jnp.concatenate([other, own], axis=axis)
        )

    coef = in_order(ssm_coef, small[:NS], 1)
    skip = in_order(ssm_skip[None], small[NS:], 1)

    dy_rows = turn_rows(where, cotangent, dp_count)
    feed = tie(feed, dy_rows)
    buffer = lax.all_gather(feed, "dp", axis=0, tiled=True).reshape(dp_count, 4, rows_each, width)
    u1, u1_rows = first_norm(tie(where, feed, small), layer_in, gain1, bias1, dp_count)
    context, state = ssm_forward(u1, coef, skip)
    context_turned = context_rows(tie(where, context), context, dp_count)
    qkv_own, ckv_own = project(u1, tie(context, context_turned), (qkv_weight,))
    heads_own, lse_own = attend_forward(qkv_own, ckv_own)
    qkv_first = tie(qkv_first, heads_own)
    qkv_second = over(qkv_first, 0)
    qkv_other, ckv_other = project(tie(u1, heads_own), context, (qkv_first, qkv_second))
    out_first = tie(out_first, qkv_other)
    out_second = over(out_first, 0)
    heads_other, lse_other = attend_forward(qkv_other, tie(ckv_other, out_first))
    out_second = tie(out_second, heads_other)
    x1, u2, u2_rows = attention_out(
        where, layer_in, heads_own, heads_other, out_weight, out_first, out_second, gain2, bias2, dp_count
    )
    hid, slope, sent, kept_own = hidden_forward(u2, dy_rows, up_weight, None)
    got_own = over(sent, 0)
    hid, slope, sent, kept_other = hidden_forward(u2, dy_rows, buffer, (hid, slope))
    got_other = over(sent, 0)

    split_y = (dp_count // 4, rows_each, 1)
    down_keep_own, down_send_own = join(tie(where, sent), kept_own, got_own, False, *split_y)
    down_got_own = over(down_send_own, 1)
    down_keep_other, down_send_other = join(tie(where, down_send_own), kept_other, got_other, False, *split_y)
    down_got_other = over(down_send_other, 1)
    layer_out, dpre, up_sent, up_kept = hidden_backward(
        tie(where, down_send_other), cotangent, hid, slope, down_weight, buffer, u2_rows, x1
    )
    up_got = over(up_sent, 0)
    layer_come = over_x(layer_out)
    down_sum = add_pairs(
        tie(where, layer_out), (down_keep_own, down_got_own), (down_keep_other, down_got_other)
    )
    up_keep, up_send = join(tie(where, down_sum), up_kept, up_got, False, *split_y)
    down_sum = scatter(down_sum, 2)
    up_got = over(up_send, 1)
    dattn, dattn_rows, dheads, sums2 = second_norm_backward(
        tie(where, up_send),
        cotangent,
        dpre,
        up_weight,
        buffer,
        x1,
        gain2,
        out_weight,
        out_first,
        out_second,
        dp_count,
    )
    dqkv_other, dckv_other = attend_backward(qkv_other, ckv_other, dheads, 1, lse_other)
    other_kept, *other_sent = projection_rows(
        u1_rows, context_turned, dqkv_other, dckv_other, dattn_rows, heads_other
    )
    other_got = [over(piece, 0) for piece in other_sent]
    layer_come = tie(layer_come, other_kept)
    up_sum = add_pairs(tie(where, other_kept, layer_come), (up_keep, up_got))
    dqkv_own, dckv_own = attend_backward(qkv_own, ckv_own, tie(dheads, up_sum), 0, lse_own)
    up_sum = scatter(up_sum, 2)
    other_keep, other_send = join(
        tie(where, dqkv_own), other_kept, [tie(piece, dqkv_own) for piece in other_got], True, *split_y
    )
    other_got = over(other_send, 1)
    own_kept, *own_sent = projection_rows(
        tie(u1_rows, other_send), context_turned, dqkv_own, dckv_own, dattn_rows, heads_own
    )
    own_got = [over(piece, 0) for piece in own_sent]
    down_sum = tie(down_sum, own_kept)

    def inputs_half(part, *deps):
        return inputs_backward(
            part,
            tie(where, *deps),
            ((dqkv_own, dckv_own), (dqkv_other, dckv_other)),
            qkv_weight,
            qkv_first,
            qkv_second,
            u1,
            coef,
            skip,
            state,
            layer_in,
            dattn,
            gain1,
        )

    grad_high, sums_high = inputs_half(1, own_kept, down_sum)
    come_high = over_x(grad_high)
    other_sum = add_pairs(tie(where, grad_high), (other_keep, other_got), power=20)
    own_keep, own_send = join(tie(where, other_sum), own_kept, own_got, False, *split_y)
    own_got = over(own_send, 1)
    up_sum = tie(up_sum, own_send)
    grad_low, sums_low, small_ssm = inputs_half(0, own_send, up_sum)
    middle = grad_low.shape[0] // 2
    come_0 = over_x(grad_low[:middle])
    small_all = jnp.concatenate([small_ssm, sums2, sums_low + sums_high], axis=0)
    small_all = small_all + over_x(small_all)
    other_sum = scatter(other_sum, 2)

    def rows_of(bit):
        return (dp_count >> (bit + 1), rows_each << (bit - 2), bit)

    own_keep, own_send = join(
        tie(where, grad_low, come_high, small_all, come_0, other_sum),
        own_keep,
        own_got,
        False,
        *rows_of(2),
        37,
    )
    own_got, small_got = over(own_send, 2), over(small_all, 0)
    hidden = up_weight.shape[1]
    final = jnp.concatenate([down_sum[:, hidden:], up_sum[:, hidden:], other_sum], axis=1)
    final_come = over_x(tie(final, own_send))
    come_1 = over_x(tie(grad_low[middle:], own_send))
    layer_pair = both_parts(tie(where, own_send), (layer_out,), (layer_come,), BF16, 32)
    small_all = small_all + tie(small_got, layer_pair)
    small_got = over(small_all, 1)
    rows = own_keep.shape[0]
    total = own_keep.astype(F32) + tie(own_got, small_all, come_1)
    for bit in range(3, bits):
        rows //= 2
        spread = total.reshape(dp_count >> (bit + 1), 2, -1, total.shape[1])
        mybit = (place >> bit) & 1
        pick = lambda index: lax.dynamic_index_in_dim(spread, index, 1, keepdims=False).reshape(rows, -1)
        send = pick(1 - mybit).astype(BF16)
        got = over(send, bit)
        small_all = small_all + tie(small_got, send)
        small_got = over(small_all, bit - 1)
        total = pick(mybit) + tie(got, small_all)
    own_total = total
    small_all = small_all + small_got
    small_got = over(small_all, bits - 1)
    grad_pair = both_parts(tie(where, small_all), (grad_low, grad_high), (come_0, come_1, come_high), F32, 32)
    small_all = small_all + tie(small_got, grad_pair)
    final_come = tie(final_come, small_all).astype(F32)
    down_come, up_come = final_come[:, :hidden], final_come[:, hidden : 2 * hidden]
    other_come = final_come[:, 2 * hidden :]
    here = lax.dynamic_slice_in_dim(small_all[: NS + 1], mine * group, group, 1)

    def ordered(values):
        return jnp.where(core == 1, swap_halves(values, group), values)

    grad_down = down_sum[:, :hidden].astype(F32) + down_come
    grad_up = up_sum[:, :hidden].astype(F32) + up_come
    grad_qkv_out = own_total + ordered(other_come)
    grad_qkv, grad_out = grad_qkv_out[:, : 3 * group], grad_qkv_out[:, 3 * group :]

    return (
        layer_pair,
        grad_pair,
        small_all[NS + 3],
        small_all[NS + 4],
        grad_qkv.reshape(rows_each, 3, group).swapaxes(0, 1),
        grad_out.T,
        here[:NS],
        here[NS],
        small_all[NS + 1],
        small_all[NS + 2],
        grad_up,
        grad_down.T,
    )


def solution(mesh):
    in_specs = (
        P(None, "dp", None, None),
        P(),
        P(),
        P(None, None, "tensor"),
        P("tensor", None),
        P(None, "tensor"),
        P("tensor"),
        P(),
        P(),
        P(None, "tensor"),
        P("tensor", None),
        P(None, "dp", None, None),
    )
    out_specs = (
        P(None, "dp", None, None),
        P(None, "dp", None, None),
        P(),
        P(),
        P(None, "dp", "tensor"),
        P("tensor", "dp"),
        P(None, "tensor"),
        P("tensor"),
        P(),
        P(),
        P("dp", "tensor"),
        P("tensor", "dp"),
    )
    body = functools.partial(shards, mesh.shape["dp"])
    return jax.shard_map(body, mesh=mesh, in_specs=in_specs, out_specs=out_specs, check_vma=False)
```

```python
import functools
import math

import jax
import jax.numpy as jnp
from jax import lax
from jax.experimental import pallas as pl
from jax.experimental.pallas import tpu as pltpu
from jax.sharding import PartitionSpec as P
import numpy as np

HD = 128
NS = 16
BLK = 512
CTX = 128
CH = 128
TILE = 256
EPS = 1e-05
F32 = jnp.float32
BF16 = jnp.bfloat16
HIGHEST = lax.Precision.HIGHEST
SCALE = HD**-0.5
LOG2 = SCALE * math.log2(math.e)


def swap(value, axis, mask, count):
    return lax.ppermute(value, axis, [(i, i ^ mask) for i in range(count)])


def tie(value, *deps):
    return lax.optimization_barrier((value, *deps))[0] if deps else value


def mm(left, right):
    return lax.dot_general(left, right, (((1,), (0,)), ((), ())), preferred_element_type=F32)


def mm_nt(left, right):
    return lax.dot_general(left, right, (((1,), (1,)), ((), ())), preferred_element_type=F32)


def mm_tn(left, right):
    return lax.dot_general(left, right, (((0,), (0,)), ((), ())), preferred_element_type=F32)


def decay_constants():
    rates = 4.0 / CH * np.exp2(-8.0 * np.arange(NS, dtype=np.float64) / (NS - 1))
    return rates, np.sqrt(-np.expm1(-2.0 * rates))


RATES, NORMS = decay_constants()


def decay_within(n, transposed):
    rows = lax.broadcasted_iota(jnp.int32, (CH, CH), 0)
    columns = lax.broadcasted_iota(jnp.int32, (CH, CH), 1)
    offset = columns - rows if transposed else rows - columns
    powers = jnp.exp(offset.astype(F32) * -float(RATES[n]))
    return jnp.where(offset >= 0, float(NORMS[n]) * powers, 0.0).astype(BF16)


def decay_vectors(rates, norms):
    steps = lax.broadcasted_iota(jnp.int32, (NS, CH), 1).astype(F32)
    carry_in = jnp.exp(-rates * (steps + 1.0))
    carry_out = (norms * jnp.exp(-rates * (CH - 1.0 - steps))).astype(BF16)
    return carry_in, carry_out, jnp.exp(-rates * CH)


def ssm_forward_kernel(v_ref, rates_ref, norms_ref, coef_ref, skip_ref, out_ref, state_ref, within_ref):
    @pl.when(pl.program_id(0) == 0)
    def _():
        for n in range(NS):
            within_ref[n] = decay_within(n, False)

    carry_in, carry_out, whole = decay_vectors(rates_ref[...], norms_ref[...])
    before = BLK // CH - 1
    state = jnp.zeros(state_ref.shape, F32)
    for k in range(before):
        state = whole * state + mm(carry_out, v_ref[k * CH : (k + 1) * CH, :])
    state_ref[...] = state
    rows = v_ref[before * CH :, :]
    total = skip_ref[...] * rows.astype(F32)
    total += lax.dot_general(
        carry_in, coef_ref[...] * state, (((0,), (0,)), ((), ())), precision=HIGHEST, preferred_element_type=F32
    )
    for n in range(NS):
        total += coef_ref[n : n + 1, :] * mm(within_ref[n], rows)
    out_ref[...] = total.astype(BF16)


def decay_arrays():
    return jnp.asarray(RATES[:, None], F32), jnp.asarray(NORMS[:, None], F32)


def ssm_forward(rows, coef, skip):
    width = rows.shape[1]
    step = 256
    column = lambda c: (0, c)
    fixed = pl.BlockSpec((NS, 1), lambda c: (0, 0))
    return pl.pallas_call(
        ssm_forward_kernel,
        grid=(width // step,),
        in_specs=[
            pl.BlockSpec((BLK, step), column),
            fixed,
            fixed,
            pl.BlockSpec((NS, step), column),
            pl.BlockSpec((1, step), column),
        ],
        out_specs=[pl.BlockSpec((CH, step), column), pl.BlockSpec((NS, step), column)],
        out_shape=[jax.ShapeDtypeStruct((CH, width), BF16), jax.ShapeDtypeStruct((NS, width), F32)],
        scratch_shapes=[pltpu.VMEM((NS, CH, CH), BF16)],
        cost_estimate=brief(31),
        name="ssm_forward",
    )(rows, *decay_arrays(), coef, skip)


def key_parts(block, tile, k_ref, v_ref, ck_ref, cv_ref):
    parts = []
    if block > 0:
        parts.append((None, ck_ref[0], cv_ref[0], False))
    for piece in range(tile + 1):
        where = slice(block * BLK + piece * TILE, block * BLK + (piece + 1) * TILE)
        parts.append((piece, k_ref[0, where, :], v_ref[0, where, :], piece == tile))
    return parts


def tile_scores(keys, query, masked):
    scores = mm_nt(keys, query)
    if masked:
        key_ids = lax.broadcasted_iota(jnp.int32, scores.shape, 0)
        query_ids = lax.broadcasted_iota(jnp.int32, scores.shape, 1)
        scores = jnp.where(key_ids <= query_ids, scores, -1e30)
    return scores


def attend_forward_kernel(q_ref, k_ref, v_ref, ck_ref, cv_ref, out_ref, lse_ref):
    for block in range(2):
        for tile in range(BLK // TILE):
            base = block * BLK + tile * TILE
            query = q_ref[0, base : base + TILE, :]
            parts = key_parts(block, tile, k_ref, v_ref, ck_ref, cv_ref)
            scores = [tile_scores(keys, query, masked) for _, keys, _, masked in parts]
            top = functools.reduce(jnp.maximum, [jnp.max(s, axis=0, keepdims=True) for s in scores]) * LOG2
            exps = [jnp.exp2(s * LOG2 - top) for s in scores]
            total = functools.reduce(jnp.add, [jnp.sum(e, axis=0, keepdims=True) for e in exps])
            out = functools.reduce(
                jnp.add, [mm_tn(values, e.astype(BF16)) for (_, _, values, _), e in zip(parts, exps)]
            )
            out_ref[base : base + TILE, :] = (out * (1.0 / total)).T.astype(BF16)
            lse_ref[0, :, base : base + TILE] = top + jnp.log2(total)


def attend_forward(qkv, ckv):
    length, width = qkv.shape[1], qkv.shape[2]
    heads = width // HD
    pick = lambda s: pl.BlockSpec((1, length, HD), lambda h: (s, 0, h))
    pick_context = lambda s: pl.BlockSpec((1, CTX, HD), lambda h: (s, 0, h))
    return pl.pallas_call(
        attend_forward_kernel,
        grid=(heads,),
        in_specs=[pick(0), pick(1), pick(2), pick_context(0), pick_context(1)],
        out_specs=[
            pl.BlockSpec((length, HD), lambda h: (0, h)),
            pl.BlockSpec((1, 1, length), lambda h: (h, 0, 0)),
        ],
        out_shape=[
            jax.ShapeDtypeStruct((length, width), BF16),
            jax.ShapeDtypeStruct((heads, 1, length), F32),
        ],
        cost_estimate=brief(31),
        name="attend_forward",
    )(qkv, qkv, qkv, ckv, ckv)


def attend_backward_kernel(q_ref, k_ref, v_ref, ck_ref, cv_ref, dout_ref, lse_ref, grad_ref, cgrad_ref):
    for block in range(2):
        grads = {}
        for tile in range(BLK // TILE):
            base = block * BLK + tile * TILE
            query = q_ref[0, base : base + TILE, :]
            dout = dout_ref[0, base : base + TILE, :]
            lse = lse_ref[0, :, base : base + TILE]
            parts = key_parts(block, tile, k_ref, v_ref, ck_ref, cv_ref)
            probs = [jnp.exp2(tile_scores(keys, query, masked) * LOG2 - lse) for _, keys, _, masked in parts]
            dprobs = [mm_nt(values, dout) for _, _, values, _ in parts]
            inner = functools.reduce(
                jnp.add, [jnp.sum(p * d, axis=0, keepdims=True) for p, d in zip(probs, dprobs)]
            )
            dquery = None
            for (name, keys, _, _), p, d in zip(parts, probs, dprobs):
                dscore = (p * (d - inner)).astype(BF16)
                term = mm_tn(keys, dscore)
                dquery = term if dquery is None else dquery + term
                dkey, dvalue = mm(dscore, query), mm(p.astype(BF16), dout)
                if name in grads:
                    grads[name] = (grads[name][0] + dkey, grads[name][1] + dvalue)
                else:
                    grads[name] = (dkey, dvalue)
            grad_ref[0, base : base + TILE, :] = (dquery.T * SCALE).astype(BF16)
        for name, (dkey, dvalue) in grads.items():
            dkey, dvalue = (dkey * SCALE).astype(BF16), dvalue.astype(BF16)
            if name is None:
                cgrad_ref[0] = dkey
                cgrad_ref[1] = dvalue
            else:
                where = slice(block * BLK + name * TILE, block * BLK + (name + 1) * TILE)
                grad_ref[1, where, :] = dkey
                grad_ref[2, where, :] = dvalue


def attend_backward(qkv, ckv, dheads, side, lse):
    length, width = qkv.shape[1], qkv.shape[2]
    heads = width // HD
    pick = lambda s: pl.BlockSpec((1, length, HD), lambda h: (s, 0, h))
    pick_context = lambda s: pl.BlockSpec((1, CTX, HD), lambda h: (s, 0, h))
    return pl.pallas_call(
        attend_backward_kernel,
        grid=(heads,),
        in_specs=[
            pick(0),
            pick(1),
            pick(2),
            pick_context(0),
            pick_context(1),
            pl.BlockSpec((1, length, HD), lambda h: (side, 0, h)),
            pl.BlockSpec((1, 1, length), lambda h: (h, 0, 0)),
        ],
        out_specs=[
            pl.BlockSpec((3, length, HD), lambda h: (0, 0, h)),
            pl.BlockSpec((2, CTX, HD), lambda h: (0, 0, h)),
        ],
        out_shape=[
            jax.ShapeDtypeStruct((3, length, width), BF16),
            jax.ShapeDtypeStruct((2, CTX, width), BF16),
        ],
        cost_estimate=brief(),
        name="attend_backward",
    )(qkv, qkv, qkv, ckv, ckv, dheads, lse)


def brief(power=32):
    return pl.CostEstimate(flops=1 << power, bytes_accessed=1 << 16, transcendentals=0)


def roomy():
    return pltpu.CompilerParams(vmem_limit_bytes=56 << 20)


def place_rows(where_ref, tall_ref, out_ref, count):
    size = tall_ref.shape[0] // count
    core = where_ref[1] & 1
    for p in range(count):
        start = pl.multiple_of((p % (count // 2) * 2 + (core ^ (p // (count // 2)))) * size, size)
        out_ref[p * size : (p + 1) * size, :] = tall_ref[pl.ds(start, size), :]


def whole_block(shape):
    return pl.BlockSpec(shape, lambda *_: (0,) * len(shape), pipeline_mode=pl.Buffered(1))


def normalize(values):
    center = values - jnp.mean(values, axis=-1, keepdims=True)
    rstd = lax.rsqrt(jnp.mean(center * center, axis=-1, keepdims=True) + EPS)
    return center * rstd, rstd


def normalize_backward(grad, hat, rstd, gain):
    dn = grad * gain
    return rstd * (dn - jnp.mean(dn, axis=-1, keepdims=True) - hat * jnp.mean(dn * hat, axis=-1, keepdims=True))


def turn_rows(where, values, count):
    length, width = values.shape[2:]
    step = 256

    def kernel(where_ref, x_ref, out_ref, tall):
        tall[...] = x_ref[0, 0].T
        place_rows(where_ref, tall, out_ref, count)

    return pl.pallas_call(
        kernel,
        grid_spec=pltpu.PrefetchScalarGridSpec(
            num_scalar_prefetch=1,
            grid=(length // step,),
            in_specs=[pl.BlockSpec((1, 1, step, width), lambda i, w: (w[0], 0, i, 0))],
            out_specs=pl.BlockSpec((width, step), lambda i, w: (0, i)),
            scratch_shapes=[pltpu.VMEM((width, step), BF16)],
        ),
        out_shape=jax.ShapeDtypeStruct((width, length), BF16),
        cost_estimate=brief(),
        name="turn_rows",
    )(where, values)


def first_norm(where, layer_in, gain, bias, count):
    length, width = layer_in.shape[2:]
    step = 256

    def kernel(where_ref, x_ref, gain_ref, bias_ref, u_ref, ut_ref, tall):
        hat, _ = normalize(x_ref[0, 0].astype(F32))
        u = (hat * gain_ref[...] + bias_ref[...]).astype(BF16)
        u_ref[...] = u
        tall[...] = u.T
        place_rows(where_ref, tall, ut_ref, count)

    return pl.pallas_call(
        kernel,
        grid_spec=pltpu.PrefetchScalarGridSpec(
            num_scalar_prefetch=1,
            grid=(length // step,),
            in_specs=[
                pl.BlockSpec((1, 1, step, width), lambda i, w: (w[0], 0, i, 0)),
                whole_block((1, width)),
                whole_block((1, width)),
            ],
            out_specs=[
                pl.BlockSpec((step, width), lambda i, w: (i, 0)),
                pl.BlockSpec((width, step), lambda i, w: (0, i)),
            ],
            scratch_shapes=[pltpu.VMEM((width, step), BF16)],
        ),
        out_shape=[
            jax.ShapeDtypeStruct((length, width), BF16),
            jax.ShapeDtypeStruct((width, length), BF16),
        ],
        cost_estimate=brief(),
        name="first_norm",
    )(where, layer_in, gain, bias)


def context_rows(where, context, count):
    def kernel(where_ref, c_ref, out_ref, tall):
        tall[...] = c_ref[...].T
        place_rows(where_ref, tall, out_ref, count)

    rows, width = context.shape
    return pl.pallas_call(
        kernel,
        in_specs=[pl.BlockSpec(memory_space=pltpu.SMEM), pl.BlockSpec(memory_space=pltpu.VMEM)],
        out_specs=pl.BlockSpec(memory_space=pltpu.VMEM),
        out_shape=jax.ShapeDtypeStruct((width, rows), BF16),
        scratch_shapes=[pltpu.VMEM((width, rows), BF16)],
        cost_estimate=brief(31),
        name="context_rows",
    )(where, context)


def project(u1, context, weights):
    length, width = u1.shape
    rows = context.shape[0]
    sizes = [w.shape[2] for w in weights]
    group = sum(sizes)

    def kernel(u_ref, c_ref, *refs):
        qkv_ref, ckv_ref, weight_s = refs[len(weights) :]
        start = 0
        for ref, size in zip(refs, sizes):
            weight_s[:, start : start + size] = ref[0]
            start += size
        for part in chunks(length):
            qkv_ref[0, part, :] = mm(u_ref[part, :], weight_s[...]).astype(BF16)

        @pl.when(pl.program_id(0) > 0)
        def _():
            ckv_ref[0] = mm(c_ref[...], weight_s[...]).astype(BF16)

    return pl.pallas_call(
        kernel,
        grid=(3,),
        in_specs=[whole_block((length, width)), whole_block((rows, width))]
        + [pl.BlockSpec((1, width, size), lambda s: (s, 0, 0)) for size in sizes],
        out_specs=[
            pl.BlockSpec((1, length, group), lambda s: (s, 0, 0)),
            pl.BlockSpec((1, rows, group), lambda s: (jnp.maximum(s - 1, 0), 0, 0)),
        ],
        out_shape=[
            jax.ShapeDtypeStruct((3, length, group), BF16),
            jax.ShapeDtypeStruct((2, rows, group), BF16),
        ],
        scratch_shapes=[pltpu.VMEM((width, group), BF16)],
        compiler_params=roomy(),
        cost_estimate=brief(31),
        name="project",
    )(u1, context, *weights)


def attention_out(where, layer_in, heads_own, heads_other, out_own, out_first, out_second, gain, bias, count):
    length, width = layer_in.shape[2:]
    group = heads_own.shape[1]
    half = group // 2
    step = 256

    def kernel(where_ref, x_ref, ho_ref, ht_ref, wo_ref, w1_ref, w2_ref, gain_ref, bias_ref, x1_ref, u_ref, ut_ref, tall):
        x1 = x_ref[0, 0].astype(F32) + mm(ho_ref[...], wo_ref[...])
        x1 += mm(ht_ref[:, :half], w1_ref[...]) + mm(ht_ref[:, half:], w2_ref[...])
        x1_ref[...] = x1
        hat, _ = normalize(x1)
        u = (hat * gain_ref[...] + bias_ref[...]).astype(BF16)
        u_ref[...] = u
        tall[...] = u.T
        place_rows(where_ref, tall, ut_ref, count)

    row = lambda i, w: (i, 0)
    return pl.pallas_call(
        kernel,
        grid_spec=pltpu.PrefetchScalarGridSpec(
            num_scalar_prefetch=1,
            grid=(length // step,),
            in_specs=[
                pl.BlockSpec((1, 1, step, width), lambda i, w: (w[0], 0, i, 0)),
                pl.BlockSpec((step, group), row),
                pl.BlockSpec((step, group), row),
                whole_block((group, width)),
                whole_block((half, width)),
                whole_block((half, width)),
                whole_block((1, width)),
                whole_block((1, width)),
            ],
            out_specs=[
                pl.BlockSpec((step, width), row),
                pl.BlockSpec((step, width), row),
                pl.BlockSpec((width, step), lambda i, w: (0, i)),
            ],
            scratch_shapes=[pltpu.VMEM((width, step), BF16)],
        ),
        out_shape=[
            jax.ShapeDtypeStruct((length, width), F32),
            jax.ShapeDtypeStruct((length, width), BF16),
            jax.ShapeDtypeStruct((width, length), BF16),
        ],
        compiler_params=roomy(),
        cost_estimate=brief(),
        name="attention_out",
    )(where, layer_in, heads_own, heads_other, out_own, out_first, out_second, gain, bias)


TALL = 256
STEP = 512


def chunks(length):
    return [slice(i, i + TALL) for i in range(0, length, TALL)]


def gelu_pair(pre):
    root = math.sqrt(2.0 / math.pi)
    straight = root * pre
    inner = straight * (1.0 + 0.044715 * (pre * pre))
    bend = jnp.tanh(inner)
    lean = 1.5 * inner - straight
    half = 0.5 * pre
    hid = half + half * bend
    slope = (0.5 + lean) + bend * (0.5 - lean * bend)
    return hid.astype(BF16), slope.astype(BF16)


def hidden_forward(u2, dy_rows, up, before):
    length, width = u2.shape
    half = width // 2
    gathered = up.ndim == 4
    steps = 2 * width // STEP
    first = 0 if before is None else steps

    def kernel(u_ref, dy_ref, up_ref, *refs):
        hid_ref, slope_ref, sent_ref, kept_ref = refs[-4:]
        weight = up_ref[...].reshape(width, STEP)
        for rows in chunks(length):
            hid, slope = gelu_pair(mm(u_ref[rows, :], weight))
            hid_ref[rows, :] = hid
            slope_ref[rows, :] = slope
        hid = hid_ref[...]
        for rows in chunks(half):
            sent_ref[rows, :] = mm(dy_ref[half + rows.start : half + rows.stop, :], hid).astype(BF16)
        for rows in chunks(half):
            kept_ref[rows, :] = mm(dy_ref[rows, :], hid).astype(BF16)

    if gathered:
        up_spec = pl.BlockSpec((up.shape[0], 1, up.shape[2], STEP), lambda j: (0, j // 2, 0, lax.rem(j, 2)))
    else:
        up_spec = pl.BlockSpec((width, STEP), lambda j: (0, j))
    tile = pl.BlockSpec((length, STEP), lambda j: (0, first + j))
    part = pl.BlockSpec((half, STEP), lambda j: (0, j))
    wide = jax.ShapeDtypeStruct((length, 2 * steps * STEP), BF16)
    return pl.pallas_call(
        kernel,
        grid=(steps,),
        in_specs=[whole_block((length, width)), whole_block((width, length)), up_spec]
        + ([] if before is None else [pl.BlockSpec(memory_space=pl.ANY)] * 2),
        out_specs=[tile, tile, part, part],
        out_shape=[wide, wide] + [jax.ShapeDtypeStruct((half, steps * STEP), BF16)] * 2,
        input_output_aliases={} if before is None else {3: 0, 4: 1},
        compiler_params=roomy(),
        cost_estimate=brief(37),
        name="hidden_forward",
    )(u2, dy_rows, up, *(before or ()))


def hidden_backward(where, cotangent, hid, slope, down_own, buffer, u2_rows, x1):
    length, width = x1.shape
    half = width // 2
    pieces, _, rows_each, _ = buffer.shape
    side = 2 * width // STEP
    steps = 2 * side

    def kernel(
        where_ref, dy_ref, hid_ref, slope_ref, down_ref, down2_ref, ut_ref, x1_ref,
        layer_ref, dpre_ref, sent_ref, kept_ref,
        down_s, mix_s, x1_s, sem,
    ):
        j = pl.program_id(0)
        fetch = pltpu.make_async_copy(x1_ref, x1_s, sem)

        @pl.when(j == 0)
        def _():
            fetch.start()
            mix_s[...] = jnp.zeros_like(mix_s)

        @pl.when(j < side)
        def _():
            down_s[...] = down_ref[...]

        @pl.when(j >= side)
        def _():
            down_s[...] = down2_ref[...].reshape(STEP, width)

        for rows in chunks(length):
            dhid = mm_nt(dy_ref[0, 0, rows, :], down_s[...])
            dpre_ref[rows, :] = (dhid * slope_ref[rows, :].astype(F32)).astype(BF16)
        for rows in chunks(length):
            mix_s[rows, :] += mm(hid_ref[rows, :], down_s[...])
        dpre = dpre_ref[...]
        for rows in chunks(half):
            sent_ref[rows, :] = mm(ut_ref[half + rows.start : half + rows.stop, :], dpre).astype(BF16)
        for rows in chunks(half):
            kept_ref[rows, :] = mm(ut_ref[rows, :], dpre).astype(BF16)

        @pl.when(j == steps - 1)
        def _():
            fetch.wait()
            for rows in chunks(length):
                layer_ref[rows, :] = (x1_s[rows, :] + mix_s[rows, :]).astype(BF16)

    low = lambda j: jnp.minimum(j, side - 1)
    high = lambda j: jnp.maximum(j - side, 0)
    tile = pl.BlockSpec((length, STEP), lambda j, w: (0, j))
    part = pl.BlockSpec((half, STEP), lambda j, w: (0, j))
    return pl.pallas_call(
        kernel,
        grid_spec=pltpu.PrefetchScalarGridSpec(
            num_scalar_prefetch=1,
            grid=(steps,),
            in_specs=[
                pl.BlockSpec((1, 1, length, width), lambda j, w: (w[0], 0, 0, 0), pipeline_mode=pl.Buffered(1)),
                tile,
                tile,
                pl.BlockSpec((STEP, width), lambda j, w: (low(j), 0)),
                pl.BlockSpec((pieces // side, 2, rows_each, width), lambda j, w: (high(j), 1, 0, 0)),
                whole_block((width, length)),
                pl.BlockSpec(memory_space=pl.ANY),
            ],
            out_specs=[whole_block((length, width)), tile, part, part],
            scratch_shapes=[
                pltpu.VMEM((STEP, width), BF16),
                pltpu.VMEM((length, width), F32),
                pltpu.VMEM((length, width), F32),
                pltpu.SemaphoreType.DMA,
            ],
        ),
        out_shape=[
            jax.ShapeDtypeStruct((length, width), BF16),
            jax.ShapeDtypeStruct((length, steps * STEP), BF16),
            jax.ShapeDtypeStruct((half, steps * STEP), BF16),
            jax.ShapeDtypeStruct((half, steps * STEP), BF16),
        ],
        compiler_params=roomy(),
        cost_estimate=brief(),
        name="hidden_backward",
    )(where, cotangent, hid, slope, down_own, buffer, u2_rows, x1)


def second_norm_backward(where, cotangent, dpre, up_own, buffer, x1, gain, out_own, out_first, out_second, count):
    length, width = x1.shape
    group = out_own.shape[0]
    pieces, _, rows_each, _ = buffer.shape
    side = 2
    tiles = 2 * side
    steps = tiles + 2
    chunk = 128

    def kernel(
        where_ref, dpre_ref, up_ref, up2_ref, dy_ref, x1_ref, gain_ref, wo_ref, w1_ref, w2_ref,
        dattn_ref, turned_ref, dheads_ref, sums_ref,
        up_s, out_s, grad_s, tall, dy_s, x1_s, sems,
    ):
        j = pl.program_id(0)
        fetches = [
            pltpu.make_async_copy(x1_ref, x1_s, sems.at[0]),
            pltpu.make_async_copy(dy_ref.at[where_ref[0], 0], dy_s, sems.at[1]),
            pltpu.make_async_copy(wo_ref, out_s.at[0], sems.at[2]),
            pltpu.make_async_copy(w1_ref, out_s.at[1, pl.ds(0, group // 2)], sems.at[3]),
            pltpu.make_async_copy(w2_ref, out_s.at[1, pl.ds(group // 2, group // 2)], sems.at[4]),
        ]

        @pl.when(j == 0)
        def _():
            for fetch in fetches:
                fetch.start()
            grad_s[...] = jnp.zeros_like(grad_s)
            sums_ref[...] = jnp.zeros_like(sums_ref)

        @pl.when(j < side)
        def _():
            up_s[...] = up_ref[...]

        @pl.when(jnp.logical_and(j >= side, j < tiles))
        def _():
            up_s[...] = up2_ref[...].reshape(width, width)

        @pl.when(j < tiles)
        def _():
            for rows in chunks(length):
                grad_s[rows, :] += mm_nt(dpre_ref[rows, :], up_s[...])

        @pl.when(j == tiles - 1)
        def _():
            for fetch in fetches:
                fetch.wait()

            @pl.loop(0, length // chunk)
            def _(i):
                rows = pl.ds(pl.multiple_of(i * chunk, chunk), chunk)
                du = grad_s[rows, :]
                hat, rstd = normalize(x1_s[rows, :])
                sums_ref[0:1, :] += jnp.sum(du * hat, axis=0, keepdims=True)
                sums_ref[1:2, :] += jnp.sum(du, axis=0, keepdims=True)
                out = dy_s[rows, :].astype(F32) + normalize_backward(du, hat, rstd, gain_ref[...])
                out = out.astype(BF16)
                dattn_ref[rows, :] = out
                tall[:, rows] = out.T

            place_rows(where_ref, tall, turned_ref, count)

        @pl.when(j >= tiles)
        def _():
            for rows in chunks(length):
                dheads_ref[0, rows, :] = mm_nt(dattn_ref[rows, :], out_s[j - tiles]).astype(BF16)

    low = lambda j: jnp.minimum(j, side - 1)
    high = lambda j: jnp.clip(j - side, 0, side - 1)
    return pl.pallas_call(
        kernel,
        grid_spec=pltpu.PrefetchScalarGridSpec(
            num_scalar_prefetch=1,
            grid=(steps,),
            in_specs=[
                pl.BlockSpec((length, width), lambda j, w: (0, jnp.minimum(j, tiles - 1))),
                pl.BlockSpec((width, width), lambda j, w: (0, low(j))),
                pl.BlockSpec((pieces, 1, rows_each, width), lambda j, w: (0, high(j), 0, 0)),
                pl.BlockSpec(memory_space=pl.ANY),
                pl.BlockSpec(memory_space=pl.ANY),
                whole_block((1, width)),
                pl.BlockSpec(memory_space=pl.ANY),
                pl.BlockSpec(memory_space=pl.ANY),
                pl.BlockSpec(memory_space=pl.ANY),
            ],
            out_specs=[
                whole_block((length, width)),
                whole_block((width, length)),
                pl.BlockSpec((1, length, group), lambda j, w: (jnp.maximum(j - tiles, 0), 0, 0)),
                whole_block((2, width)),
            ],
            scratch_shapes=[
                pltpu.VMEM((width, width), BF16),
                pltpu.VMEM((2, group, width), BF16),
                pltpu.VMEM((length, width), F32),
                pltpu.VMEM((width, length), BF16),
                pltpu.VMEM((length, width), BF16),
                pltpu.VMEM((length, width), F32),
                pltpu.SemaphoreType.DMA((5,)),
            ],
        ),
        out_shape=[
            jax.ShapeDtypeStruct((length, width), BF16),
            jax.ShapeDtypeStruct((width, length), BF16),
            jax.ShapeDtypeStruct((2, length, group), BF16),
            jax.ShapeDtypeStruct((2, width), F32),
        ],
        compiler_params=roomy(),
        cost_estimate=brief(),
        name="second_norm_backward",
    )(where, dpre, up_own, buffer, cotangent, x1, gain, out_own, out_first, out_second)


def projection_rows(u1_rows, context_turned, dqkv, dckv, dattn_rows, heads):
    width, length = u1_rows.shape
    half = width // 2
    group = heads.shape[1]

    def kernel(ut_ref, cut_ref, grad_ref, cgrad_ref, dt_ref, heads_ref, kept_ref, *refs):
        sent_refs, (dt_s, heads_s, sems) = refs[:4], refs[4:]
        s = pl.program_id(0)
        fetches = [
            pltpu.make_async_copy(dt_ref, dt_s, sems.at[0]),
            pltpu.make_async_copy(heads_ref, heads_s, sems.at[1]),
        ]

        @pl.when(s == 0)
        def _():
            for fetch in fetches:
                fetch.start()

        def emit(product):
            for rows in chunks(half):
                kept_ref[rows, :] = product(rows.start).astype(BF16)
            for rows in chunks(half):
                sent = product(half + rows.start).astype(BF16)
                for k, ref in enumerate(sent_refs):

                    @pl.when(s == k)
                    def _(ref=ref, rows=rows, sent=sent):
                        ref[rows, :] = sent

        @pl.when(s < 3)
        def _():
            grad = grad_ref[0]
            cgrad = jnp.where(s > 0, cgrad_ref[0], jnp.zeros_like(cgrad_ref[0]))

            def product(start):
                here = slice(start, start + TALL)
                return mm(ut_ref[here, :], grad) + mm(cut_ref[here, :], cgrad)

            emit(product)

        @pl.when(s == 3)
        def _():
            for fetch in fetches:
                fetch.wait()
            heads = heads_s[...]
            emit(lambda start: mm(dt_s[start : start + TALL, :], heads))

    part = pl.BlockSpec((half, group), lambda s: (0, s))
    return pl.pallas_call(
        kernel,
        grid=(4,),
        in_specs=[
            whole_block((width, length)),
            whole_block((width, CTX)),
            pl.BlockSpec((1, length, group), lambda s: (jnp.minimum(s, 2), 0, 0)),
            pl.BlockSpec((1, CTX, group), lambda s: (jnp.clip(s - 1, 0, 1), 0, 0)),
            pl.BlockSpec(memory_space=pl.ANY),
            pl.BlockSpec(memory_space=pl.ANY),
        ],
        out_specs=[part] + [whole_block((half, group))] * 4,
        out_shape=[jax.ShapeDtypeStruct((half, 4 * group), BF16)]
        + [jax.ShapeDtypeStruct((half, group), BF16)] * 4,
        scratch_shapes=[
            pltpu.VMEM((width, length), BF16),
            pltpu.VMEM((length, group), BF16),
            pltpu.SemaphoreType.DMA((2,)),
        ],
        compiler_params=roomy(),
        cost_estimate=brief(),
        name="projection_rows",
    )(u1_rows, context_turned, dqkv, dckv, dattn_rows, heads)


def inputs_backward(part, where, dsides, qkv_own, qkv_first, qkv_second, u1, coef, skip, state, layer_in, dattn, gain):
    length, width = layer_in.shape[2] // 2, layer_in.shape[3]
    group = qkv_own.shape[2]
    steps = 6
    chunk = 128
    before = BLK // CH - 1

    def kernel(
        where_ref, do_ref, dt_ref, co_ref, ct_ref, own_ref, w1_ref, w2_ref, v_ref, rates_ref,
        norms_ref, coef_ref, skip_ref, state_ref, x_ref, dx_ref, gain_ref,
        out_ref, sums_ref, *rest,
    ):
        grad_s, cgrad_s, weight_s, total, ctotal, within = rest[-6:]
        small_ref = rest[0]
        j = pl.program_id(0)

        @pl.when(j == 0)
        def _():
            total[...] = jnp.zeros_like(total)
            ctotal[...] = jnp.zeros_like(ctotal)
            sums_ref[...] = jnp.zeros_like(sums_ref)
            if part == 0:
                for n in range(NS):
                    within[n] = decay_within(n, True)

        @pl.when(j < 3)
        def _():
            grad_s[...] = do_ref[0]
            cgrad_s[...] = co_ref[0]
            weight_s[...] = own_ref[0]

        @pl.when(j >= 3)
        def _():
            grad_s[...] = dt_ref[0]
            cgrad_s[...] = ct_ref[0]
            weight_s[:, : group // 2] = w1_ref[0]
            weight_s[:, group // 2 :] = w2_ref[0]

        @pl.when(lax.rem(j, 3) == 0)
        def _():
            cgrad_s[...] = jnp.zeros_like(cgrad_s)

        for rows in chunks(length):
            total[rows, :] += mm_nt(grad_s[rows, :], weight_s[...])
        if part == 0:
            ctotal[...] += mm_nt(cgrad_s[...], weight_s[...])

        def state_space():
            carry_in, carry_out, whole = decay_vectors(rates_ref[...], norms_ref[...])

            @pl.loop(0, width // 256)
            def _(c):
                here = pl.ds(pl.multiple_of(c * 256, 256), 256)
                rows = v_ref[:, here].astype(F32)
                grad = ctotal[:, here].astype(BF16)
                wide = grad.astype(F32)
                du = skip_ref[:, here] * wide
                reach = jnp.dot(carry_in, wide, precision=HIGHEST, preferred_element_type=F32)
                for n in range(NS):
                    back = mm(within[n], grad)
                    du += coef_ref[n : n + 1, here] * back
                    small_ref[n : n + 1, here] = (
                        jnp.sum(rows * back, axis=0, keepdims=True) + state_ref[n : n + 1, here] * reach[n : n + 1, :]
                    )
                small_ref[NS : NS + 1, here] = jnp.sum(rows * wide, axis=0, keepdims=True)
                total[before * CH : (before + 1) * CH, here] += du
                carried = coef_ref[:, here] * reach
                for k in reversed(range(before)):
                    total[k * CH : (k + 1) * CH, here] += lax.dot_general(
                        carry_out.astype(F32),
                        carried,
                        (((0,), (0,)), ((), ())),
                        precision=HIGHEST,
                        preferred_element_type=F32,
                    )
                    carried = whole * carried

        @pl.when(j == steps - 1)
        def _():
            if part == 0:
                state_space()

            @pl.loop(0, length // chunk)
            def _(i):
                rows = pl.ds(pl.multiple_of(i * chunk, chunk), chunk)
                du = total[rows, :]
                hat, rstd = normalize(x_ref[0, 0, rows, :].astype(F32))
                sums_ref[0:1, :] += jnp.sum(du * hat, axis=0, keepdims=True)
                sums_ref[1:2, :] += jnp.sum(du, axis=0, keepdims=True)
                out = dx_ref[rows, :].astype(F32) + normalize_backward(du, hat, rstd, gain_ref[...])
                out_ref[rows, :] = out.astype(BF16)

    low = lambda j: jnp.minimum(j, 2)
    high = lambda j: jnp.maximum(j - 3, 0)
    back = lambda s: jnp.maximum(s - 1, 0)
    mine = pl.BlockSpec((1, 1, length, width), lambda j, w: (w[0], 0, part, 0), pipeline_mode=pl.Buffered(1))
    (dqkv_own, dckv_own), (dqkv_other, dckv_other) = dsides
    return pl.pallas_call(
        kernel,
        grid_spec=pltpu.PrefetchScalarGridSpec(
            num_scalar_prefetch=1,
            grid=(steps,),
            in_specs=[
                pl.BlockSpec((1, length, group), lambda j, w: (low(j), part, 0)),
                pl.BlockSpec((1, length, group), lambda j, w: (high(j), part, 0)),
                pl.BlockSpec((1, CTX, group), lambda j, w: (back(low(j)), 0, 0)),
                pl.BlockSpec((1, CTX, group), lambda j, w: (back(high(j)), 0, 0)),
                pl.BlockSpec((1, width, group), lambda j, w: (low(j), 0, 0)),
                pl.BlockSpec((1, width, group // 2), lambda j, w: (high(j), 0, 0)),
                pl.BlockSpec((1, width, group // 2), lambda j, w: (high(j), 0, 0)),
                pl.BlockSpec((CH, width), lambda j, w: (before, 0)),
                whole_block((NS, 1)),
                whole_block((NS, 1)),
                whole_block((NS, width)),
                whole_block((1, width)),
                whole_block((NS, width)),
                mine,
                pl.BlockSpec((length, width), lambda j, w: (part, 0), pipeline_mode=pl.Buffered(1)),
                whole_block((1, width)),
            ],
            out_specs=[
                whole_block((length, width)),
                whole_block((2, width)),
                *([whole_block((NS + 1, width))] if part == 0 else []),
            ],
            scratch_shapes=[
                pltpu.VMEM((length, group), BF16),
                pltpu.VMEM((CTX, group), BF16),
                pltpu.VMEM((width, group), BF16),
                pltpu.VMEM((length, width), F32),
                pltpu.VMEM((CTX, width), F32),
                pltpu.VMEM((NS, CH, CH), BF16),
            ],
        ),
        out_shape=[
            jax.ShapeDtypeStruct((length, width), BF16),
            jax.ShapeDtypeStruct((2, width), F32),
            *([jax.ShapeDtypeStruct((NS + 1, width), F32)] if part == 0 else []),
        ],
        compiler_params=roomy(),
        cost_estimate=brief(),
        name="inputs_backward",
    )(
        where, dqkv_own, dqkv_other, dckv_own, dckv_other, qkv_own, qkv_first, qkv_second,
        u1, *decay_arrays(), coef, skip, state, layer_in, dattn, gain,
    )


def join(where, kept, got, swap, above, below, bit, power=32):
    rows, columns = kept.shape
    pieces = list(got) if isinstance(got, (list, tuple)) else [got]
    width = columns // len(pieces) if len(pieces) > 1 else 2 * STEP
    shape = (above, 2, below)

    def kernel(where_ref, kept_ref, *refs):
        keep_ref, send_ref = refs[-2:]
        mine = (where_ref[1] >> bit) & 1

        def emit(got_ref):
            for out_ref, index in ((keep_ref, mine), (send_ref, 1 - mine)):
                come = got_ref[:, pl.ds(index, 1)][:, 0].astype(F32)
                if swap:
                    come = jnp.concatenate([come[..., width // 2 :], come[..., : width // 2]], axis=-1)
                out_ref[...] = (kept_ref[:, pl.ds(index, 1)][:, 0].astype(F32) + come).astype(BF16)

        if len(pieces) == 1:
            emit(refs[0])
        else:
            for k in range(len(pieces)):

                @pl.when(pl.program_id(0) == k)
                def _(ref=refs[k]):
                    emit(ref)

    tile = pl.BlockSpec((above, 2, below, width), lambda j, w: (0, 0, 0, j))
    out = pl.BlockSpec((above, below, width), lambda j, w: (0, 0, j))
    many = [tile] if len(pieces) == 1 else [whole_block((*shape, width))] * len(pieces)
    keep, send = pl.pallas_call(
        kernel,
        grid_spec=pltpu.PrefetchScalarGridSpec(
            num_scalar_prefetch=1, grid=(columns // width,), in_specs=[tile, *many], out_specs=[out, out]
        ),
        out_shape=[jax.ShapeDtypeStruct((above, below, columns), BF16)] * 2,
        compiler_params=roomy(),
        cost_estimate=brief(power),
        name="join",
    )(where, kept.reshape(*shape, columns), *[piece.reshape(*shape, -1) for piece in pieces])
    return keep.reshape(rows // 2, columns), send.reshape(rows // 2, columns)


def add_pairs(where, *pairs, power=37):
    rows, columns = pairs[0][0].shape
    width = min(columns, 4 * STEP)
    tiles = columns // width

    def kernel(where_ref, *refs):
        out_ref = refs[-1]
        for k in range(len(pairs)):

            @pl.when(pl.program_id(0) // tiles == k)
            def _(left=refs[2 * k], right=refs[2 * k + 1]):
                out_ref[...] = (left[...].astype(F32) + right[...].astype(F32)).astype(BF16)

    def spec(k):
        return pl.BlockSpec((rows, width), lambda j, w: (0, jnp.clip(j - k * tiles, 0, tiles - 1)))

    return pl.pallas_call(
        kernel,
        grid_spec=pltpu.PrefetchScalarGridSpec(
            num_scalar_prefetch=1,
            grid=(len(pairs) * tiles,),
            in_specs=[spec(k) for k in range(len(pairs)) for _ in range(2)],
            out_specs=pl.BlockSpec((rows, width), lambda j, w: (0, j)),
        ),
        out_shape=jax.ShapeDtypeStruct((rows, len(pairs) * columns), BF16),
        cost_estimate=brief(power),
        name="add_pairs",
    )(where, *[value for pair in pairs for value in pair])


def both_parts(where, own, come, kind, power):
    step = min(piece.shape[0] for piece in own + come)
    width = own[0].shape[1]
    steps = sum(piece.shape[0] for piece in own) // step
    def kernel(where_ref, *refs):
        out_ref = refs[-1]
        here = pl.program_id(0) == where_ref[0]
        for side, pieces in enumerate((refs[: len(own)], refs[len(own) : -1])):
            mine = jnp.logical_not(here) if side else here
            at = 0
            for ref in pieces:
                for start in range(0, ref.shape[0], step):

                    @pl.when(mine & (pl.program_id(1) == at))
                    def _(ref=ref, start=start):
                        out_ref[0, 0] = ref[start : start + step, :].astype(kind)

                    at += 1

    return pl.pallas_call(
        kernel,
        grid_spec=pltpu.PrefetchScalarGridSpec(
            num_scalar_prefetch=1,
            grid=(2, steps),
            in_specs=[whole_block(piece.shape) for piece in own + come],
            out_specs=pl.BlockSpec((1, 1, step, width), lambda m, i, w: (m, 0, i, 0)),
        ),
        out_shape=jax.ShapeDtypeStruct((2, 1, steps * step, width), kind),
        compiler_params=roomy(),
        cost_estimate=brief(power),
        name="both_parts",
    )(where, *own, *come)


def swap_halves(values, width):
    half = width // 2
    order = [start + half * k for start in range(0, values.shape[1], width) for k in (1, 0)]
    return jnp.concatenate([values[:, i : i + half] for i in order], axis=1)


def shards(
    dp_count,
    layer_in,
    ln1_gain,
    ln1_bias,
    qkv_weight,
    out_weight,
    ssm_coef,
    ssm_skip,
    ln2_gain,
    ln2_bias,
    up_weight,
    down_weight,
    cotangent,
):
    width = layer_in.shape[3]
    group = qkv_weight.shape[2]
    mine = lax.axis_index("tensor")
    place = lax.axis_index("dp")
    where = jnp.stack([mine, place]).astype(jnp.int32)
    rows_each = width // dp_count
    gain1, bias1, gain2, bias2 = ln1_gain[None], ln1_bias[None], ln2_gain[None], ln2_bias[None]

    over_x = lambda v: swap(v, "tensor", 1, 2)
    over = lambda v, bit: swap(v, "dp", 1 << bit, dp_count)
    core = place & 1

    def scatter(values, depth):
        groups = [[(k << depth) | low for k in range(dp_count >> depth)] for low in range(1 << depth)]
        return lax.psum_scatter(values, "dp", scatter_dimension=0, axis_index_groups=groups, tiled=True)

    bits = dp_count.bit_length() - 1

    def part_of(weight, axis, index, count):
        size = weight.shape[axis] // count
        return lax.dynamic_slice_in_dim(weight, index * size, size, axis)

    up_mine = part_of(up_weight, 0, place, dp_count)
    feed = jnp.concatenate([up_mine[:, :width], up_mine[:, width:], part_of(down_weight, 0, place, dp_count)], axis=0)
    feed = over_x(feed)
    qkv_first = over_x(part_of(qkv_weight, 2, core, 2))
    small = over_x(jnp.concatenate([ssm_coef, ssm_skip[None]], axis=0))
    out_first = over_x(part_of(out_weight, 0, core, 2))

    def in_order(own, other, axis):
        return jnp.where(
            mine == 0, jnp.concatenate([own, other], axis=axis), jnp.concatenate([other, own], axis=axis)
        )

    coef = in_order(ssm_coef, small[:NS], 1)
    skip = in_order(ssm_skip[None], small[NS:], 1)

    dy_rows = turn_rows(where, cotangent, dp_count)
    feed = tie(feed, dy_rows)
    buffer = lax.all_gather(feed, "dp", axis=0, tiled=True).reshape(dp_count, 4, rows_each, width)
    u1, u1_rows = first_norm(tie(where, feed, small), layer_in, gain1, bias1, dp_count)
    context, state = ssm_forward(u1, coef, skip)
    context_turned = context_rows(tie(where, context), context, dp_count)
    qkv_own, ckv_own = project(u1, tie(context, context_turned), (qkv_weight,))
    heads_own, lse_own = attend_forward(qkv_own, ckv_own)
    qkv_first = tie(qkv_first, heads_own)
    qkv_second = over(qkv_first, 0)
    qkv_other, ckv_other = project(tie(u1, heads_own), context, (qkv_first, qkv_second))
    out_first = tie(out_first, qkv_other)
    out_second = over(out_first, 0)
    heads_other, lse_other = attend_forward(qkv_other, tie(ckv_other, out_first))
    out_second = tie(out_second, heads_other)
    x1, u2, u2_rows = attention_out(
        where, layer_in, heads_own, heads_other, out_weight, out_first, out_second, gain2, bias2, dp_count
    )
    hid, slope, sent, kept_own = hidden_forward(u2, dy_rows, up_weight, None)
    got_own = over(sent, 0)
    hid, slope, sent, kept_other = hidden_forward(u2, dy_rows, buffer, (hid, slope))
    got_other = over(sent, 0)

    split_y = (dp_count // 4, rows_each, 1)
    down_keep_own, down_send_own = join(tie(where, sent), kept_own, got_own, False, *split_y)
    down_got_own = over(down_send_own, 1)
    down_keep_other, down_send_other = join(tie(where, down_send_own), kept_other, got_other, False, *split_y)
    down_got_other = over(down_send_other, 1)
    layer_out, dpre, up_sent, up_kept = hidden_backward(
        tie(where, down_send_other), cotangent, hid, slope, down_weight, buffer, u2_rows, x1
    )
    up_got = over(up_sent, 0)
    layer_come = over_x(layer_out)
    down_sum = add_pairs(
        tie(where, layer_out), (down_keep_own, down_got_own), (down_keep_other, down_got_other)
    )
    up_keep, up_send = join(tie(where, down_sum), up_kept, up_got, False, *split_y)
    down_sum = scatter(down_sum, 2)
    up_got = over(up_send, 1)
    dattn, dattn_rows, dheads, sums2 = second_norm_backward(
        tie(where, up_send),
        cotangent,
        dpre,
        up_weight,
        buffer,
        x1,
        gain2,
        out_weight,
        out_first,
        out_second,
        dp_count,
    )
    dqkv_other, dckv_other = attend_backward(qkv_other, ckv_other, dheads, 1, lse_other)
    other_kept, *other_sent = projection_rows(
        u1_rows, context_turned, dqkv_other, dckv_other, dattn_rows, heads_other
    )
    other_got = [over(piece, 0) for piece in other_sent]
    layer_come = tie(layer_come, other_kept)
    up_sum = add_pairs(tie(where, other_kept, layer_come), (up_keep, up_got))
    dqkv_own, dckv_own = attend_backward(qkv_own, ckv_own, tie(dheads, up_sum), 0, lse_own)
    up_sum = scatter(up_sum, 2)
    other_keep, other_send = join(
        tie(where, dqkv_own), other_kept, [tie(piece, dqkv_own) for piece in other_got], True, *split_y
    )
    other_got = over(other_send, 1)
    own_kept, *own_sent = projection_rows(
        tie(u1_rows, other_send), context_turned, dqkv_own, dckv_own, dattn_rows, heads_own
    )
    own_got = [over(piece, 0) for piece in own_sent]
    down_sum = tie(down_sum, own_kept)

    def inputs_half(part, *deps):
        return inputs_backward(
            part,
            tie(where, *deps),
            ((dqkv_own, dckv_own), (dqkv_other, dckv_other)),
            qkv_weight,
            qkv_first,
            qkv_second,
            u1,
            coef,
            skip,
            state,
            layer_in,
            dattn,
            gain1,
        )

    grad_high, sums_high = inputs_half(1, own_kept, down_sum)
    come_high = over_x(grad_high)
    other_sum = add_pairs(tie(where, grad_high), (other_keep, other_got), power=20)
    own_keep, own_send = join(tie(where, other_sum), own_kept, own_got, False, *split_y)
    own_got = over(own_send, 1)
    up_sum = tie(up_sum, own_send)
    grad_low, sums_low, small_ssm = inputs_half(0, own_send, up_sum)
    middle = grad_low.shape[0] // 2
    come_0 = over_x(grad_low[:middle])
    small_all = jnp.concatenate([small_ssm, sums2, sums_low + sums_high], axis=0)
    small_all = small_all + over(small_all, 0)
    other_sum = scatter(other_sum, 2)

    def rows_of(bit):
        return (dp_count >> (bit + 1), rows_each << (bit - 2), bit)

    own_keep, own_send = join(
        tie(where, grad_low, come_high, small_all, other_sum),
        own_keep,
        own_got,
        False,
        *rows_of(2),
        37,
    )
    own_got, small_got = over(own_send, 2), over_x(small_all)
    hidden = up_weight.shape[1]
    final = jnp.concatenate([down_sum[:, hidden:], up_sum[:, hidden:], other_sum], axis=1)
    final_come = over_x(tie(final, own_send))
    come_1 = over_x(tie(grad_low[middle:], own_send))
    layer_pair = both_parts(tie(where, own_send), (layer_out,), (layer_come,), BF16, 32)
    small_all = small_all + tie(small_got, layer_pair)
    small_got = over(small_all, 1)
    rows = own_keep.shape[0]
    total = own_keep.astype(F32) + tie(own_got, small_all, come_0)
    for bit in range(3, bits):
        rows //= 2
        spread = total.reshape(dp_count >> (bit + 1), 2, -1, total.shape[1])
        mybit = (place >> bit) & 1
        pick = lambda index: lax.dynamic_index_in_dim(spread, index, 1, keepdims=False).reshape(rows, -1)
        send = pick(1 - mybit).astype(BF16)
        got = over(send, bit)
        small_all = small_all + tie(small_got, send)
        small_got = over(small_all, bit - 1)
        total = pick(mybit) + tie(got, small_all, come_1)
    own_total = total
    small_all = small_all + small_got
    small_got = over(small_all, bits - 1)
    grad_pair = both_parts(tie(where, small_all), (grad_low, grad_high), (come_0, come_1, come_high), F32, 32)
    small_all = small_all + tie(small_got, grad_pair)
    final_come = tie(final_come, small_all).astype(F32)
    down_come, up_come = final_come[:, :hidden], final_come[:, hidden : 2 * hidden]
    other_come = final_come[:, 2 * hidden :]
    here = lax.dynamic_slice_in_dim(small_all[: NS + 1], mine * group, group, 1)

    def ordered(values):
        return jnp.where(core == 1, swap_halves(values, group), values)

    grad_down = down_sum[:, :hidden].astype(F32) + down_come
    grad_up = up_sum[:, :hidden].astype(F32) + up_come
    grad_qkv_out = own_total + ordered(other_come)
    grad_qkv, grad_out = grad_qkv_out[:, : 3 * group], grad_qkv_out[:, 3 * group :]

    return (
        layer_pair,
        grad_pair,
        small_all[NS + 3],
        small_all[NS + 4],
        grad_qkv.reshape(rows_each, 3, group).swapaxes(0, 1),
        grad_out.T,
        here[:NS],
        here[NS],
        small_all[NS + 1],
        small_all[NS + 2],
        grad_up,
        grad_down.T,
    )


def solution(mesh):
    in_specs = (
        P(None, "dp", None, None),
        P(),
        P(),
        P(None, None, "tensor"),
        P("tensor", None),
        P(None, "tensor"),
        P("tensor"),
        P(),
        P(),
        P(None, "tensor"),
        P("tensor", None),
        P(None, "dp", None, None),
    )
    out_specs = (
        P(None, "dp", None, None),
        P(None, "dp", None, None),
        P(),
        P(),
        P(None, "dp", "tensor"),
        P("tensor", "dp"),
        P(None, "tensor"),
        P("tensor"),
        P(),
        P(),
        P("dp", "tensor"),
        P("tensor", "dp"),
    )
    body = functools.partial(shards, mesh.shape["dp"])
    return jax.shard_map(body, mesh=mesh, in_specs=in_specs, out_specs=out_specs, check_vma=False)
```

```python
import functools
import math

import jax
import jax.numpy as jnp
from jax import lax
from jax.experimental import pallas as pl
from jax.experimental.pallas import tpu as pltpu
from jax.sharding import PartitionSpec as P
import numpy as np

HD = 128
NS = 16
BLK = 512
CTX = 128
CH = 128
TILE = 256
EPS = 1e-05
F32 = jnp.float32
BF16 = jnp.bfloat16
HIGHEST = lax.Precision.HIGHEST
SCALE = HD**-0.5
LOG2 = SCALE * math.log2(math.e)


def swap(value, axis, mask, count):
    return lax.ppermute(value, axis, [(i, i ^ mask) for i in range(count)])


def tie(value, *deps):
    return lax.optimization_barrier((value, *deps))[0] if deps else value


def mm(left, right):
    return lax.dot_general(left, right, (((1,), (0,)), ((), ())), preferred_element_type=F32)


def mm_nt(left, right):
    return lax.dot_general(left, right, (((1,), (1,)), ((), ())), preferred_element_type=F32)


def mm_tn(left, right):
    return lax.dot_general(left, right, (((0,), (0,)), ((), ())), preferred_element_type=F32)


def decay_constants():
    rates = 4.0 / CH * np.exp2(-8.0 * np.arange(NS, dtype=np.float64) / (NS - 1))
    return rates, np.sqrt(-np.expm1(-2.0 * rates))


RATES, NORMS = decay_constants()


def decay_within(n, transposed):
    rows = lax.broadcasted_iota(jnp.int32, (CH, CH), 0)
    columns = lax.broadcasted_iota(jnp.int32, (CH, CH), 1)
    offset = columns - rows if transposed else rows - columns
    powers = jnp.exp(offset.astype(F32) * -float(RATES[n]))
    return jnp.where(offset >= 0, float(NORMS[n]) * powers, 0.0).astype(BF16)


def decay_vectors(rates, norms):
    steps = lax.broadcasted_iota(jnp.int32, (NS, CH), 1).astype(F32)
    carry_in = jnp.exp(-rates * (steps + 1.0))
    carry_out = (norms * jnp.exp(-rates * (CH - 1.0 - steps))).astype(BF16)
    return carry_in, carry_out, jnp.exp(-rates * CH)


def ssm_forward_kernel(v_ref, rates_ref, norms_ref, coef_ref, skip_ref, out_ref, state_ref, within_ref):
    @pl.when(pl.program_id(0) == 0)
    def _():
        for n in range(NS):
            within_ref[n] = decay_within(n, False)

    carry_in, carry_out, whole = decay_vectors(rates_ref[...], norms_ref[...])
    before = BLK // CH - 1
    state = jnp.zeros(state_ref.shape, F32)
    for k in range(before):
        state = whole * state + mm(carry_out, v_ref[k * CH : (k + 1) * CH, :])
    state_ref[...] = state
    rows = v_ref[before * CH :, :]
    total = skip_ref[...] * rows.astype(F32)
    total += lax.dot_general(
        carry_in, coef_ref[...] * state, (((0,), (0,)), ((), ())), precision=HIGHEST, preferred_element_type=F32
    )
    for n in range(NS):
        total += coef_ref[n : n + 1, :] * mm(within_ref[n], rows)
    out_ref[...] = total.astype(BF16)


def decay_arrays():
    return jnp.asarray(RATES[:, None], F32), jnp.asarray(NORMS[:, None], F32)


def ssm_forward(rows, coef, skip):
    width = rows.shape[1]
    step = 256
    column = lambda c: (0, c)
    fixed = pl.BlockSpec((NS, 1), lambda c: (0, 0))
    return pl.pallas_call(
        ssm_forward_kernel,
        grid=(width // step,),
        in_specs=[
            pl.BlockSpec((BLK, step), column),
            fixed,
            fixed,
            pl.BlockSpec((NS, step), column),
            pl.BlockSpec((1, step), column),
        ],
        out_specs=[pl.BlockSpec((CH, step), column), pl.BlockSpec((NS, step), column)],
        out_shape=[jax.ShapeDtypeStruct((CH, width), BF16), jax.ShapeDtypeStruct((NS, width), F32)],
        scratch_shapes=[pltpu.VMEM((NS, CH, CH), BF16)],
        cost_estimate=brief(31),
        name="ssm_forward",
    )(rows, *decay_arrays(), coef, skip)


def key_parts(block, tile, k_ref, v_ref, ck_ref, cv_ref):
    parts = []
    if block > 0:
        parts.append((None, ck_ref[0], cv_ref[0], False))
    for piece in range(tile + 1):
        where = slice(block * BLK + piece * TILE, block * BLK + (piece + 1) * TILE)
        parts.append((piece, k_ref[0, where, :], v_ref[0, where, :], piece == tile))
    return parts


def tile_scores(keys, query, masked):
    scores = mm_nt(keys, query)
    if masked:
        key_ids = lax.broadcasted_iota(jnp.int32, scores.shape, 0)
        query_ids = lax.broadcasted_iota(jnp.int32, scores.shape, 1)
        scores = jnp.where(key_ids <= query_ids, scores, -1e30)
    return scores


def attend_forward_kernel(q_ref, k_ref, v_ref, ck_ref, cv_ref, out_ref, lse_ref):
    for block in range(2):
        for tile in range(BLK // TILE):
            base = block * BLK + tile * TILE
            query = q_ref[0, base : base + TILE, :]
            parts = key_parts(block, tile, k_ref, v_ref, ck_ref, cv_ref)
            scores = [tile_scores(keys, query, masked) for _, keys, _, masked in parts]
            top = functools.reduce(jnp.maximum, [jnp.max(s, axis=0, keepdims=True) for s in scores]) * LOG2
            exps = [jnp.exp2(s * LOG2 - top) for s in scores]
            total = functools.reduce(jnp.add, [jnp.sum(e, axis=0, keepdims=True) for e in exps])
            out = functools.reduce(
                jnp.add, [mm_tn(values, e.astype(BF16)) for (_, _, values, _), e in zip(parts, exps)]
            )
            out_ref[base : base + TILE, :] = (out * (1.0 / total)).T.astype(BF16)
            lse_ref[0, :, base : base + TILE] = top + jnp.log2(total)


def attend_forward(qkv, ckv):
    length, width = qkv.shape[1], qkv.shape[2]
    heads = width // HD
    pick = lambda s: pl.BlockSpec((1, length, HD), lambda h: (s, 0, h))
    pick_context = lambda s: pl.BlockSpec((1, CTX, HD), lambda h: (s, 0, h))
    return pl.pallas_call(
        attend_forward_kernel,
        grid=(heads,),
        in_specs=[pick(0), pick(1), pick(2), pick_context(0), pick_context(1)],
        out_specs=[
            pl.BlockSpec((length, HD), lambda h: (0, h)),
            pl.BlockSpec((1, 1, length), lambda h: (h, 0, 0)),
        ],
        out_shape=[
            jax.ShapeDtypeStruct((length, width), BF16),
            jax.ShapeDtypeStruct((heads, 1, length), F32),
        ],
        cost_estimate=brief(31),
        name="attend_forward",
    )(qkv, qkv, qkv, ckv, ckv)


def attend_backward_kernel(q_ref, k_ref, v_ref, ck_ref, cv_ref, dout_ref, lse_ref, grad_ref, cgrad_ref):
    for block in range(2):
        grads = {}
        for tile in range(BLK // TILE):
            base = block * BLK + tile * TILE
            query = q_ref[0, base : base + TILE, :]
            dout = dout_ref[0, base : base + TILE, :]
            lse = lse_ref[0, :, base : base + TILE]
            parts = key_parts(block, tile, k_ref, v_ref, ck_ref, cv_ref)
            probs = [jnp.exp2(tile_scores(keys, query, masked) * LOG2 - lse) for _, keys, _, masked in parts]
            dprobs = [mm_nt(values, dout) for _, _, values, _ in parts]
            inner = functools.reduce(
                jnp.add, [jnp.sum(p * d, axis=0, keepdims=True) for p, d in zip(probs, dprobs)]
            )
            dquery = None
            for (name, keys, _, _), p, d in zip(parts, probs, dprobs):
                dscore = (p * (d - inner)).astype(BF16)
                term = mm_tn(keys, dscore)
                dquery = term if dquery is None else dquery + term
                dkey, dvalue = mm(dscore, query), mm(p.astype(BF16), dout)
                if name in grads:
                    grads[name] = (grads[name][0] + dkey, grads[name][1] + dvalue)
                else:
                    grads[name] = (dkey, dvalue)
            grad_ref[0, base : base + TILE, :] = (dquery.T * SCALE).astype(BF16)
        for name, (dkey, dvalue) in grads.items():
            dkey, dvalue = (dkey * SCALE).astype(BF16), dvalue.astype(BF16)
            if name is None:
                cgrad_ref[0] = dkey
                cgrad_ref[1] = dvalue
            else:
                where = slice(block * BLK + name * TILE, block * BLK + (name + 1) * TILE)
                grad_ref[1, where, :] = dkey
                grad_ref[2, where, :] = dvalue


def attend_backward(qkv, ckv, dheads, side, lse):
    length, width = qkv.shape[1], qkv.shape[2]
    heads = width // HD
    pick = lambda s: pl.BlockSpec((1, length, HD), lambda h: (s, 0, h))
    pick_context = lambda s: pl.BlockSpec((1, CTX, HD), lambda h: (s, 0, h))
    return pl.pallas_call(
        attend_backward_kernel,
        grid=(heads,),
        in_specs=[
            pick(0),
            pick(1),
            pick(2),
            pick_context(0),
            pick_context(1),
            pl.BlockSpec((1, length, HD), lambda h: (side, 0, h)),
            pl.BlockSpec((1, 1, length), lambda h: (h, 0, 0)),
        ],
        out_specs=[
            pl.BlockSpec((3, length, HD), lambda h: (0, 0, h)),
            pl.BlockSpec((2, CTX, HD), lambda h: (0, 0, h)),
        ],
        out_shape=[
            jax.ShapeDtypeStruct((3, length, width), BF16),
            jax.ShapeDtypeStruct((2, CTX, width), BF16),
        ],
        cost_estimate=brief(),
        name="attend_backward",
    )(qkv, qkv, qkv, ckv, ckv, dheads, lse)


def brief(power=32):
    return pl.CostEstimate(flops=1 << power, bytes_accessed=1 << 16, transcendentals=0)


def roomy():
    return pltpu.CompilerParams(vmem_limit_bytes=56 << 20)


def place_rows(where_ref, tall_ref, out_ref, count):
    size = tall_ref.shape[0] // count
    core = where_ref[1] & 1
    for p in range(count):
        start = pl.multiple_of((p % (count // 2) * 2 + (core ^ (p // (count // 2)))) * size, size)
        out_ref[p * size : (p + 1) * size, :] = tall_ref[pl.ds(start, size), :]


def whole_block(shape):
    return pl.BlockSpec(shape, lambda *_: (0,) * len(shape), pipeline_mode=pl.Buffered(1))


def normalize(values):
    center = values - jnp.mean(values, axis=-1, keepdims=True)
    rstd = lax.rsqrt(jnp.mean(center * center, axis=-1, keepdims=True) + EPS)
    return center * rstd, rstd


def normalize_backward(grad, hat, rstd, gain):
    dn = grad * gain
    return rstd * (dn - jnp.mean(dn, axis=-1, keepdims=True) - hat * jnp.mean(dn * hat, axis=-1, keepdims=True))


def turn_rows(where, values, count):
    length, width = values.shape[2:]
    step = 256

    def kernel(where_ref, x_ref, out_ref, tall):
        tall[...] = x_ref[0, 0].T
        place_rows(where_ref, tall, out_ref, count)

    return pl.pallas_call(
        kernel,
        grid_spec=pltpu.PrefetchScalarGridSpec(
            num_scalar_prefetch=1,
            grid=(length // step,),
            in_specs=[pl.BlockSpec((1, 1, step, width), lambda i, w: (w[0], 0, i, 0))],
            out_specs=pl.BlockSpec((width, step), lambda i, w: (0, i)),
            scratch_shapes=[pltpu.VMEM((width, step), BF16)],
        ),
        out_shape=jax.ShapeDtypeStruct((width, length), BF16),
        cost_estimate=brief(),
        name="turn_rows",
    )(where, values)


def first_norm(where, layer_in, gain, bias, count):
    length, width = layer_in.shape[2:]
    step = 256

    def kernel(where_ref, x_ref, gain_ref, bias_ref, u_ref, ut_ref, tall):
        hat, _ = normalize(x_ref[0, 0].astype(F32))
        u = (hat * gain_ref[...] + bias_ref[...]).astype(BF16)
        u_ref[...] = u
        tall[...] = u.T
        place_rows(where_ref, tall, ut_ref, count)

    return pl.pallas_call(
        kernel,
        grid_spec=pltpu.PrefetchScalarGridSpec(
            num_scalar_prefetch=1,
            grid=(length // step,),
            in_specs=[
                pl.BlockSpec((1, 1, step, width), lambda i, w: (w[0], 0, i, 0)),
                whole_block((1, width)),
                whole_block((1, width)),
            ],
            out_specs=[
                pl.BlockSpec((step, width), lambda i, w: (i, 0)),
                pl.BlockSpec((width, step), lambda i, w: (0, i)),
            ],
            scratch_shapes=[pltpu.VMEM((width, step), BF16)],
        ),
        out_shape=[
            jax.ShapeDtypeStruct((length, width), BF16),
            jax.ShapeDtypeStruct((width, length), BF16),
        ],
        cost_estimate=brief(),
        name="first_norm",
    )(where, layer_in, gain, bias)


def context_rows(where, context, count):
    def kernel(where_ref, c_ref, out_ref, tall):
        tall[...] = c_ref[...].T
        place_rows(where_ref, tall, out_ref, count)

    rows, width = context.shape
    return pl.pallas_call(
        kernel,
        in_specs=[pl.BlockSpec(memory_space=pltpu.SMEM), pl.BlockSpec(memory_space=pltpu.VMEM)],
        out_specs=pl.BlockSpec(memory_space=pltpu.VMEM),
        out_shape=jax.ShapeDtypeStruct((width, rows), BF16),
        scratch_shapes=[pltpu.VMEM((width, rows), BF16)],
        cost_estimate=brief(31),
        name="context_rows",
    )(where, context)


def project(u1, context, weights):
    length, width = u1.shape
    rows = context.shape[0]
    sizes = [w.shape[2] for w in weights]
    group = sum(sizes)

    def kernel(u_ref, c_ref, *refs):
        qkv_ref, ckv_ref, weight_s = refs[len(weights) :]
        start = 0
        for ref, size in zip(refs, sizes):
            weight_s[:, start : start + size] = ref[0]
            start += size
        for part in chunks(length):
            qkv_ref[0, part, :] = mm(u_ref[part, :], weight_s[...]).astype(BF16)

        @pl.when(pl.program_id(0) > 0)
        def _():
            ckv_ref[0] = mm(c_ref[...], weight_s[...]).astype(BF16)

    return pl.pallas_call(
        kernel,
        grid=(3,),
        in_specs=[whole_block((length, width)), whole_block((rows, width))]
        + [pl.BlockSpec((1, width, size), lambda s: (s, 0, 0)) for size in sizes],
        out_specs=[
            pl.BlockSpec((1, length, group), lambda s: (s, 0, 0)),
            pl.BlockSpec((1, rows, group), lambda s: (jnp.maximum(s - 1, 0), 0, 0)),
        ],
        out_shape=[
            jax.ShapeDtypeStruct((3, length, group), BF16),
            jax.ShapeDtypeStruct((2, rows, group), BF16),
        ],
        scratch_shapes=[pltpu.VMEM((width, group), BF16)],
        compiler_params=roomy(),
        cost_estimate=brief(31),
        name="project",
    )(u1, context, *weights)


def attention_out(where, layer_in, heads_own, heads_other, out_own, out_first, out_second, gain, bias, count):
    length, width = layer_in.shape[2:]
    group = heads_own.shape[1]
    half = group // 2
    step = 256

    def kernel(where_ref, x_ref, ho_ref, ht_ref, wo_ref, w1_ref, w2_ref, gain_ref, bias_ref, x1_ref, u_ref, ut_ref, tall):
        x1 = x_ref[0, 0].astype(F32) + mm(ho_ref[...], wo_ref[...])
        x1 += mm(ht_ref[:, :half], w1_ref[...]) + mm(ht_ref[:, half:], w2_ref[...])
        x1_ref[...] = x1
        hat, _ = normalize(x1)
        u = (hat * gain_ref[...] + bias_ref[...]).astype(BF16)
        u_ref[...] = u
        tall[...] = u.T
        place_rows(where_ref, tall, ut_ref, count)

    row = lambda i, w: (i, 0)
    return pl.pallas_call(
        kernel,
        grid_spec=pltpu.PrefetchScalarGridSpec(
            num_scalar_prefetch=1,
            grid=(length // step,),
            in_specs=[
                pl.BlockSpec((1, 1, step, width), lambda i, w: (w[0], 0, i, 0)),
                pl.BlockSpec((step, group), row),
                pl.BlockSpec((step, group), row),
                whole_block((group, width)),
                whole_block((half, width)),
                whole_block((half, width)),
                whole_block((1, width)),
                whole_block((1, width)),
            ],
            out_specs=[
                pl.BlockSpec((step, width), row),
                pl.BlockSpec((step, width), row),
                pl.BlockSpec((width, step), lambda i, w: (0, i)),
            ],
            scratch_shapes=[pltpu.VMEM((width, step), BF16)],
        ),
        out_shape=[
            jax.ShapeDtypeStruct((length, width), F32),
            jax.ShapeDtypeStruct((length, width), BF16),
            jax.ShapeDtypeStruct((width, length), BF16),
        ],
        compiler_params=roomy(),
        cost_estimate=brief(),
        name="attention_out",
    )(where, layer_in, heads_own, heads_other, out_own, out_first, out_second, gain, bias)


TALL = 256
STEP = 512


def chunks(length):
    return [slice(i, i + TALL) for i in range(0, length, TALL)]


def gelu_pair(pre):
    root = math.sqrt(2.0 / math.pi)
    straight = root * pre
    inner = straight * (1.0 + 0.044715 * (pre * pre))
    bend = jnp.tanh(inner)
    lean = 1.5 * inner - straight
    half = 0.5 * pre
    hid = half + half * bend
    slope = (0.5 + lean) + bend * (0.5 - lean * bend)
    return hid.astype(BF16), slope.astype(BF16)


def hidden_forward(u2, dy_rows, up, before):
    length, width = u2.shape
    half = width // 2
    gathered = up.ndim == 4
    steps = 2 * width // STEP
    first = 0 if before is None else steps

    def kernel(u_ref, dy_ref, up_ref, *refs):
        hid_ref, slope_ref, sent_ref, kept_ref = refs[-4:]
        weight = up_ref[...].reshape(width, STEP)
        for rows in chunks(length):
            hid, slope = gelu_pair(mm(u_ref[rows, :], weight))
            hid_ref[rows, :] = hid
            slope_ref[rows, :] = slope
        hid = hid_ref[...]
        for rows in chunks(half):
            sent_ref[rows, :] = mm(dy_ref[half + rows.start : half + rows.stop, :], hid).astype(BF16)
        for rows in chunks(half):
            kept_ref[rows, :] = mm(dy_ref[rows, :], hid).astype(BF16)

    if gathered:
        up_spec = pl.BlockSpec((up.shape[0], 1, up.shape[2], STEP), lambda j: (0, j // 2, 0, lax.rem(j, 2)))
    else:
        up_spec = pl.BlockSpec((width, STEP), lambda j: (0, j))
    tile = pl.BlockSpec((length, STEP), lambda j: (0, first + j))
    part = pl.BlockSpec((half, STEP), lambda j: (0, j))
    wide = jax.ShapeDtypeStruct((length, 2 * steps * STEP), BF16)
    return pl.pallas_call(
        kernel,
        grid=(steps,),
        in_specs=[whole_block((length, width)), whole_block((width, length)), up_spec]
        + ([] if before is None else [pl.BlockSpec(memory_space=pl.ANY)] * 2),
        out_specs=[tile, tile, part, part],
        out_shape=[wide, wide] + [jax.ShapeDtypeStruct((half, steps * STEP), BF16)] * 2,
        input_output_aliases={} if before is None else {3: 0, 4: 1},
        compiler_params=roomy(),
        cost_estimate=brief(37),
        name="hidden_forward",
    )(u2, dy_rows, up, *(before or ()))


def hidden_backward(where, cotangent, hid, slope, down_own, buffer, u2_rows, x1):
    length, width = x1.shape
    half = width // 2
    pieces, _, rows_each, _ = buffer.shape
    side = 2 * width // STEP
    steps = 2 * side

    def kernel(
        where_ref, dy_ref, hid_ref, slope_ref, down_ref, down2_ref, ut_ref, x1_ref,
        layer_ref, dpre_ref, sent_ref, kept_ref,
        down_s, mix_s, x1_s, sem,
    ):
        j = pl.program_id(0)
        fetch = pltpu.make_async_copy(x1_ref, x1_s, sem)

        @pl.when(j == 0)
        def _():
            fetch.start()
            mix_s[...] = jnp.zeros_like(mix_s)

        @pl.when(j < side)
        def _():
            down_s[...] = down_ref[...]

        @pl.when(j >= side)
        def _():
            down_s[...] = down2_ref[...].reshape(STEP, width)

        for rows in chunks(length):
            dhid = mm_nt(dy_ref[0, 0, rows, :], down_s[...])
            dpre_ref[rows, :] = (dhid * slope_ref[rows, :].astype(F32)).astype(BF16)
        for rows in chunks(length):
            mix_s[rows, :] += mm(hid_ref[rows, :], down_s[...])
        dpre = dpre_ref[...]
        for rows in chunks(half):
            sent_ref[rows, :] = mm(ut_ref[half + rows.start : half + rows.stop, :], dpre).astype(BF16)
        for rows in chunks(half):
            kept_ref[rows, :] = mm(ut_ref[rows, :], dpre).astype(BF16)

        @pl.when(j == steps - 1)
        def _():
            fetch.wait()
            for rows in chunks(length):
                layer_ref[rows, :] = (x1_s[rows, :] + mix_s[rows, :]).astype(BF16)

    low = lambda j: jnp.minimum(j, side - 1)
    high = lambda j: jnp.maximum(j - side, 0)
    tile = pl.BlockSpec((length, STEP), lambda j, w: (0, j))
    part = pl.BlockSpec((half, STEP), lambda j, w: (0, j))
    return pl.pallas_call(
        kernel,
        grid_spec=pltpu.PrefetchScalarGridSpec(
            num_scalar_prefetch=1,
            grid=(steps,),
            in_specs=[
                pl.BlockSpec((1, 1, length, width), lambda j, w: (w[0], 0, 0, 0), pipeline_mode=pl.Buffered(1)),
                tile,
                tile,
                pl.BlockSpec((STEP, width), lambda j, w: (low(j), 0)),
                pl.BlockSpec((pieces // side, 2, rows_each, width), lambda j, w: (high(j), 1, 0, 0)),
                whole_block((width, length)),
                pl.BlockSpec(memory_space=pl.ANY),
            ],
            out_specs=[whole_block((length, width)), tile, part, part],
            scratch_shapes=[
                pltpu.VMEM((STEP, width), BF16),
                pltpu.VMEM((length, width), F32),
                pltpu.VMEM((length, width), F32),
                pltpu.SemaphoreType.DMA,
            ],
        ),
        out_shape=[
            jax.ShapeDtypeStruct((length, width), BF16),
            jax.ShapeDtypeStruct((length, steps * STEP), BF16),
            jax.ShapeDtypeStruct((half, steps * STEP), BF16),
            jax.ShapeDtypeStruct((half, steps * STEP), BF16),
        ],
        compiler_params=roomy(),
        cost_estimate=brief(),
        name="hidden_backward",
    )(where, cotangent, hid, slope, down_own, buffer, u2_rows, x1)


def second_norm_backward(where, cotangent, dpre, up_own, buffer, x1, gain, out_own, out_first, out_second, count):
    length, width = x1.shape
    group = out_own.shape[0]
    pieces, _, rows_each, _ = buffer.shape
    side = 2
    tiles = 2 * side
    steps = tiles + 2
    chunk = 128

    def kernel(
        where_ref, dpre_ref, up_ref, up2_ref, dy_ref, x1_ref, gain_ref, wo_ref, w1_ref, w2_ref,
        dattn_ref, turned_ref, dheads_ref, sums_ref,
        up_s, out_s, grad_s, tall, dy_s, x1_s, sems,
    ):
        j = pl.program_id(0)
        fetches = [
            pltpu.make_async_copy(x1_ref, x1_s, sems.at[0]),
            pltpu.make_async_copy(dy_ref.at[where_ref[0], 0], dy_s, sems.at[1]),
            pltpu.make_async_copy(wo_ref, out_s.at[0], sems.at[2]),
            pltpu.make_async_copy(w1_ref, out_s.at[1, pl.ds(0, group // 2)], sems.at[3]),
            pltpu.make_async_copy(w2_ref, out_s.at[1, pl.ds(group // 2, group // 2)], sems.at[4]),
        ]

        @pl.when(j == 0)
        def _():
            for fetch in fetches:
                fetch.start()
            grad_s[...] = jnp.zeros_like(grad_s)
            sums_ref[...] = jnp.zeros_like(sums_ref)

        @pl.when(j < side)
        def _():
            up_s[...] = up_ref[...]

        @pl.when(jnp.logical_and(j >= side, j < tiles))
        def _():
            up_s[...] = up2_ref[...].reshape(width, width)

        @pl.when(j < tiles)
        def _():
            for rows in chunks(length):
                grad_s[rows, :] += mm_nt(dpre_ref[rows, :], up_s[...])

        @pl.when(j == tiles - 1)
        def _():
            for fetch in fetches:
                fetch.wait()

            @pl.loop(0, length // chunk)
            def _(i):
                rows = pl.ds(pl.multiple_of(i * chunk, chunk), chunk)
                du = grad_s[rows, :]
                hat, rstd = normalize(x1_s[rows, :])
                sums_ref[0:1, :] += jnp.sum(du * hat, axis=0, keepdims=True)
                sums_ref[1:2, :] += jnp.sum(du, axis=0, keepdims=True)
                out = dy_s[rows, :].astype(F32) + normalize_backward(du, hat, rstd, gain_ref[...])
                out = out.astype(BF16)
                dattn_ref[rows, :] = out
                tall[:, rows] = out.T

            place_rows(where_ref, tall, turned_ref, count)

        @pl.when(j >= tiles)
        def _():
            for rows in chunks(length):
                dheads_ref[0, rows, :] = mm_nt(dattn_ref[rows, :], out_s[j - tiles]).astype(BF16)

    low = lambda j: jnp.minimum(j, side - 1)
    high = lambda j: jnp.clip(j - side, 0, side - 1)
    return pl.pallas_call(
        kernel,
        grid_spec=pltpu.PrefetchScalarGridSpec(
            num_scalar_prefetch=1,
            grid=(steps,),
            in_specs=[
                pl.BlockSpec((length, width), lambda j, w: (0, jnp.minimum(j, tiles - 1))),
                pl.BlockSpec((width, width), lambda j, w: (0, low(j))),
                pl.BlockSpec((pieces, 1, rows_each, width), lambda j, w: (0, high(j), 0, 0)),
                pl.BlockSpec(memory_space=pl.ANY),
                pl.BlockSpec(memory_space=pl.ANY),
                whole_block((1, width)),
                pl.BlockSpec(memory_space=pl.ANY),
                pl.BlockSpec(memory_space=pl.ANY),
                pl.BlockSpec(memory_space=pl.ANY),
            ],
            out_specs=[
                whole_block((length, width)),
                whole_block((width, length)),
                pl.BlockSpec((1, length, group), lambda j, w: (jnp.maximum(j - tiles, 0), 0, 0)),
                whole_block((2, width)),
            ],
            scratch_shapes=[
                pltpu.VMEM((width, width), BF16),
                pltpu.VMEM((2, group, width), BF16),
                pltpu.VMEM((length, width), F32),
                pltpu.VMEM((width, length), BF16),
                pltpu.VMEM((length, width), BF16),
                pltpu.VMEM((length, width), F32),
                pltpu.SemaphoreType.DMA((5,)),
            ],
        ),
        out_shape=[
            jax.ShapeDtypeStruct((length, width), BF16),
            jax.ShapeDtypeStruct((width, length), BF16),
            jax.ShapeDtypeStruct((2, length, group), BF16),
            jax.ShapeDtypeStruct((2, width), F32),
        ],
        compiler_params=roomy(),
        cost_estimate=brief(),
        name="second_norm_backward",
    )(where, dpre, up_own, buffer, cotangent, x1, gain, out_own, out_first, out_second)


def projection_rows(u1_rows, context_turned, dqkv, dckv, dattn_rows, heads):
    width, length = u1_rows.shape
    half = width // 2
    group = heads.shape[1]

    def kernel(ut_ref, cut_ref, grad_ref, cgrad_ref, dt_ref, heads_ref, kept_ref, *refs):
        sent_refs, (dt_s, heads_s, sems) = refs[:4], refs[4:]
        s = pl.program_id(0)
        fetches = [
            pltpu.make_async_copy(dt_ref, dt_s, sems.at[0]),
            pltpu.make_async_copy(heads_ref, heads_s, sems.at[1]),
        ]

        @pl.when(s == 0)
        def _():
            for fetch in fetches:
                fetch.start()

        def emit(product):
            for rows in chunks(half):
                kept_ref[rows, :] = product(rows.start).astype(BF16)
            for rows in chunks(half):
                sent = product(half + rows.start).astype(BF16)
                for k, ref in enumerate(sent_refs):

                    @pl.when(s == k)
                    def _(ref=ref, rows=rows, sent=sent):
                        ref[rows, :] = sent

        @pl.when(s < 3)
        def _():
            grad = grad_ref[0]
            cgrad = jnp.where(s > 0, cgrad_ref[0], jnp.zeros_like(cgrad_ref[0]))

            def product(start):
                here = slice(start, start + TALL)
                return mm(ut_ref[here, :], grad) + mm(cut_ref[here, :], cgrad)

            emit(product)

        @pl.when(s == 3)
        def _():
            for fetch in fetches:
                fetch.wait()
            heads = heads_s[...]
            emit(lambda start: mm(dt_s[start : start + TALL, :], heads))

    part = pl.BlockSpec((half, group), lambda s: (0, s))
    return pl.pallas_call(
        kernel,
        grid=(4,),
        in_specs=[
            whole_block((width, length)),
            whole_block((width, CTX)),
            pl.BlockSpec((1, length, group), lambda s: (jnp.minimum(s, 2), 0, 0)),
            pl.BlockSpec((1, CTX, group), lambda s: (jnp.clip(s - 1, 0, 1), 0, 0)),
            pl.BlockSpec(memory_space=pl.ANY),
            pl.BlockSpec(memory_space=pl.ANY),
        ],
        out_specs=[part] + [whole_block((half, group))] * 4,
        out_shape=[jax.ShapeDtypeStruct((half, 4 * group), BF16)]
        + [jax.ShapeDtypeStruct((half, group), BF16)] * 4,
        scratch_shapes=[
            pltpu.VMEM((width, length), BF16),
            pltpu.VMEM((length, group), BF16),
            pltpu.SemaphoreType.DMA((2,)),
        ],
        compiler_params=roomy(),
        cost_estimate=brief(),
        name="projection_rows",
    )(u1_rows, context_turned, dqkv, dckv, dattn_rows, heads)


def inputs_backward(part, where, dsides, qkv_own, qkv_first, qkv_second, u1, coef, skip, state, layer_in, dattn, gain):
    length, width = layer_in.shape[2] // 2, layer_in.shape[3]
    group = qkv_own.shape[2]
    steps = 6
    chunk = 128
    before = BLK // CH - 1

    def kernel(
        where_ref, do_ref, dt_ref, co_ref, ct_ref, own_ref, w1_ref, w2_ref, v_ref, rates_ref,
        norms_ref, coef_ref, skip_ref, state_ref, x_ref, dx_ref, gain_ref,
        out_ref, sums_ref, *rest,
    ):
        grad_s, cgrad_s, weight_s, total, ctotal, within = rest[-6:]
        small_ref = rest[0]
        j = pl.program_id(0)

        @pl.when(j == 0)
        def _():
            total[...] = jnp.zeros_like(total)
            ctotal[...] = jnp.zeros_like(ctotal)
            sums_ref[...] = jnp.zeros_like(sums_ref)
            if part == 0:
                for n in range(NS):
                    within[n] = decay_within(n, True)

        @pl.when(j < 3)
        def _():
            grad_s[...] = do_ref[0]
            cgrad_s[...] = co_ref[0]
            weight_s[...] = own_ref[0]

        @pl.when(j >= 3)
        def _():
            grad_s[...] = dt_ref[0]
            cgrad_s[...] = ct_ref[0]
            weight_s[:, : group // 2] = w1_ref[0]
            weight_s[:, group // 2 :] = w2_ref[0]

        @pl.when(lax.rem(j, 3) == 0)
        def _():
            cgrad_s[...] = jnp.zeros_like(cgrad_s)

        for rows in chunks(length):
            total[rows, :] += mm_nt(grad_s[rows, :], weight_s[...])
        if part == 0:
            ctotal[...] += mm_nt(cgrad_s[...], weight_s[...])

        def state_space():
            carry_in, carry_out, whole = decay_vectors(rates_ref[...], norms_ref[...])

            @pl.loop(0, width // 256)
            def _(c):
                here = pl.ds(pl.multiple_of(c * 256, 256), 256)
                rows = v_ref[:, here].astype(F32)
                grad = ctotal[:, here].astype(BF16)
                wide = grad.astype(F32)
                du = skip_ref[:, here] * wide
                reach = jnp.dot(carry_in, wide, precision=HIGHEST, preferred_element_type=F32)
                for n in range(NS):
                    back = mm(within[n], grad)
                    du += coef_ref[n : n + 1, here] * back
                    small_ref[n : n + 1, here] = (
                        jnp.sum(rows * back, axis=0, keepdims=True) + state_ref[n : n + 1, here] * reach[n : n + 1, :]
                    )
                small_ref[NS : NS + 1, here] = jnp.sum(rows * wide, axis=0, keepdims=True)
                total[before * CH : (before + 1) * CH, here] += du
                carried = coef_ref[:, here] * reach
                for k in reversed(range(before)):
                    total[k * CH : (k + 1) * CH, here] += lax.dot_general(
                        carry_out.astype(F32),
                        carried,
                        (((0,), (0,)), ((), ())),
                        precision=HIGHEST,
                        preferred_element_type=F32,
                    )
                    carried = whole * carried

        @pl.when(j == steps - 1)
        def _():
            if part == 0:
                state_space()

            @pl.loop(0, length // chunk)
            def _(i):
                rows = pl.ds(pl.multiple_of(i * chunk, chunk), chunk)
                du = total[rows, :]
                hat, rstd = normalize(x_ref[0, 0, rows, :].astype(F32))
                sums_ref[0:1, :] += jnp.sum(du * hat, axis=0, keepdims=True)
                sums_ref[1:2, :] += jnp.sum(du, axis=0, keepdims=True)
                out = dx_ref[rows, :].astype(F32) + normalize_backward(du, hat, rstd, gain_ref[...])
                out_ref[rows, :] = out.astype(BF16)

    low = lambda j: jnp.minimum(j, 2)
    high = lambda j: jnp.maximum(j - 3, 0)
    back = lambda s: jnp.maximum(s - 1, 0)
    mine = pl.BlockSpec((1, 1, length, width), lambda j, w: (w[0], 0, part, 0), pipeline_mode=pl.Buffered(1))
    (dqkv_own, dckv_own), (dqkv_other, dckv_other) = dsides
    return pl.pallas_call(
        kernel,
        grid_spec=pltpu.PrefetchScalarGridSpec(
            num_scalar_prefetch=1,
            grid=(steps,),
            in_specs=[
                pl.BlockSpec((1, length, group), lambda j, w: (low(j), part, 0)),
                pl.BlockSpec((1, length, group), lambda j, w: (high(j), part, 0)),
                pl.BlockSpec((1, CTX, group), lambda j, w: (back(low(j)), 0, 0)),
                pl.BlockSpec((1, CTX, group), lambda j, w: (back(high(j)), 0, 0)),
                pl.BlockSpec((1, width, group), lambda j, w: (low(j), 0, 0)),
                pl.BlockSpec((1, width, group // 2), lambda j, w: (high(j), 0, 0)),
                pl.BlockSpec((1, width, group // 2), lambda j, w: (high(j), 0, 0)),
                pl.BlockSpec((CH, width), lambda j, w: (before, 0)),
                whole_block((NS, 1)),
                whole_block((NS, 1)),
                whole_block((NS, width)),
                whole_block((1, width)),
                whole_block((NS, width)),
                mine,
                pl.BlockSpec((length, width), lambda j, w: (part, 0), pipeline_mode=pl.Buffered(1)),
                whole_block((1, width)),
            ],
            out_specs=[
                whole_block((length, width)),
                whole_block((2, width)),
                *([whole_block((NS + 1, width))] if part == 0 else []),
            ],
            scratch_shapes=[
                pltpu.VMEM((length, group), BF16),
                pltpu.VMEM((CTX, group), BF16),
                pltpu.VMEM((width, group), BF16),
                pltpu.VMEM((length, width), F32),
                pltpu.VMEM((CTX, width), F32),
                pltpu.VMEM((NS, CH, CH), BF16),
            ],
        ),
        out_shape=[
            jax.ShapeDtypeStruct((length, width), BF16),
            jax.ShapeDtypeStruct((2, width), F32),
            *([jax.ShapeDtypeStruct((NS + 1, width), F32)] if part == 0 else []),
        ],
        compiler_params=roomy(),
        cost_estimate=brief(),
        name="inputs_backward",
    )(
        where, dqkv_own, dqkv_other, dckv_own, dckv_other, qkv_own, qkv_first, qkv_second,
        u1, *decay_arrays(), coef, skip, state, layer_in, dattn, gain,
    )


def join(where, kept, got, swap, above, below, bit, power=32):
    rows, columns = kept.shape
    pieces = list(got) if isinstance(got, (list, tuple)) else [got]
    width = columns // len(pieces) if len(pieces) > 1 else 2 * STEP
    shape = (above, 2, below)

    def kernel(where_ref, kept_ref, *refs):
        keep_ref, send_ref = refs[-2:]
        mine = (where_ref[1] >> bit) & 1

        def emit(got_ref):
            for out_ref, index in ((keep_ref, mine), (send_ref, 1 - mine)):
                come = got_ref[:, pl.ds(index, 1)][:, 0].astype(F32)
                if swap:
                    come = jnp.concatenate([come[..., width // 2 :], come[..., : width // 2]], axis=-1)
                out_ref[...] = (kept_ref[:, pl.ds(index, 1)][:, 0].astype(F32) + come).astype(BF16)

        if len(pieces) == 1:
            emit(refs[0])
        else:
            for k in range(len(pieces)):

                @pl.when(pl.program_id(0) == k)
                def _(ref=refs[k]):
                    emit(ref)

    tile = pl.BlockSpec((above, 2, below, width), lambda j, w: (0, 0, 0, j))
    out = pl.BlockSpec((above, below, width), lambda j, w: (0, 0, j))
    many = [tile] if len(pieces) == 1 else [whole_block((*shape, width))] * len(pieces)
    keep, send = pl.pallas_call(
        kernel,
        grid_spec=pltpu.PrefetchScalarGridSpec(
            num_scalar_prefetch=1, grid=(columns // width,), in_specs=[tile, *many], out_specs=[out, out]
        ),
        out_shape=[jax.ShapeDtypeStruct((above, below, columns), BF16)] * 2,
        compiler_params=roomy(),
        cost_estimate=brief(power),
        name="join",
    )(where, kept.reshape(*shape, columns), *[piece.reshape(*shape, -1) for piece in pieces])
    return keep.reshape(rows // 2, columns), send.reshape(rows // 2, columns)


def add_pairs(where, *pairs, power=37):
    rows, columns = pairs[0][0].shape
    width = min(columns, 4 * STEP)
    tiles = columns // width

    def kernel(where_ref, *refs):
        out_ref = refs[-1]
        for k in range(len(pairs)):

            @pl.when(pl.program_id(0) // tiles == k)
            def _(left=refs[2 * k], right=refs[2 * k + 1]):
                out_ref[...] = (left[...].astype(F32) + right[...].astype(F32)).astype(BF16)

    def spec(k):
        return pl.BlockSpec((rows, width), lambda j, w: (0, jnp.clip(j - k * tiles, 0, tiles - 1)))

    return pl.pallas_call(
        kernel,
        grid_spec=pltpu.PrefetchScalarGridSpec(
            num_scalar_prefetch=1,
            grid=(len(pairs) * tiles,),
            in_specs=[spec(k) for k in range(len(pairs)) for _ in range(2)],
            out_specs=pl.BlockSpec((rows, width), lambda j, w: (0, j)),
        ),
        out_shape=jax.ShapeDtypeStruct((rows, len(pairs) * columns), BF16),
        cost_estimate=brief(power),
        name="add_pairs",
    )(where, *[value for pair in pairs for value in pair])


def both_parts(where, own, come, kind, power):
    step = min(piece.shape[0] for piece in own + come)
    width = own[0].shape[1]
    steps = sum(piece.shape[0] for piece in own) // step
    def kernel(where_ref, *refs):
        out_ref = refs[-1]
        here = pl.program_id(0) == where_ref[0]
        for side, pieces in enumerate((refs[: len(own)], refs[len(own) : -1])):
            mine = jnp.logical_not(here) if side else here
            at = 0
            for ref in pieces:
                for start in range(0, ref.shape[0], step):

                    @pl.when(mine & (pl.program_id(1) == at))
                    def _(ref=ref, start=start):
                        out_ref[0, 0] = ref[start : start + step, :].astype(kind)

                    at += 1

    return pl.pallas_call(
        kernel,
        grid_spec=pltpu.PrefetchScalarGridSpec(
            num_scalar_prefetch=1,
            grid=(2, steps),
            in_specs=[whole_block(piece.shape) for piece in own + come],
            out_specs=pl.BlockSpec((1, 1, step, width), lambda m, i, w: (m, 0, i, 0)),
        ),
        out_shape=jax.ShapeDtypeStruct((2, 1, steps * step, width), kind),
        compiler_params=roomy(),
        cost_estimate=brief(power),
        name="both_parts",
    )(where, *own, *come)


def swap_halves(values, width):
    half = width // 2
    order = [start + half * k for start in range(0, values.shape[1], width) for k in (1, 0)]
    return jnp.concatenate([values[:, i : i + half] for i in order], axis=1)


def shards(
    dp_count,
    layer_in,
    ln1_gain,
    ln1_bias,
    qkv_weight,
    out_weight,
    ssm_coef,
    ssm_skip,
    ln2_gain,
    ln2_bias,
    up_weight,
    down_weight,
    cotangent,
):
    width = layer_in.shape[3]
    group = qkv_weight.shape[2]
    mine = lax.axis_index("tensor")
    place = lax.axis_index("dp")
    where = jnp.stack([mine, place]).astype(jnp.int32)
    rows_each = width // dp_count
    gain1, bias1, gain2, bias2 = ln1_gain[None], ln1_bias[None], ln2_gain[None], ln2_bias[None]

    over_x = lambda v: swap(v, "tensor", 1, 2)
    over = lambda v, bit: swap(v, "dp", 1 << bit, dp_count)
    core = place & 1

    def scatter(values, depth):
        groups = [[(k << depth) | low for k in range(dp_count >> depth)] for low in range(1 << depth)]
        return lax.psum_scatter(values, "dp", scatter_dimension=0, axis_index_groups=groups, tiled=True)

    bits = dp_count.bit_length() - 1

    def part_of(weight, axis, index, count):
        size = weight.shape[axis] // count
        return lax.dynamic_slice_in_dim(weight, index * size, size, axis)

    up_mine = part_of(up_weight, 0, place, dp_count)
    feed = jnp.concatenate([up_mine[:, :width], up_mine[:, width:], part_of(down_weight, 0, place, dp_count)], axis=0)
    feed = over_x(feed)
    qkv_first = over_x(part_of(qkv_weight, 2, core, 2))
    small = over_x(jnp.concatenate([ssm_coef, ssm_skip[None]], axis=0))
    out_first = over_x(part_of(out_weight, 0, core, 2))

    def in_order(own, other, axis):
        return jnp.where(
            mine == 0, jnp.concatenate([own, other], axis=axis), jnp.concatenate([other, own], axis=axis)
        )

    coef = in_order(ssm_coef, small[:NS], 1)
    skip = in_order(ssm_skip[None], small[NS:], 1)

    dy_rows = turn_rows(where, cotangent, dp_count)
    feed = tie(feed, dy_rows)
    buffer = lax.all_gather(feed, "dp", axis=0, tiled=True).reshape(dp_count, 4, rows_each, width)
    u1, u1_rows = first_norm(tie(where, feed, small), layer_in, gain1, bias1, dp_count)
    context, state = ssm_forward(u1, coef, skip)
    context_turned = context_rows(tie(where, context), context, dp_count)
    qkv_own, ckv_own = project(u1, tie(context, context_turned), (qkv_weight,))
    heads_own, lse_own = attend_forward(qkv_own, ckv_own)
    qkv_first = tie(qkv_first, heads_own)
    qkv_second = over(qkv_first, 0)
    qkv_other, ckv_other = project(tie(u1, heads_own), context, (qkv_first, qkv_second))
    out_first = tie(out_first, qkv_other)
    out_second = over(out_first, 0)
    heads_other, lse_other = attend_forward(qkv_other, tie(ckv_other, out_first))
    out_second = tie(out_second, heads_other)
    x1, u2, u2_rows = attention_out(
        where, layer_in, heads_own, heads_other, out_weight, out_first, out_second, gain2, bias2, dp_count
    )
    hid, slope, sent, kept_own = hidden_forward(u2, dy_rows, up_weight, None)
    got_own = over(sent, 0)
    hid, slope, sent, kept_other = hidden_forward(u2, dy_rows, buffer, (hid, slope))
    got_other = over(sent, 0)

    split_y = (dp_count // 4, rows_each, 1)
    down_keep_own, down_send_own = join(tie(where, sent), kept_own, got_own, False, *split_y)
    down_got_own = over(down_send_own, 1)
    down_keep_other, down_send_other = join(tie(where, down_send_own), kept_other, got_other, False, *split_y)
    down_got_other = over(down_send_other, 1)
    layer_out, dpre, up_sent, up_kept = hidden_backward(
        tie(where, down_send_other), cotangent, hid, slope, down_weight, buffer, u2_rows, x1
    )
    up_got = over(up_sent, 0)
    layer_come = over_x(layer_out)
    down_sum = add_pairs(
        tie(where, layer_out), (down_keep_own, down_got_own), (down_keep_other, down_got_other)
    )
    up_keep, up_send = join(tie(where, down_sum), up_kept, up_got, False, *split_y)
    down_sum = scatter(down_sum, 2)
    up_got = over(up_send, 1)
    dattn, dattn_rows, dheads, sums2 = second_norm_backward(
        tie(where, up_send),
        cotangent,
        dpre,
        up_weight,
        buffer,
        x1,
        gain2,
        out_weight,
        out_first,
        out_second,
        dp_count,
    )
    dqkv_other, dckv_other = attend_backward(qkv_other, ckv_other, dheads, 1, lse_other)
    other_kept, *other_sent = projection_rows(
        u1_rows, context_turned, dqkv_other, dckv_other, dattn_rows, heads_other
    )
    other_got = [over(piece, 0) for piece in other_sent]
    layer_come = tie(layer_come, other_kept)
    up_sum = add_pairs(tie(where, other_kept, layer_come), (up_keep, up_got))
    dqkv_own, dckv_own = attend_backward(qkv_own, ckv_own, tie(dheads, up_sum), 0, lse_own)
    up_sum = scatter(up_sum, 2)
    other_keep, other_send = join(
        tie(where, dqkv_own), other_kept, [tie(piece, dqkv_own) for piece in other_got], True, *split_y
    )
    other_got = over(other_send, 1)
    own_kept, *own_sent = projection_rows(
        tie(u1_rows, other_send), context_turned, dqkv_own, dckv_own, dattn_rows, heads_own
    )
    own_got = [over(piece, 0) for piece in own_sent]
    down_sum = tie(down_sum, own_kept)
    layer_pair = both_parts(tie(where, own_kept), (layer_out,), (layer_come,), BF16, 32)
    own_got = [tie(piece, layer_pair) for piece in own_got]

    def inputs_half(part, *deps):
        return inputs_backward(
            part,
            tie(where, *deps),
            ((dqkv_own, dckv_own), (dqkv_other, dckv_other)),
            qkv_weight,
            qkv_first,
            qkv_second,
            u1,
            coef,
            skip,
            state,
            layer_in,
            dattn,
            gain1,
        )

    grad_high, sums_high = inputs_half(1, own_kept, down_sum, *own_got)
    come_high = over_x(grad_high)
    other_sum = add_pairs(tie(where, grad_high), (other_keep, other_got), power=20)
    own_keep, own_send = join(tie(where, other_sum), own_kept, own_got, False, *split_y)
    own_got = over(own_send, 1)
    up_sum = tie(up_sum, own_send)
    grad_low, sums_low, small_ssm = inputs_half(0, own_send, up_sum)
    middle = grad_low.shape[0] // 2
    come_0 = over_x(grad_low[:middle])
    small_all = jnp.concatenate([small_ssm, sums2, sums_low + sums_high], axis=0)
    small_all = small_all + over(small_all, 0)
    other_sum = scatter(other_sum, 2)

    def rows_of(bit):
        return (dp_count >> (bit + 1), rows_each << (bit - 2), bit)

    own_keep, own_send = join(
        tie(where, grad_low, come_high, small_all, other_sum),
        own_keep,
        own_got,
        False,
        *rows_of(2),
        37,
    )
    own_got, small_got = over(own_send, 2), over_x(small_all)
    hidden = up_weight.shape[1]
    final = jnp.concatenate([down_sum[:, hidden:], up_sum[:, hidden:], other_sum], axis=1)
    final_come = over_x(tie(final, own_send))
    come_1 = over_x(tie(grad_low[middle:], own_send))
    small_all = small_all + tie(small_got, own_send)
    small_got = over(small_all, 1)
    rows = own_keep.shape[0]
    total = own_keep.astype(F32) + tie(own_got, small_all, come_0)
    for bit in range(3, bits):
        rows //= 2
        spread = total.reshape(dp_count >> (bit + 1), 2, -1, total.shape[1])
        mybit = (place >> bit) & 1
        pick = lambda index: lax.dynamic_index_in_dim(spread, index, 1, keepdims=False).reshape(rows, -1)
        send = pick(1 - mybit).astype(BF16)
        got = over(send, bit)
        small_all = small_all + tie(small_got, send)
        small_got = over(small_all, bit - 1)
        total = pick(mybit) + tie(got, small_all, come_1)
    own_total = total
    small_all = small_all + small_got
    small_got = over(small_all, bits - 1)
    grad_pair = both_parts(tie(where, small_all), (grad_low, grad_high), (come_0, come_1, come_high), F32, 32)
    small_all = small_all + tie(small_got, grad_pair)
    final_come = tie(final_come, small_all).astype(F32)
    down_come, up_come = final_come[:, :hidden], final_come[:, hidden : 2 * hidden]
    other_come = final_come[:, 2 * hidden :]
    here = lax.dynamic_slice_in_dim(small_all[: NS + 1], mine * group, group, 1)

    def ordered(values):
        return jnp.where(core == 1, swap_halves(values, group), values)

    grad_down = down_sum[:, :hidden].astype(F32) + down_come
    grad_up = up_sum[:, :hidden].astype(F32) + up_come
    grad_qkv_out = own_total + ordered(other_come)
    grad_qkv, grad_out = grad_qkv_out[:, : 3 * group], grad_qkv_out[:, 3 * group :]

    return (
        layer_pair,
        grad_pair,
        small_all[NS + 3],
        small_all[NS + 4],
        grad_qkv.reshape(rows_each, 3, group).swapaxes(0, 1),
        grad_out.T,
        here[:NS],
        here[NS],
        small_all[NS + 1],
        small_all[NS + 2],
        grad_up,
        grad_down.T,
    )


def solution(mesh):
    in_specs = (
        P(None, "dp", None, None),
        P(),
        P(),
        P(None, None, "tensor"),
        P("tensor", None),
        P(None, "tensor"),
        P("tensor"),
        P(),
        P(),
        P(None, "tensor"),
        P("tensor", None),
        P(None, "dp", None, None),
    )
    out_specs = (
        P(None, "dp", None, None),
        P(None, "dp", None, None),
        P(),
        P(),
        P(None, "dp", "tensor"),
        P("tensor", "dp"),
        P(None, "tensor"),
        P("tensor"),
        P(),
        P(),
        P("dp", "tensor"),
        P("tensor", "dp"),
    )
    body = functools.partial(shards, mesh.shape["dp"])
    return jax.shard_map(body, mesh=mesh, in_specs=in_specs, out_specs=out_specs, check_vma=False)
```
